32 devices in a mesh: lon: 4 (over y, x), lat: 8 (over z, core).
Axes of the slice: x: 2, y: 2, z: 4, core: 2. Of those that a mesh axis runs over, the one named last changes fastest.
Arguments:
- state_adjoint: float32 [4, 4, 512, 1024], P(None, None, 'lat', 'lon'), may hold values from -6 to 6
- east_velocity: float32 [4, 512, 1024], P(None, 'lat', 'lon'), may hold values from -1.2 to 1.2
- north_velocity: float32 [4, 512, 1024], P(None, 'lat', 'lon'), may hold values from -1.2 to 1.2
- ocean_mask: int32 [4, 512, 1024], P(None, 'lat', 'lon'), may hold values 0 or 1
- partner: int32 [1024], P('lon'), may hold values from 0 to 1023, as said below
Outputs:
- sensitivity: float32 [4, 4, 512, 1024], P(None, None, 'lat', 'lon')
The draws below stay inside these ranges and needn't reach their ends.
Inputs may be any that keep to these rules, and one draw needn't show every extreme that they name: partner[i] = (c - i) mod 1024 with one c for all columns, 1023 <= c <= 1278; hence partner[partner[i]] = i.
All inputs are finite; a program needn't handle non-finite values. No bound on the sum of `ocean_mask` on one device may be relied on, other than what follows from the above.
Results may differ from the reference program's by a relative error of at most 0.00002.
Values sent between devices are 32-bit elements; how exact they have to be, the bound alone decides.
No kernel may reach another device: no remote copies, remote signals or barrier semaphores. Data moves between devices by JAX's collectives and lax.ppermute only.
A program may use at most 64 MiB of HBM per device.

```python
import jax
import jax.numpy as jnp
from jax import lax

CX = 256
LEV = 4
STEPS = 2
FIELDS = 4
NX = 1024
NY = 512


def draw_partner(key, part):
    pivot = NX - 1 + jax.random.randint(key, (), 0, CX, dtype=jnp.int32)
    columns = jnp.arange(NX, dtype=jnp.int32)
    return ((pivot - columns) % NX).astype(jnp.int32)


def touch_ends(values, stream_key, smallest, largest):
    shape = values.shape
    place = [jax.random.randint(jax.random.fold_in(stream_key, axis), (), 0, shape[axis]) for axis in range(len(shape))]
    values = values.at[tuple(place)].set(smallest)
    longest = shape.index(max(shape))
    place[longest] = (place[longest] + 1) % shape[longest]
    return values.at[tuple(place)].set(largest)


def block_levels(key, shape, shards, least, top_value):
    gain, own = 1.0, jax.random.fold_in(key, 6)
    for dim, blocks in shards:
        steps = jnp.exp(jax.random.uniform(jax.random.fold_in(own, dim), (blocks,), jnp.float32, least / len(shards), top_value / len(shards)))
        gain = gain * jnp.repeat(steps, shape[dim] // blocks).reshape([-1 if axis == dim else 1 for axis in range(len(shape))])
    return gain


def gaussian(key, extent, spread, most, pieces=(), held_as=jnp.bfloat16):
    values = jax.random.normal(key, extent, jnp.float32) * spread
    if len(pieces) > 0:
        values = block_levels(key, extent, pieces, -0.22, 0.18) * values
    return jnp.clip(values, min=-most, max=most).astype(held_as)


def setup_inputs(seed: int = 0) -> dict:
    splits = jax.random.split(jax.random.key(seed), 6)
    state_adjoint = gaussian(splits[0], (FIELDS, LEV, NY, NX), 1.0, 6.0, ((2, 8), (3, 4)), jnp.float32)
    east_velocity = gaussian(splits[1], (LEV, NY, NX), 0.4, 1.2, ((1, 8), (2, 4)), jnp.float32)
    north_velocity = gaussian(splits[2], (LEV, NY, NX), 0.4, 1.2, ((1, 8), (2, 4)), jnp.float32)
    ocean_mask = touch_ends((jax.random.randint(splits[3], (LEV, NY, NX), 0, 4) < 3).astype(jnp.int32), jax.random.fold_in(splits[3], 1), 0, 1)
    partner = draw_partner(jax.random.fold_in(splits[5], 71), 0)
    return {"state_adjoint": state_adjoint, "east_velocity": east_velocity, "north_velocity": north_velocity, "ocean_mask": ocean_mask, "partner": partner}


def level_steps(fields, east_speed, north_speed, wet_cells, partner):
    fold_signs = jnp.array([1.0, 1.0, -1.0, -1.0], dtype=jnp.float32).reshape(4, 1)
    current = fields
    for iteration in range(STEPS):
        masked = wet_cells * current
        east_adj = jnp.roll(masked, -1, axis=2)
        west_adj = jnp.roll(masked, 1, axis=2)
        west_speed = jnp.roll(east_speed, 1, axis=1)
        zero_row = jnp.zeros_like(masked[:, :1, :])
        north_adj = jnp.concatenate([masked[:, 1:, :], zero_row], axis=1)
        south_adj = jnp.concatenate([zero_row, masked[:, :-1, :]], axis=1)
        south_speed = jnp.concatenate([jnp.zeros_like(north_speed[:1]), north_speed[:-1]], axis=0)
        transport = (0.5 * east_speed * (east_adj - masked) + 0.5 * west_speed * (masked - west_adj)
                     + 0.5 * north_speed * (north_adj - masked) + 0.5 * south_speed * (masked - south_adj))
        fold_flux = (1.0 + north_speed[-1, :]) * masked[:, -1, :]
        folded = 0.5 * fold_signs * jnp.take(fold_flux, partner, axis=1)
        total = masked + transport
        total = total.at[:, -1, :].add(folded)
        current = wet_cells * total
    return current


def reference(state_adjoint, east_velocity, north_velocity, ocean_mask, partner):
    def per_level(level):
        fields = lax.dynamic_index_in_dim(state_adjoint, level, 1, keepdims=False)
        east_speed = lax.dynamic_index_in_dim(east_velocity, level, 0, keepdims=False)
        north_speed = lax.dynamic_index_in_dim(north_velocity, level, 0, keepdims=False)
        wet_cells = lax.dynamic_index_in_dim(ocean_mask, level, 0, keepdims=False).astype(jnp.float32)
        return level_steps(fields, east_speed, north_speed, wet_cells, partner)

    result = lax.map(per_level, jnp.arange(LEV, dtype=jnp.int32))
    return jnp.moveaxis(result, 0, 1)
```

```python
import functools

import jax
import jax.numpy as jnp
from jax import lax
from jax.experimental import pallas as pl
from jax.experimental.pallas import tpu as pltpu
from jax.sharding import PartitionSpec as P

FIELDS = 4
QU, QV, QW, QN = 4, 5, 6, 7
LANES, SUBS = 128, 8


def iota(dim):
    return lax.broadcasted_iota(jnp.int32, (SUBS, LANES), dim)


def place():
    lon, lat = lax.axis_index("lon"), lax.axis_index("lat")
    return lon, lon % 2 == 0, lat % 2 == 0, lat == lax.axis_size("lat") - 1


def row_kernel(levels, s_lo, s_hi, u_lo, u_hi, v_lo, v_hi, m_lo, m_hi, a_ref, b_ref):
    _, _, lat_even, _ = place()
    for l in range(levels):
        lo_w = m_lo[l, 0:2, :].astype(jnp.float32)
        hi_w = m_hi[l, 6:8, :].astype(jnp.float32)
        pairs = [(s_lo[f, l, 0:2, :] * lo_w, s_hi[f, l, 6:8, :] * hi_w) for f in range(FIELDS)]
        pairs += [(u_lo[l, 0:2, :], u_hi[l, 6:8, :]), (v_lo[l, 0:2, :], v_hi[l, 6:8, :]), (lo_w, hi_w)]
        pairs += [(jnp.zeros_like(lo_w), jnp.zeros_like(lo_w))]
        for q, (lo, hi) in enumerate(pairs):
            at = pl.ds(16 * l + 2 * q, 2)
            a_ref[at, :] = jnp.where(lat_even, hi, lo)
            b_ref[at, :] = jnp.where(lat_even, lo, hi)


def column_kernel(s_ref, u_ref, v_ref, m_ref, a_ref, b_ref, p_ref, q_ref, halo):
    l = pl.program_id(0)
    _, lon_even, lat_even, top = place()
    lane, sub = iota(1), iota(0)
    tiles = s_ref.shape[2] // SUBS
    last = s_ref.shape[3] - LANES
    halo[...] = jnp.zeros_like(halo)
    for q in range(QN):
        a, b = a_ref[2 * q : 2 * q + 2, :], b_ref[2 * q : 2 * q + 2, :]
        halo[q, 0:2, :] = jnp.where(lat_even, a, b)
        halo[q, 6:8, :] = jnp.where(lat_even, b, a)
    for t in range(tiles + 1):
        east = jnp.zeros((SUBS, LANES), jnp.float32)
        west = jnp.zeros((SUBS, LANES), jnp.float32)
        rows = pl.ds(SUBS * t, SUBS)
        if t < tiles:
            w0 = m_ref[0, rows, 0:LANES].astype(jnp.float32)
            w1 = m_ref[0, rows, last : last + LANES].astype(jnp.float32)
        for q in range(QN):
            if t == tiles:
                first, end = halo[q, :, 0:LANES], halo[q, :, last : last + LANES]
                first = jnp.where(top & (sub < 2), pltpu.roll(end, 1, 1), first)
            elif q < FIELDS:
                first, end = s_ref[q, 0, rows, 0:LANES] * w0, s_ref[q, 0, rows, last : last + LANES] * w1
            elif q == QW:
                first, end = w0, w1
            else:
                ref = u_ref if q == QU else v_ref
                first, end = ref[0, rows, 0:LANES], ref[0, rows, last : last + LANES]
            here = lane // 2 == q
            west = jnp.where(here, pltpu.roll(first, 2 * q, 1) if q else first, west)
            east = jnp.where(here, pltpu.roll(end, 2 * q + 2, 1), east)
        mine = lane // 16 == l
        for ref, pack in ((p_ref, jnp.where(lon_even, east, west)), (q_ref, jnp.where(lon_even, west, east))):
            ref[rows, :] = jnp.where(mine, pltpu.roll(pack, 16 * l, 1), ref[rows, :])


def step_kernel(c_ref, s_ref, u_ref, v_ref, m_ref, a_ref, b_ref, f_ref, p_ref, q_ref, o_ref, hu, hv, wt, mir, r0, r1):
    l = pl.program_id(0)
    lon, lon_even, lat_even, top = place()
    lane, sub = iota(1), iota(0)
    tiles, width = s_ref.shape[2] // SUBS, s_ref.shape[3]
    cols = width // LANES
    ncol = lax.axis_size("lon") * width
    shift = lax.rem(c_ref[0] + lon * width + 1, ncol)

    def at(t, c):
        return pl.ds(SUBS * t, SUBS), pl.ds(LANES * c, LANES)

    @pl.when(top)
    def _():
        for c in range(cols + 1):
            i = LANES * c + lane
            if c == cols:
                i = jnp.where(lane < LANES // 2, i, lane - LANES)
            for g in range(2):
                p = shift + (width - 1) - i
                if g == 1:
                    p = jnp.where(sub < 2, p - 1, p)
                p = jnp.clip(p, 0, 2 * width - 1)
                got = jnp.zeros((SUBS, LANES), jnp.float32)
                for s in range(2 * cols):
                    src = b_ref if s < cols else f_ref
                    tile = src[pl.ds(SUBS * g, SUBS), pl.ds(LANES * (s % cols), LANES)]
                    picked = jnp.take_along_axis(tile, p % LANES, axis=1, mode="promise_in_bounds")
                    got = jnp.where(p // LANES == s, picked, got)
                mir[pl.ds(SUBS * g, SUBS), pl.ds(LANES * c, LANES)] = got

    def halo_tiles(q):
        side = []
        for t in range(tiles + 1):
            p, w = p_ref[pl.ds(SUBS * t, SUBS), :], q_ref[pl.ds(SUBS * t, SUBS), :]
            e, w = jnp.where(lon_even, p, w), jnp.where(lon_even, w, p)
            back = 16 * l + 2 * q
            e, w = pltpu.roll(e, LANES - back, 1), pltpu.roll(w, LANES + 126 - back, 1)
            side.append(jnp.where(lane < LANES // 2, e, w))
            corner = e
        out = []
        for c in range(cols + 1):
            if c < cols:
                a, b = (ref[2 * q : 2 * q + 2, LANES * c : LANES * c + LANES] for ref in (a_ref, b_ref))
                n, s = jnp.where(lat_even, a, b), jnp.where(lat_even, b, a)
                zero = jnp.zeros((4, LANES), jnp.float32)
                tile = jnp.concatenate([n, zero, s], axis=0)
            else:
                tile = side[tiles]
            second, first = (
                jnp.broadcast_to(mir[2 * q + k : 2 * q + k + 1, LANES * c : LANES * c + LANES], (SUBS, LANES))
                for k in range(2)
            )
            seam = jnp.broadcast_to(corner[1:2, 0:1], (SUBS, LANES))
            if c == cols and q != QU:
                first = jnp.where((shift == 0) & (lane == 0), seam, first)
            if c == cols - 1 and q == QU:
                first = jnp.where((shift == 0) & (lane == LANES - 1), seam, first)
            if q == QU:
                first = -first
            if q == QV:
                second, first = first, -second
            tile = jnp.where(top & (sub == 0), first, tile)
            tile = jnp.where(top & (sub == 1), second, tile)
            out.append(tile)
        return out, side[:tiles]

    own = {QU: (u_ref, hu), QV: (v_ref, hv), QW: (m_ref, wt)}
    for q in range(FIELDS):
        own[q] = (s_ref, r0.at[q])
    for q in (QW, QU, QV, 0, 1, 2, 3):
        src, dst = own[q]
        halo, side = halo_tiles(q)
        half = q in (QU, QV)
        for c in range(cols + 1):
            dst[at(tiles, c)] = 0.5 * halo[c] if half else halo[c]
        for t in range(tiles):
            dst[at(t, cols)] = 0.5 * side[t] if half else side[t]
            for c in range(cols):
                if q < FIELDS:
                    dst[at(t, c)] = src[(q, 0) + at(t, c)] * wt[at(t, c)]
                elif q == QW:
                    dst[at(t, c)] = src[(0,) + at(t, c)].astype(jnp.float32)
                else:
                    dst[at(t, c)] = 0.5 * src[(0,) + at(t, c)]

    east_edge, west_edge = lane == 0, lane == LANES - 1
    north_edge, south_edge = sub == 0, sub == SUBS - 1
    top_row, mirror_row = top & (sub == SUBS - 1), top & (sub == 0)
    ring = cols + 1

    def north_of(here, above):
        return pltpu.roll(jnp.where(north_edge, above, here), SUBS - 1, 0)

    def south_of(here, below):
        return pltpu.roll(jnp.where(south_edge, below, here), 1, 0)

    def step(field, src, row_tiles, columns, store):
        sign = 1.0 if field < 2 else -1.0
        low = [None] * ring
        for c in columns:
            r = src[at(tiles, c)]
            low[c] = hv[at(tiles, c)] * (north_of(r, src[at(0, c)]) - r)
        for t in row_tiles:
            now = [src[at(t, c)] for c in range(ring)]
            flux = []
            for c in range(ring):
                ahead = pltpu.roll(jnp.where(east_edge, now[(c + 1) % ring], now[c]), LANES - 1, 1)
                flux.append(hu[at(t, c)] * (ahead - now[c]))
            for c in columns:
                back = pltpu.roll(jnp.where(west_edge, flux[(c - 1) % ring], flux[c]), 1, 1)
                r, h = now[c], hv[at(t, c)]
                above = north_of(r, src[at((t + 1) % (tiles + 1), c)])
                up = h * (above - r)
                down = south_of(up, low[c])
                low[c] = up
                if t == tiles - 1:
                    met = pltpu.roll(hv[at(tiles, c)], SUBS - 2, 0)
                    up = jnp.where(top_row, sign * (0.5 + met) * above - h * r, up)
                if t == tiles:
                    met, edge = pltpu.roll(h, SUBS - 1, 0), pltpu.roll(hv[at(tiles - 1, c)], 1, 0)
                    below = pltpu.roll(src[at(tiles - 1, c)], 1, 0)
                    down = jnp.where(mirror_row, sign * (0.5 + edge) * below - met * r, down)
                store(t, c, wt[at(t, c)] * (r + flux[c] + back + up + down))

    for f in range(FIELDS):

        def keep(t, c, value, f=f):
            r1[(f,) + at(t, c)] = value

        def give(t, c, value, f=f):
            o_ref[(f, 0) + at(t, c)] = value

        step(f, r0.at[f], range(tiles + 1), range(ring), keep)
        step(f, r1.at[f], range(tiles), range(cols), give)


def per_device(state_adjoint, east_velocity, north_velocity, ocean_mask, partner):
    nlon, nlat = lax.axis_size("lon"), lax.axis_size("lat")
    fields, levels, rows, width = state_adjoint.shape
    axes = ("lon", "lat")

    def device(lon, lat):
        return lon % nlon * nlat + lat

    def both(a, b):
        return [(a, b), (b, a)]

    fold = [(device(nlon - 1 - i, nlat - 1), device(i, nlat - 1)) for i in range(nlon)]
    fold_next = [(device(nlon - i, nlat - 1), device(i, nlat - 1)) for i in range(nlon)]
    within = [e for i in range(nlon) for j in range(0, nlat, 2) for e in both(device(i, j), device(i, j + 1))]
    across = [e for i in range(nlon) for j in range(1, nlat - 1, 2) for e in both(device(i, j), device(i, j + 1))]
    even = [e for i in range(0, nlon, 2) for j in range(nlat) for e in both(device(i, j), device(i + 1, j))]
    odd = [e for i in range(1, nlon, 2) for j in range(nlat) for e in both(device(i, j), device(i + 1, j))]

    f32 = jnp.float32
    last = rows // SUBS - 1
    tile4 = [pl.BlockSpec((fields, levels, SUBS, width), lambda _, k=k: (0, 0, k, 0)) for k in (0, last)]
    tile3 = [pl.BlockSpec((levels, SUBS, width), lambda _, k=k: (0, k, 0)) for k in (0, last)]
    message = jax.ShapeDtypeStruct((16 * levels, width), f32)
    to_a, to_b = pl.pallas_call(
        functools.partial(row_kernel, levels),
        grid=(1,),
        out_shape=(message, message),
        in_specs=tile4 + tile3 * 3,
        name="pack_rows",
    )(
        state_adjoint, state_adjoint, east_velocity, east_velocity, north_velocity, north_velocity, ocean_mask, ocean_mask
    )
    from_a = lax.ppermute(to_a, axes, within)
    from_b = lax.ppermute(to_b, axes, across + fold)
    from_f = lax.ppermute(to_b, axes, fold_next)

    level4 = pl.BlockSpec((fields, 1, rows, width), lambda l: (0, l, 0, 0))
    level3 = pl.BlockSpec((1, rows, width), lambda l: (l, 0, 0))
    level2 = pl.BlockSpec((16, width), lambda l: (l, 0))
    column = pl.BlockSpec((rows + SUBS, LANES), lambda l: (0, 0))
    packed = jax.ShapeDtypeStruct((rows + SUBS, LANES), f32)
    to_p, to_q = pl.pallas_call(
        column_kernel,
        grid=(levels,),
        out_shape=(packed, packed),
        in_specs=[level4, level3, level3, level3, level2, level2],
        out_specs=(column, column),
        scratch_shapes=[pltpu.VMEM((QN, SUBS, width), f32)],
        name="pack_columns",
    )(state_adjoint, east_velocity, north_velocity, ocean_mask, from_a, from_b)
    from_p = lax.ppermute(to_p, axes, even)
    from_q = lax.ppermute(to_q, axes, odd)

    ext = (rows + SUBS, width + LANES)
    return pl.pallas_call(
        step_kernel,
        grid=(levels,),
        out_shape=jax.ShapeDtypeStruct(state_adjoint.shape, f32),
        in_specs=[pl.BlockSpec(memory_space=pltpu.SMEM), level4, level3, level3, level3, level2, level2, level2, column, column],
        out_specs=level4,
        scratch_shapes=[
            pltpu.VMEM(ext, f32),
            pltpu.VMEM(ext, f32),
            pltpu.VMEM(ext, f32),
            pltpu.VMEM((16, width + LANES), f32),
            pltpu.VMEM((fields,) + ext, f32),
            pltpu.VMEM((fields,) + ext, f32),
        ],
        name="both_steps",
    )(partner, state_adjoint, east_velocity, north_velocity, ocean_mask, from_a, from_b, from_f, from_p, from_q)


def solution(mesh):
    placed = (
        P(None, None, "lat", "lon"),
        P(None, "lat", "lon"),
        P(None, "lat", "lon"),
        P(None, "lat", "lon"),
        P("lon"),
    )
    return jax.shard_map(
        per_device,
        mesh=mesh,
        in_specs=placed,
        out_specs=P(None, None, "lat", "lon"),
        check_vma=False,
    )
```

```python
import jax
import jax.numpy as jnp
from jax import lax
from jax.experimental import pallas as pl
from jax.experimental.pallas import tpu as pltpu
from jax.sharding import PartitionSpec as P

FIELDS, LEVELS = 4, 4
QN = FIELDS + 3
LANES, SUBS = 128, 8
SOUTH, OWN = 1, 2
VMEM = pl.BlockSpec(memory_space=pltpu.VMEM)
SCOPED = 4 << 20
UNROLL1, UNROLL2 = 5, 4


def iota(dim):
    return lax.broadcasted_iota(jnp.int32, (SUBS, LANES), dim)


def rows(t, by=0):
    start = SUBS * t
    if not isinstance(start, int):
        start = pl.multiple_of(start, SUBS)
    return pl.ds(start + by, SUBS)


def cols(c):
    return pl.ds(LANES * c, LANES)


def lat_place():
    lat = lax.axis_index("lat")
    return lat % 2 == 0, lat == lax.axis_size("lat") - 1


def sign_of(field):
    return 1.0 if field < 2 else -1.0


def row_kernel(s_in, u_in, v_in, m_in, a_ref, b_ref, s_ref, u_ref, v_ref, m_ref, sems):
    copies = []
    for i, (src, dst) in enumerate(((u_in, u_ref), (v_in, v_ref), (m_in, m_ref))):
        copies.append(pltpu.make_async_copy(src, dst, sems.at[i]))
    for f in range(FIELDS):
        copies.append(pltpu.make_async_copy(s_in.at[f], s_ref.at[f], sems.at[3 + f]))
    for copy in copies:
        copy.start()
    for copy in copies:
        copy.wait()
    lat_even, _ = lat_place()
    sub = iota(0)
    last = s_ref.shape[2] // SUBS - 1

    @pl.loop(0, LEVELS)
    def _(l):
        for c in range(2):
            both = []
            for t in (0, last):
                w = m_ref[l, rows(t), cols(c)].astype(jnp.float32)
                values = [s_ref[f, l, rows(t), cols(c)] * w for f in range(FIELDS)]
                both.append(values + [0.5 * u_ref[l, rows(t), cols(c)], 0.5 * v_ref[l, rows(t), cols(c)], w, w])
            for g in range(2):
                low, high = both[0][4 * g], pltpu.roll(both[1][4 * g], 2, 0)
                for k in range(1, 4):
                    low = jnp.where(sub // 2 == k, pltpu.roll(both[0][4 * g + k], 2 * k, 0), low)
                    high = jnp.where(sub // 2 == k, pltpu.roll(both[1][4 * g + k], (2 * k + 2) % SUBS, 0), high)
                a_ref[rows(2 * l + g), cols(c)] = jnp.where(lat_even, high, low)
                b_ref[rows(2 * l + g), cols(c)] = jnp.where(lat_even, low, high)


def insert(packs, quarter, l, q, side, tile):
    seg = LEVELS * (q % 2) + l if q < FIELDS else l
    g = q // 2 if q < FIELDS else q - 2
    moved = pltpu.roll(tile, (16 * seg + (12 if side else 4)) % LANES, 1)
    packs[g] = jnp.where(quarter == 4 * seg + 1 + side, moved, packs[g])


def finish(packs, lane):
    for g in range(2, 5):
        packs[g] = jnp.where(lane < LANES // 2, packs[g], pltpu.roll(packs[g], LANES // 2, 1))


def outgoing(packs, lane, lon_even):
    east = jnp.zeros((SUBS, LANES), jnp.float32)
    west = jnp.zeros((SUBS, LANES), jnp.float32)
    pair = lane // 2 % 8
    for g, tile in enumerate(packs):
        east = jnp.where(pair == 1 + g, pltpu.roll(tile, LANES - 8 + 2 * g, 1), east)
        west = jnp.where(pair == (6 + g) % 8, pltpu.roll(tile, 8 + 2 * g, 1), west)
    return jnp.where(lon_even, east, west), jnp.where(lon_even, west, east)


def prepare_kernel(s_ref, u_ref, v_ref, m_ref, r_ref, u2_ref, v2_ref, w_ref, k_ref, p_ref, q_ref):
    lane = iota(1)
    quarter = lane // 4
    lon_even = lax.axis_index("lon") % 2 == 0

    @pl.loop(0, s_ref.shape[2] // SUBS, unroll=2)
    def _(t):
        src, dst = rows(t), rows(t + OWN)
        packs = [jnp.zeros((SUBS, LANES), jnp.float32)] * 5
        for l in range(LEVELS):
            for c in range(2):
                w = m_ref[l, src, cols(c)].astype(jnp.float32)
                values = [s_ref[f, l, src, cols(c)] * w for f in range(FIELDS)]
                values += [0.5 * u_ref[l, src, cols(c)], 0.5 * v_ref[l, src, cols(c)], w]
                for q, value in enumerate(values):
                    ref = (u2_ref, v2_ref, w_ref)[q - FIELDS] if q >= FIELDS else r_ref
                    ref[LEVELS * q + l if q < FIELDS else l, c, dst, :] = value
                    insert(packs, quarter, l, q, c, value)
        finish(packs, lane)
        for g in range(5):
            k_ref[g, src, :] = packs[g]
        p_ref[src, :], q_ref[src, :] = outgoing(packs, lane, lon_even)


def halo_kernel(
    c_ref, a_ref, b_ref, f_ref, r_in, u2_in, v2_in, w_in, k_in, p_in, q_in,
    r_ref, u2_ref, v2_ref, w_ref, k_ref, p_ref, q_ref, north, south,
):
    lane, sub = iota(1), iota(0)
    quarter = lane // 4
    lat_even, top = lat_place()
    lon = lax.axis_index("lon")
    lon_even = lon % 2 == 0
    width = a_ref.shape[1]
    tiles = k_ref.shape[1] // SUBS - 1

    @pl.loop(0, 2 * LEVELS)
    def _(i):
        for c in range(2):
            a, b = a_ref[rows(i), cols(c)], b_ref[rows(i), cols(c)]
            north[c, rows(i + 1), :] = jnp.where(lat_even, a, b)
            south[c, rows(i + 1), :] = jnp.where(lat_even, b, a)

    @pl.when(top)
    def _():
        ncol = lax.axis_size("lon") * width
        shift = jnp.clip(lax.rem(c_ref[0] + lon * width + 1, ncol), 0, width - 1)

        @pl.loop(0, LEVELS)
        def _(l):
            for g in range(2):
                for c in range(2):
                    p = shift + (width - 1) - LANES * c - lane
                    got = jnp.zeros((SUBS, LANES), jnp.float32)
                    for s in range(4):
                        tile = (b_ref if s < 2 else f_ref)[rows(2 * l + g), cols(s % 2)]
                        picked = jnp.take_along_axis(tile, p % LANES, axis=1, mode="promise_in_bounds")
                        got = jnp.where(p // LANES == s, picked, got)
                    swapped = jnp.where(sub % 2 == 0, pltpu.roll(got, SUBS - 1, 0), pltpu.roll(got, 1, 0))
                    if g == 1:
                        swapped = jnp.where(sub == 2, -got, jnp.where(sub == 3, got, swapped))
                    north[c, rows(2 * l + g + 1), :] = swapped

    packs = [jnp.zeros((SUBS, LANES), jnp.float32)] * 5
    for l in range(LEVELS):
        for q in range(QN):
            tile = []
            for c in range(2):
                at = SUBS + 16 * l + 2 * q
                tile.append(jnp.where(sub < 4, north[c, pl.ds(at, SUBS), :], south[c, pl.ds(at - 6, SUBS), :]))
                insert(packs, quarter, l, q, c, tile[c])
            for c in range(2):
                ref = (u2_ref, v2_ref, w_ref)[q - FIELDS] if q >= FIELDS else r_ref
                index = LEVELS * q + l if q < FIELDS else l
                ref[index, c, rows(SOUTH), :] = tile[c]
                if q == FIELDS:
                    mirrored = -pltpu.roll(jnp.where(lane == 0, tile[1 - c], tile[c]), LANES - 1, 1)
                    tile_n = jnp.where(top & (sub == 0), mirrored, tile[c])
                else:
                    tile_n = tile[c]
                ref[index, c, rows(tiles + OWN), :] = tile_n
    finish(packs, lane)

    for g in range(5):
        k_ref[g, rows(tiles), :] = packs[g]
    p_ref[rows(tiles), :], q_ref[rows(tiles), :] = outgoing(packs, lane, lon_even)


def seam(r, r_mirror, h, h_mirror, w, sign):
    return w * r_mirror * (sign * (0.5 + h_mirror) - h)


def seam_mirror(r, r_top, h_top, h, w, sign):
    return w * (sign * (0.5 + h_top) * r_top - h * r - h_top * (r - r_top))


def step_kernel(r_ref, u2_ref, v2_ref, w_ref, o_ref, r1):
    lane, sub = iota(1), iota(0)
    _, top = lat_place()
    tiles = o_ref.shape[2] // SUBS
    end = OWN + tiles

    def update(l, t, load):
        u = [u2_ref[l, c, rows(t), :] for c in range(2)]
        u_west = [pltpu.roll(jnp.where(lane == LANES - 1, u[1 - c], u[c]), 1, 1) for c in range(2)]
        v = [v2_ref[l, c, rows(t), :] for c in range(2)]
        v_south = [v2_ref[l, c, rows(t, -1), :] for c in range(2)]
        w = [w_ref[l, c, rows(t), :] for c in range(2)]
        out = []
        for f in range(FIELDS):
            r = [load(f, c, rows(t)) for c in range(2)]
            for c in range(2):
                ahead = pltpu.roll(jnp.where(lane == 0, r[1 - c], r[c]), LANES - 1, 1)
                behind = pltpu.roll(jnp.where(lane == LANES - 1, r[1 - c], r[c]), 1, 1)
                along = u[c] * (ahead - r[c]) + u_west[c] * (r[c] - behind)
                up = v[c] * (load(f, c, rows(t, 1)) - r[c])
                down = v_south[c] * (r[c] - load(f, c, rows(t, -1)))
                out.append((f, c, w[c] * (r[c] + along + up + down)))
        return out

    @pl.loop(0, LEVELS)
    def _(l):
        def first(f, c, at):
            return r_ref[LEVELS * f + l, c, at, :]

        def second(f, c, at):
            return r1[f, c, at, :]

        @pl.loop(SOUTH, end + 1, unroll=UNROLL1)
        def _(t):
            for f, c, value in update(l, t, first):
                r1[f, c, rows(t), :] = value

        def at_top(f, c, load):
            v, v_mirror = v2_ref[l, c, rows(end - 1), :], v2_ref[l, c, rows(end - 1, 2), :]
            r, r_mirror = load(f, c, rows(end - 1)), load(f, c, rows(end - 1, 1))
            add = seam(r, r_mirror, v, v_mirror, w_ref[l, c, rows(end - 1), :], sign_of(f))
            return jnp.where(sub == SUBS - 1, add, 0.0)

        @pl.when(top)
        def _():
            for f in range(FIELDS):
                for c in range(2):
                    v_top, v_mirror = v2_ref[l, c, rows(end, -1), :], v2_ref[l, c, rows(end, 1), :]
                    r, r_top = first(f, c, rows(end)), first(f, c, rows(end, -1))
                    add = seam_mirror(r, r_top, v_top, v_mirror, w_ref[l, c, rows(end), :], sign_of(f))
                    r1[f, c, rows(end), :] += jnp.where(sub == 0, add, 0.0)
                    r1[f, c, rows(end - 1), :] += at_top(f, c, first)

        @pl.loop(OWN, end, unroll=UNROLL2)
        def _(t):
            for f, c, value in update(l, t, second):
                o_ref[f, l, rows(t - OWN), cols(c)] = value

        @pl.when(top)
        def _():
            for f in range(FIELDS):
                for c in range(2):
                    o_ref[f, l, rows(tiles - 1), cols(c)] += at_top(f, c, second)


def edge_kernel(k_ref, p_ref, q_ref, i_ref, o_ref, z, z1, buf, sems):
    lane, sub = iota(1), iota(0)
    _, top = lat_place()
    lon_even = lax.axis_index("lon") % 2 == 0
    tiles = i_ref.shape[2] // SUBS
    end = OWN + tiles
    pair = lane // 2 % 8

    def join(t):
        p, q = p_ref[rows(t), :], q_ref[rows(t), :]
        from_west, from_east = jnp.where(lon_even, q, p), jnp.where(lon_even, p, q)
        out = []
        for g in range(5):
            back = (LANES - 2 * g) % LANES
            west, east = (pltpu.roll(x, back, 1) if back else x for x in (from_west, from_east))
            out.append(jnp.where(pair == 1, west, jnp.where(pair == 6, east, k_ref[g, rows(t), :])))
        return out

    @pl.loop(0, tiles, unroll=True)
    def _(t):
        for g, value in enumerate(join(t)):
            z[g, rows(t + OWN), :] = value

    for g, value in enumerate(join(tiles)):
        z[g, rows(SOUTH), :] = value
        if g == 2:
            value = jnp.where(top & (sub == 0), -pltpu.roll(value, LANES - 1, 1), value)
        z[g, rows(end), :] = value

    def update(t, load, mirrored):
        u, v, v_south, w = z[2, rows(t), :], z[3, rows(t), :], z[3, rows(t, -1), :], z[4, rows(t), :]
        u_west = pltpu.roll(u, 1, 1)
        out = []
        for h in range(2):
            r, r_north, r_south = load(h, rows(t)), load(h, rows(t, 1)), load(h, rows(t, -1))
            along = u * (pltpu.roll(r, LANES - 1, 1) - r) + u_west * (r - pltpu.roll(r, 1, 1))
            value = w * (r + along + v * (r_north - r) + v_south * (r - r_south))
            add = seam(r, r_north, v, z[3, rows(t, 2), :], w, sign_of(2 * h))
            value += jnp.where(top & (t == end - 1) & (sub == SUBS - 1), add, 0.0)
            if mirrored:
                add = seam_mirror(r, r_south, v_south, z[3, rows(t, 1), :], w, sign_of(2 * h))
                value += jnp.where(top & (t == end) & (sub == 0), add, 0.0)
            out.append(value)
        return out

    @pl.loop(SOUTH, end + 1, unroll=True)
    def _(t):
        for h, value in enumerate(update(t, lambda h, at: z[h, at, :], True)):
            z1[h, rows(t), :] = value

    def send(t):
        at = rows(t)
        return pltpu.make_async_copy(buf.at[:, :, at, :], o_ref.at[:, :, at, :], sems.at[t])

    @pl.loop(0, tiles, unroll=UNROLL2)
    def _(t):
        value = update(t + OWN, lambda h, at: z1[h, at, :], False)
        for f in range(FIELDS):
            for l in range(LEVELS):
                seg = 16 * (LEVELS * (f % 2) + l)
                west = pltpu.roll(value[f // 2], LANES - 4 - seg, 1)
                east = pltpu.roll(value[f // 2], (LANES + 116 - seg) % LANES, 1)
                buf[f, l, rows(t), cols(0)] = jnp.where(lane < 2, west, i_ref[f, l, rows(t), cols(0)])
                buf[f, l, rows(t), cols(1)] = jnp.where(lane >= LANES - 2, east, i_ref[f, l, rows(t), cols(1)])
        send(t).start()

    @pl.loop(0, tiles)
    def _(t):
        send(t).wait()


def per_device(state_adjoint, east_velocity, north_velocity, ocean_mask, partner):
    nlon, nlat = lax.axis_size("lon"), lax.axis_size("lat")
    fields, levels, height, width = state_adjoint.shape
    axes = ("lon", "lat")
    f32 = jnp.float32

    def device(lon, lat):
        return lon % nlon * nlat + lat

    def both(a, b):
        return [(a, b), (b, a)]

    fold = [(device(nlon - 1 - i, nlat - 1), device(i, nlat - 1)) for i in range(nlon)]
    fold_next = [(device(nlon - i, nlat - 1), device(i, nlat - 1)) for i in range(nlon)]
    within = [e for i in range(nlon) for j in range(0, nlat, 2) for e in both(device(i, j), device(i, j + 1))]
    across = [e for i in range(nlon) for j in range(1, nlat - 1, 2) for e in both(device(i, j), device(i, j + 1))]
    even = [e for i in range(0, nlon, 2) for j in range(nlat) for e in both(device(i, j), device(i + 1, j))]
    odd = [e for i in range(1, nlon, 2) for j in range(nlat) for e in both(device(i, j), device(i + 1, j))]

    def held(x):
        return pltpu.with_memory_space_constraint(x, pltpu.VMEM)

    def call(kernel, name, args, outs, scratch=(), scalars=0, aliases=None, micros=1):
        return pl.pallas_call(
            kernel,
            out_shape=tuple(pltpu.VMEM(shape, f32) for shape in outs),
            in_specs=[pl.BlockSpec(memory_space=pltpu.SMEM)] * scalars + [VMEM] * (len(args) - scalars),
            out_specs=(VMEM,) * len(outs),
            scratch_shapes=[pltpu.VMEM(shape, f32) for shape in scratch],
            input_output_aliases=aliases or {},
            cost_estimate=pl.CostEstimate(flops=0, bytes_accessed=micros * 3_000_000, transcendentals=0),
            compiler_params=pltpu.CompilerParams(vmem_limit_bytes=SCOPED),
            name=name,
        )(*args[:scalars], *(held(x) for x in args[scalars:]))

    inputs = (state_adjoint, east_velocity, north_velocity, ocean_mask)
    message = (16 * levels, width)
    to_a, to_b, *inputs = pl.pallas_call(
        row_kernel,
        out_shape=(pltpu.VMEM(message, f32), pltpu.VMEM(message, f32), *(pltpu.VMEM(x.shape, x.dtype) for x in inputs)),
        in_specs=[pl.BlockSpec(memory_space=pltpu.HBM)] * 4,
        out_specs=(VMEM,) * 6,
        scratch_shapes=[pltpu.SemaphoreType.DMA((3 + fields,))],
        compiler_params=pltpu.CompilerParams(vmem_limit_bytes=SCOPED),
        name="pack_rows",
    )(*(pltpu.with_memory_space_constraint(x, pltpu.HBM) for x in inputs))
    from_a = lax.ppermute(to_a, axes, within)
    from_b = lax.ppermute(to_b, axes, across + fold)
    from_f = lax.ppermute(to_b, axes, fold_next)

    tall = height + 4 * SUBS
    ext = [(fields * levels, 2, tall, LANES)] + [(levels, 2, tall, LANES)] * 3
    pack = (height + SUBS, LANES)
    laid = call(prepare_kernel, "prepare", inputs, (*ext, (5,) + pack, pack, pack))
    *laid, packs, to_p, to_q = call(
        halo_kernel,
        "place_rows",
        (partner, from_a, from_b, from_f, *laid),
        (*ext, (5,) + pack, pack, pack),
        [(2, message[0] + 2 * SUBS, LANES)] * 2,
        scalars=1,
        aliases={4 + i: i for i in range(7)},
    )
    from_p = lax.ppermute(to_p, axes, even)
    from_q = lax.ppermute(to_q, axes, odd)

    (inner,) = call(step_kernel, "both_steps", laid, (state_adjoint.shape,), [(fields, 2, tall, LANES)], micros=3)
    return pl.pallas_call(
        edge_kernel,
        out_shape=jax.ShapeDtypeStruct(state_adjoint.shape, f32),
        in_specs=[VMEM] * 4,
        out_specs=pl.BlockSpec(memory_space=pl.ANY),
        scratch_shapes=[
            pltpu.VMEM((5, tall, LANES), f32),
            pltpu.VMEM((2, tall, LANES), f32),
            pltpu.VMEM(state_adjoint.shape, f32),
            pltpu.SemaphoreType.DMA((height // SUBS,)),
        ],
        compiler_params=pltpu.CompilerParams(vmem_limit_bytes=SCOPED),
        name="edge_columns",
    )(*(held(x) for x in (packs, from_p, from_q, inner)))


def solution(mesh):
    placed = (
        P(None, None, "lat", "lon"),
        P(None, "lat", "lon"),
        P(None, "lat", "lon"),
        P(None, "lat", "lon"),
        P("lon"),
    )
    return jax.shard_map(
        per_device,
        mesh=mesh,
        in_specs=placed,
        out_specs=P(None, None, "lat", "lon"),
        check_vma=False,
    )
```

```python
import jax
import jax.numpy as jnp
from jax import lax
from jax.experimental import pallas as pl
from jax.experimental.pallas import tpu as pltpu
from jax.sharding import PartitionSpec as P

FIELDS, LEVELS = 4, 4
QN = FIELDS + 3
LANES, SUBS = 128, 8
SOUTH, OWN = 1, 2
VMEM = pl.BlockSpec(memory_space=pltpu.VMEM)
SCOPED = 4 << 20
UNROLL1, UNROLL2 = 10, 8


def iota(dim):
    return lax.broadcasted_iota(jnp.int32, (SUBS, LANES), dim)


def rows(t, by=0):
    start = SUBS * t
    if not isinstance(start, int):
        start = pl.multiple_of(start, SUBS)
    return pl.ds(start + by, SUBS)


def cols(c):
    return pl.ds(LANES * c, LANES)


def lat_place():
    lat = lax.axis_index("lat")
    return lat % 2 == 0, lat == lax.axis_size("lat") - 1


def sign_of(field):
    return 1.0 if field < 2 else -1.0


def row_kernel(s_in, u_in, v_in, m_in, a_ref, b_ref, s_ref, u_ref, v_ref, m_ref, sems):
    lat_even, _ = lat_place()
    sub = iota(0)
    copies = []
    for i, (src, dst) in enumerate(((s_in, s_ref), (u_in, u_ref), (v_in, v_ref), (m_in, m_ref))):
        lead = (slice(None),) * (len(src.shape) - 2)
        for k, t in enumerate((0, src.shape[-2] // SUBS - 1)):
            copies.append(pltpu.make_async_copy(src.at[lead + (rows(t), slice(None))], dst.at[k], sems.at[i, k]))
    for copy in copies:
        copy.start()
    for copy in copies:
        copy.wait()

    @pl.loop(0, LEVELS)
    def _(l):
        for c in range(2):
            both = []
            for k in range(2):
                w = m_ref[k, l, :, cols(c)].astype(jnp.float32)
                values = [s_ref[k, f, l, :, cols(c)] * w for f in range(FIELDS)]
                both.append(values + [0.5 * u_ref[k, l, :, cols(c)], 0.5 * v_ref[k, l, :, cols(c)], w, w])
            for g in range(2):
                low, high = both[0][4 * g], pltpu.roll(both[1][4 * g], 2, 0)
                for k in range(1, 4):
                    low = jnp.where(sub // 2 == k, pltpu.roll(both[0][4 * g + k], 2 * k, 0), low)
                    high = jnp.where(sub // 2 == k, pltpu.roll(both[1][4 * g + k], (2 * k + 2) % SUBS, 0), high)
                a_ref[rows(2 * l + g), cols(c)] = jnp.where(lat_even, high, low)
                b_ref[rows(2 * l + g), cols(c)] = jnp.where(lat_even, low, high)


def insert(packs, quarter, l, q, side, tile):
    seg = LEVELS * (q % 2) + l if q < FIELDS else l
    g = q // 2 if q < FIELDS else q - 2
    moved = pltpu.roll(tile, (16 * seg + (12 if side else 4)) % LANES, 1)
    packs[g] = jnp.where(quarter == 4 * seg + 1 + side, moved, packs[g])


def finish(packs, lane):
    for g in range(2, 5):
        packs[g] = jnp.where(lane < LANES // 2, packs[g], pltpu.roll(packs[g], LANES // 2, 1))


def outgoing(packs, lane, lon_even):
    east = jnp.zeros((SUBS, LANES), jnp.float32)
    west = jnp.zeros((SUBS, LANES), jnp.float32)
    pair = lane // 2 % 8
    for g, tile in enumerate(packs):
        east = jnp.where(pair == 1 + g, pltpu.roll(tile, LANES - 8 + 2 * g, 1), east)
        west = jnp.where(pair == (6 + g) % 8, pltpu.roll(tile, 8 + 2 * g, 1), west)
    return jnp.where(lon_even, east, west), jnp.where(lon_even, west, east)


def prepare_kernel(s_ref, u_ref, v_ref, m_ref, r_ref, u2_ref, v2_ref, w_ref, k_ref, p_ref, q_ref):
    lane = iota(1)
    quarter = lane // 4
    lon_even = lax.axis_index("lon") % 2 == 0

    @pl.loop(0, s_ref.shape[2] // SUBS, unroll=2)
    def _(t):
        src, dst = rows(t), rows(t + OWN)
        packs = [jnp.zeros((SUBS, LANES), jnp.float32)] * 5
        for l in range(LEVELS):
            for c in range(2):
                w = m_ref[l, src, cols(c)].astype(jnp.float32)
                values = [s_ref[f, l, src, cols(c)] * w for f in range(FIELDS)]
                values += [0.5 * u_ref[l, src, cols(c)], 0.5 * v_ref[l, src, cols(c)], w]
                for q, value in enumerate(values):
                    ref = (u2_ref, v2_ref, w_ref)[q - FIELDS] if q >= FIELDS else r_ref
                    ref[LEVELS * q + l if q < FIELDS else l, c, dst, :] = value
                    insert(packs, quarter, l, q, c, value)
        finish(packs, lane)
        for g in range(5):
            k_ref[g, src, :] = packs[g]
        p_ref[src, :], q_ref[src, :] = outgoing(packs, lane, lon_even)


def halo_kernel(
    c_ref, a_ref, b_ref, f_ref, r_in, u2_in, v2_in, w_in, k_in, p_in, q_in,
    r_ref, u2_ref, v2_ref, w_ref, k_ref, p_ref, q_ref, north, south,
):
    lane, sub = iota(1), iota(0)
    quarter = lane // 4
    lat_even, top = lat_place()
    lon = lax.axis_index("lon")
    lon_even = lon % 2 == 0
    width = a_ref.shape[1]
    tiles = k_ref.shape[1] // SUBS - 1

    @pl.loop(0, 2 * LEVELS)
    def _(i):
        for c in range(2):
            a, b = a_ref[rows(i), cols(c)], b_ref[rows(i), cols(c)]
            north[c, rows(i + 1), :] = jnp.where(lat_even, a, b)
            south[c, rows(i + 1), :] = jnp.where(lat_even, b, a)

    @pl.when(top)
    def _():
        ncol = lax.axis_size("lon") * width
        source = [lax.rem(c_ref[pl.ds(c, SUBS, stride=0), :] + (lon + 1) * width, ncol) for c in range(2)]

        @pl.loop(0, LEVELS)
        def _(l):
            for g in range(2):
                for c in range(2):
                    p = source[c]
                    got = jnp.zeros((SUBS, LANES), jnp.float32)
                    for s in range(4):
                        tile = (b_ref if s < 2 else f_ref)[rows(2 * l + g), cols(s % 2)]
                        picked = jnp.take_along_axis(tile, p % LANES, axis=1, mode="promise_in_bounds")
                        got = jnp.where(p // LANES == s, picked, got)
                    swapped = jnp.where(sub % 2 == 0, pltpu.roll(got, SUBS - 1, 0), pltpu.roll(got, 1, 0))
                    if g == 1:
                        swapped = jnp.where(sub == 2, -got, jnp.where(sub == 3, got, swapped))
                    north[c, rows(2 * l + g + 1), :] = swapped

    packs = [jnp.zeros((SUBS, LANES), jnp.float32)] * 5
    for l in range(LEVELS):
        for q in range(QN):
            tile = []
            for c in range(2):
                at = SUBS + 16 * l + 2 * q
                tile.append(jnp.where(sub < 4, north[c, pl.ds(at, SUBS), :], south[c, pl.ds(at - 6, SUBS), :]))
                insert(packs, quarter, l, q, c, tile[c])
            for c in range(2):
                ref = (u2_ref, v2_ref, w_ref)[q - FIELDS] if q >= FIELDS else r_ref
                index = LEVELS * q + l if q < FIELDS else l
                ref[index, c, rows(SOUTH), :] = tile[c]
                if q == FIELDS:
                    mirrored = -pltpu.roll(jnp.where(lane == 0, tile[1 - c], tile[c]), LANES - 1, 1)
                    tile_n = jnp.where(top & (sub == 0), mirrored, tile[c])
                else:
                    tile_n = tile[c]
                ref[index, c, rows(tiles + OWN), :] = tile_n
    finish(packs, lane)

    for g in range(5):
        k_ref[g, rows(tiles), :] = packs[g]
    p_ref[rows(tiles), :], q_ref[rows(tiles), :] = outgoing(packs, lane, lon_even)


def seam(r, r_mirror, h, h_mirror, w, sign):
    return w * r_mirror * (sign * (0.5 + h_mirror) - h)


def seam_mirror(r, r_top, h_top, h, w, sign):
    return w * (sign * (0.5 + h_top) * r_top - h * r - h_top * (r - r_top))


def step_kernel(r_ref, u2_ref, v2_ref, w_ref, o_ref, r1):
    lane, sub = iota(1), iota(0)
    _, top = lat_place()
    tiles = o_ref.shape[2] // SUBS
    end = OWN + tiles

    def update(l, t, load):
        u = [u2_ref[l, c, rows(t), :] for c in range(2)]
        u_west = [pltpu.roll(jnp.where(lane == LANES - 1, u[1 - c], u[c]), 1, 1) for c in range(2)]
        v = [v2_ref[l, c, rows(t), :] for c in range(2)]
        v_south = [v2_ref[l, c, rows(t, -1), :] for c in range(2)]
        w = [w_ref[l, c, rows(t), :] for c in range(2)]
        out = []
        for f in range(FIELDS):
            r = [load(f, c, rows(t)) for c in range(2)]
            for c in range(2):
                ahead = pltpu.roll(jnp.where(lane == 0, r[1 - c], r[c]), LANES - 1, 1)
                behind = pltpu.roll(jnp.where(lane == LANES - 1, r[1 - c], r[c]), 1, 1)
                along = u[c] * (ahead - r[c]) + u_west[c] * (r[c] - behind)
                up = v[c] * (load(f, c, rows(t, 1)) - r[c])
                down = v_south[c] * (r[c] - load(f, c, rows(t, -1)))
                out.append((f, c, w[c] * (r[c] + along + up + down)))
        return out

    @pl.loop(0, LEVELS)
    def _(l):
        def first(f, c, at):
            return r_ref[LEVELS * f + l, c, at, :]

        def second(f, c, at):
            return r1[f, c, at, :]

        @pl.loop(SOUTH, end + 1, unroll=UNROLL1)
        def _(t):
            for f, c, value in update(l, t, first):
                r1[f, c, rows(t), :] = value

        def at_top(f, c, load):
            v, v_mirror = v2_ref[l, c, rows(end - 1), :], v2_ref[l, c, rows(end - 1, 2), :]
            r, r_mirror = load(f, c, rows(end - 1)), load(f, c, rows(end - 1, 1))
            add = seam(r, r_mirror, v, v_mirror, w_ref[l, c, rows(end - 1), :], sign_of(f))
            return jnp.where(sub == SUBS - 1, add, 0.0)

        @pl.when(top)
        def _():
            for f in range(FIELDS):
                for c in range(2):
                    v_top, v_mirror = v2_ref[l, c, rows(end, -1), :], v2_ref[l, c, rows(end, 1), :]
                    r, r_top = first(f, c, rows(end)), first(f, c, rows(end, -1))
                    add = seam_mirror(r, r_top, v_top, v_mirror, w_ref[l, c, rows(end), :], sign_of(f))
                    r1[f, c, rows(end), :] += jnp.where(sub == 0, add, 0.0)
                    r1[f, c, rows(end - 1), :] += at_top(f, c, first)

        @pl.loop(OWN, end, unroll=UNROLL2)
        def _(t):
            for f, c, value in update(l, t, second):
                o_ref[f, l, rows(t - OWN), cols(c)] = value

        @pl.when(top)
        def _():
            for f in range(FIELDS):
                for c in range(2):
                    o_ref[f, l, rows(tiles - 1), cols(c)] += at_top(f, c, second)


def edge_kernel(k_ref, p_ref, q_ref, i_ref, o_ref, z, z1, buf, sems):
    lane, sub = iota(1), iota(0)
    _, top = lat_place()
    lon_even = lax.axis_index("lon") % 2 == 0
    tiles = i_ref.shape[2] // SUBS
    end = OWN + tiles
    pair = lane // 2 % 8

    def join(t):
        p, q = p_ref[rows(t), :], q_ref[rows(t), :]
        from_west, from_east = jnp.where(lon_even, q, p), jnp.where(lon_even, p, q)
        out = []
        for g in range(5):
            back = (LANES - 2 * g) % LANES
            west, east = (pltpu.roll(x, back, 1) if back else x for x in (from_west, from_east))
            out.append(jnp.where(pair == 1, west, jnp.where(pair == 6, east, k_ref[g, rows(t), :])))
        return out

    @pl.loop(0, tiles, unroll=True)
    def _(t):
        for g, value in enumerate(join(t)):
            z[g, rows(t + OWN), :] = value

    for g, value in enumerate(join(tiles)):
        z[g, rows(SOUTH), :] = value
        if g == 2:
            value = jnp.where(top & (sub == 0), -pltpu.roll(value, LANES - 1, 1), value)
        z[g, rows(end), :] = value

    def update(t, load, mirrored):
        u, v, v_south, w = z[2, rows(t), :], z[3, rows(t), :], z[3, rows(t, -1), :], z[4, rows(t), :]
        u_west = pltpu.roll(u, 1, 1)
        out = []
        for h in range(2):
            r, r_north, r_south = load(h, rows(t)), load(h, rows(t, 1)), load(h, rows(t, -1))
            along = u * (pltpu.roll(r, LANES - 1, 1) - r) + u_west * (r - pltpu.roll(r, 1, 1))
            value = w * (r + along + v * (r_north - r) + v_south * (r - r_south))
            add = seam(r, r_north, v, z[3, rows(t, 2), :], w, sign_of(2 * h))
            value += jnp.where(top & (t == end - 1) & (sub == SUBS - 1), add, 0.0)
            if mirrored:
                add = seam_mirror(r, r_south, v_south, z[3, rows(t, 1), :], w, sign_of(2 * h))
                value += jnp.where(top & (t == end) & (sub == 0), add, 0.0)
            out.append(value)
        return out

    @pl.loop(SOUTH, end + 1, unroll=True)
    def _(t):
        for h, value in enumerate(update(t, lambda h, at: z[h, at, :], True)):
            z1[h, rows(t), :] = value

    def send(t):
        at = rows(t)
        return pltpu.make_async_copy(buf.at[:, :, at, :], o_ref.at[:, :, at, :], sems.at[t])

    @pl.loop(0, tiles, unroll=UNROLL2)
    def _(t):
        value = update(t + OWN, lambda h, at: z1[h, at, :], False)
        for f in range(FIELDS):
            for l in range(LEVELS):
                seg = 16 * (LEVELS * (f % 2) + l)
                west = pltpu.roll(value[f // 2], LANES - 4 - seg, 1)
                east = pltpu.roll(value[f // 2], (LANES + 116 - seg) % LANES, 1)
                buf[f, l, rows(t), cols(0)] = jnp.where(lane < 2, west, i_ref[f, l, rows(t), cols(0)])
                buf[f, l, rows(t), cols(1)] = jnp.where(lane >= LANES - 2, east, i_ref[f, l, rows(t), cols(1)])
        send(t).start()

    @pl.loop(0, tiles)
    def _(t):
        send(t).wait()


def per_device(state_adjoint, east_velocity, north_velocity, ocean_mask, partner):
    nlon, nlat = lax.axis_size("lon"), lax.axis_size("lat")
    fields, levels, height, width = state_adjoint.shape
    axes = ("lon", "lat")
    f32 = jnp.float32

    def device(lon, lat):
        return lon % nlon * nlat + lat

    def both(a, b):
        return [(a, b), (b, a)]

    fold = [(device(nlon - 1 - i, nlat - 1), device(i, nlat - 1)) for i in range(nlon)]
    fold_next = [(device(nlon - i, nlat - 1), device(i, nlat - 1)) for i in range(nlon)]
    within = [e for i in range(nlon) for j in range(0, nlat, 2) for e in both(device(i, j), device(i, j + 1))]
    across = [e for i in range(nlon) for j in range(1, nlat - 1, 2) for e in both(device(i, j), device(i, j + 1))]
    even = [e for i in range(0, nlon, 2) for j in range(nlat) for e in both(device(i, j), device(i + 1, j))]
    odd = [e for i in range(1, nlon, 2) for j in range(nlat) for e in both(device(i, j), device(i + 1, j))]

    def held(x):
        return pltpu.with_memory_space_constraint(x, pltpu.VMEM)

    def call(kernel, name, args, outs, scratch=(), aliases=None, micros=1):
        return pl.pallas_call(
            kernel,
            out_shape=tuple(pltpu.VMEM(shape, f32) for shape in outs),
            in_specs=[VMEM] * len(args),
            out_specs=(VMEM,) * len(outs),
            scratch_shapes=[pltpu.VMEM(shape, f32) for shape in scratch],
            input_output_aliases=aliases or {},
            cost_estimate=pl.CostEstimate(flops=0, bytes_accessed=micros * 3_000_000, transcendentals=0),
            compiler_params=pltpu.CompilerParams(vmem_limit_bytes=SCOPED),
            name=name,
        )(*(held(x) for x in args))

    inputs = (state_adjoint, east_velocity, north_velocity, ocean_mask)
    message = (16 * levels, width)
    to_a, to_b = pl.pallas_call(
        row_kernel,
        out_shape=(pltpu.VMEM(message, f32), pltpu.VMEM(message, f32)),
        in_specs=[pl.BlockSpec(memory_space=pltpu.HBM)] * 4,
        out_specs=(VMEM,) * 2,
        scratch_shapes=[pltpu.VMEM((2,) + x.shape[:-2] + (SUBS, width), x.dtype) for x in inputs]
        + [pltpu.SemaphoreType.DMA((4, 2))],
        compiler_params=pltpu.CompilerParams(vmem_limit_bytes=SCOPED),
        name="pack_rows",
    )(*(pltpu.with_memory_space_constraint(x, pltpu.HBM) for x in inputs))
    from_a = lax.ppermute(to_a, axes, within)
    from_b = lax.ppermute(to_b, axes, across + fold)
    to_f, _ = lax.optimization_barrier((to_b, from_a))
    from_f = lax.ppermute(to_f, axes, fold_next)

    tall = height + 4 * SUBS
    ext = [(fields * levels, 2, tall, LANES)] + [(levels, 2, tall, LANES)] * 3
    pack = (height + SUBS, LANES)
    laid = call(prepare_kernel, "prepare", inputs, (*ext, (5,) + pack, pack, pack))
    *laid, packs, to_p, to_q = call(
        halo_kernel,
        "place_rows",
        (partner.reshape(2, LANES), from_a, from_b, from_f, *laid),
        (*ext, (5,) + pack, pack, pack),
        [(2, message[0] + 2 * SUBS, LANES)] * 2,
        aliases={4 + i: i for i in range(7)},
    )
    from_p = lax.ppermute(to_p, axes, even)
    from_q = lax.ppermute(to_q, axes, odd)

    (inner,) = call(step_kernel, "both_steps", laid, (state_adjoint.shape,), [(fields, 2, tall, LANES)], micros=3)
    return pl.pallas_call(
        edge_kernel,
        out_shape=jax.ShapeDtypeStruct(state_adjoint.shape, f32),
        in_specs=[VMEM] * 4,
        out_specs=pl.BlockSpec(memory_space=pl.ANY),
        scratch_shapes=[
            pltpu.VMEM((5, tall, LANES), f32),
            pltpu.VMEM((2, tall, LANES), f32),
            pltpu.VMEM(state_adjoint.shape, f32),
            pltpu.SemaphoreType.DMA((height // SUBS,)),
        ],
        compiler_params=pltpu.CompilerParams(vmem_limit_bytes=SCOPED),
        name="edge_columns",
    )(*(held(x) for x in (packs, from_p, from_q, inner)))


def solution(mesh):
    placed = (
        P(None, None, "lat", "lon"),
        P(None, "lat", "lon"),
        P(None, "lat", "lon"),
        P(None, "lat", "lon"),
        P("lon"),
    )
    return jax.shard_map(
        per_device,
        mesh=mesh,
        in_specs=placed,
        out_specs=P(None, None, "lat", "lon"),
        check_vma=False,
    )
```

```python
import jax
import jax.numpy as jnp
from jax import lax
from jax.experimental import pallas as pl
from jax.experimental.pallas import tpu as pltpu
from jax.sharding import PartitionSpec as P

FIELDS, LEVELS = 4, 4
QN = FIELDS + 3
LANES, SUBS = 128, 8
SOUTH, OWN = 1, 2
VMEM = pl.BlockSpec(memory_space=pltpu.VMEM)
SCOPED = 4 << 20
UNROLL1, UNROLL2 = 10, 8


def iota(dim):
    return lax.broadcasted_iota(jnp.int32, (SUBS, LANES), dim)


def rows(t, by=0):
    start = SUBS * t
    if not isinstance(start, int):
        start = pl.multiple_of(start, SUBS)
    return pl.ds(start + by, SUBS)


def cols(c):
    return pl.ds(LANES * c, LANES)


def lat_place():
    lat = lax.axis_index("lat")
    return lat % 2 == 0, lat == lax.axis_size("lat") - 1


def sign_of(field):
    return 1.0 if field < 2 else -1.0


def row_kernel(s_in, u_in, v_in, m_in, a_ref, b_ref, s_ref, u_ref, v_ref, m_ref, sems):
    lat_even, _ = lat_place()
    sub = iota(0)
    copies = []
    for i, (src, dst) in enumerate(((s_in, s_ref), (u_in, u_ref), (v_in, v_ref), (m_in, m_ref))):
        lead = (slice(None),) * (len(src.shape) - 2)
        for k, t in enumerate((0, src.shape[-2] // SUBS - 1)):
            copies.append(pltpu.make_async_copy(src.at[lead + (rows(t), slice(None))], dst.at[k], sems.at[i, k]))
    for copy in copies:
        copy.start()
    for copy in copies:
        copy.wait()

    @pl.loop(0, LEVELS)
    def _(l):
        for c in range(2):
            both = []
            for k in range(2):
                w = m_ref[k, l, :, cols(c)].astype(jnp.float32)
                values = [s_ref[k, f, l, :, cols(c)] * w for f in range(FIELDS)]
                both.append(values + [0.5 * u_ref[k, l, :, cols(c)], 0.5 * v_ref[k, l, :, cols(c)], w, w])
            for g in range(2):
                low, high = both[0][4 * g], pltpu.roll(both[1][4 * g], 2, 0)
                for k in range(1, 4):
                    low = jnp.where(sub // 2 == k, pltpu.roll(both[0][4 * g + k], 2 * k, 0), low)
                    high = jnp.where(sub // 2 == k, pltpu.roll(both[1][4 * g + k], (2 * k + 2) % SUBS, 0), high)
                a_ref[rows(2 * l + g), cols(c)] = jnp.where(lat_even, high, low)
                b_ref[rows(2 * l + g), cols(c)] = jnp.where(lat_even, low, high)


def insert(packs, quarter, l, q, side, tile):
    seg = LEVELS * (q % 2) + l if q < FIELDS else l
    g = q // 2 if q < FIELDS else q - 2
    moved = pltpu.roll(tile, (16 * seg + (12 if side else 4)) % LANES, 1)
    packs[g] = jnp.where(quarter == 4 * seg + 1 + side, moved, packs[g])


def finish(packs, lane):
    for g in range(2, 5):
        packs[g] = jnp.where(lane < LANES // 2, packs[g], pltpu.roll(packs[g], LANES // 2, 1))


def outgoing(packs, lane, lon_even):
    east = jnp.zeros((SUBS, LANES), jnp.float32)
    west = jnp.zeros((SUBS, LANES), jnp.float32)
    pair = lane // 2 % 8
    for g, tile in enumerate(packs):
        east = jnp.where(pair == 1 + g, pltpu.roll(tile, LANES - 8 + 2 * g, 1), east)
        west = jnp.where(pair == (6 + g) % 8, pltpu.roll(tile, 8 + 2 * g, 1), west)
    return jnp.where(lon_even, east, west), jnp.where(lon_even, west, east)


def prepare_kernel(s_ref, u_ref, v_ref, m_ref, r_ref, u2_ref, v2_ref, w_ref, k_ref, p_ref, q_ref):
    lane = iota(1)
    quarter = lane // 4
    lon_even = lax.axis_index("lon") % 2 == 0

    @pl.loop(0, s_ref.shape[2] // SUBS, unroll=2)
    def _(t):
        src, dst = rows(t), rows(t + OWN)
        packs = [jnp.zeros((SUBS, LANES), jnp.float32)] * 5
        for l in range(LEVELS):
            for c in range(2):
                w = m_ref[l, src, cols(c)].astype(jnp.float32)
                values = [s_ref[f, l, src, cols(c)] * w for f in range(FIELDS)]
                values += [0.5 * u_ref[l, src, cols(c)], 0.5 * v_ref[l, src, cols(c)], w]
                for q, value in enumerate(values):
                    ref = (u2_ref, v2_ref, w_ref)[q - FIELDS] if q >= FIELDS else r_ref
                    ref[LEVELS * q + l if q < FIELDS else l, c, dst, :] = value
                    insert(packs, quarter, l, q, c, value)
        finish(packs, lane)
        for g in range(5):
            k_ref[g, src, :] = packs[g]
        p_ref[src, :], q_ref[src, :] = outgoing(packs, lane, lon_even)


def partner_columns(c_ref, width):
    ncol = lax.axis_size("lon") * width
    lon = lax.axis_index("lon")
    return [lax.rem(c_ref[pl.ds(c, SUBS, stride=0), :] + (lon + 1) * width, ncol) for c in range(2)]


def halo_kernel(
    a_ref, b_ref, r_in, u2_in, v2_in, w_in, k_in, p_in, q_in,
    r_ref, u2_ref, v2_ref, w_ref, k_ref, p_ref, q_ref, north, south,
):
    lane, sub = iota(1), iota(0)
    quarter = lane // 4
    lat_even, top = lat_place()
    lon_even = lax.axis_index("lon") % 2 == 0
    tiles = k_ref.shape[1] // SUBS - 1

    @pl.loop(0, 2 * LEVELS)
    def _(i):
        for c in range(2):
            a, b = a_ref[rows(i), cols(c)], b_ref[rows(i), cols(c)]
            north[c, rows(i + 1), :] = jnp.where(lat_even, a, b)
            south[c, rows(i + 1), :] = jnp.where(lat_even, b, a)

    packs = [jnp.zeros((SUBS, LANES), jnp.float32)] * 5
    for l in range(LEVELS):
        for q in range(QN):
            ref = (u2_ref, v2_ref, w_ref)[q - FIELDS] if q >= FIELDS else r_ref
            index = LEVELS * q + l if q < FIELDS else l
            at = SUBS + 16 * l + 2 * q
            tile = []
            for c in range(2):
                tile.append(jnp.where(sub < 4, north[c, pl.ds(at, SUBS), :], south[c, pl.ds(at - 6, SUBS), :]))
                ref[index, c, rows(SOUTH), :] = tile[c]
                ref[index, c, rows(tiles + OWN), :] = tile[c]
            last = pltpu.roll(tile[1], 1, 1)
            insert(packs, quarter, l, q, 0, jnp.where(top & (sub < 2), last, tile[0]))
            insert(packs, quarter, l, q, 1, tile[1])
    finish(packs, lane)
    for g in range(5):
        k_ref[g, rows(tiles), :] = packs[g]
    p_ref[rows(tiles), :], q_ref[rows(tiles), :] = outgoing(packs, lane, lon_even)


def mirror_kernel(
    c_ref, b_ref, f_ref, r_in, u2_in, v2_in, w_in, k_in, r_ref, u2_ref, v2_ref, w_ref, k_ref, mirrored
):
    lane, sub = iota(1), iota(0)
    quarter = lane // 4
    _, top = lat_place()
    width = b_ref.shape[1]
    tiles = k_ref.shape[1] // SUBS - 1

    @pl.when(top)
    def _():
        source = partner_columns(c_ref, width)
        before = jnp.broadcast_to(source[0][:, :1] + 1, (SUBS, LANES))
        after = jnp.broadcast_to(jnp.maximum(source[1][:, LANES - 1 :] - 1, 0), (SUBS, LANES))

        @pl.loop(0, LEVELS)
        def _(l):
            for g in range(2):
                raw = [(b_ref if s < 2 else f_ref)[rows(2 * l + g), cols(s % 2)] for s in range(4)]
                for c, p in enumerate((*source, before, after)):
                    got = jnp.zeros((SUBS, LANES), jnp.float32)
                    for s in range(4):
                        picked = jnp.take_along_axis(raw[s], p % LANES, axis=1, mode="promise_in_bounds")
                        got = jnp.where(p // LANES == s, picked, got)
                    swapped = jnp.where(sub % 2 == 0, pltpu.roll(got, SUBS - 1, 0), pltpu.roll(got, 1, 0))
                    if g == 1:
                        swapped = jnp.where(sub == 2, -got, jnp.where(sub == 3, got, swapped))
                    mirrored[c, rows(2 * l + g), :] = swapped

        packs = [jnp.zeros((SUBS, LANES), jnp.float32)] * 5
        for l in range(LEVELS):
            for q in range(QN):
                ref = (u2_ref, v2_ref, w_ref)[q - FIELDS] if q >= FIELDS else r_ref
                index = LEVELS * q + l if q < FIELDS else l
                seg = LEVELS * (q % 2) + l if q < FIELDS else l
                pack = q // 2 if q < FIELDS else q - 2
                tile = [mirrored[c, pl.ds(16 * l + 2 * q, SUBS), :] for c in range(4)]
                for c in range(2):
                    insert(packs, quarter, l, q, c, tile[c])
                    north = tile[c]
                    if q == FIELDS:
                        north = -pltpu.roll(jnp.where(lane == 0, tile[1 - c], tile[c]), LANES - 1, 1)
                    ref[index, c, rows(tiles + OWN), :] = north
                packs[pack] = jnp.where(lane == 16 * seg + 3, tile[2], packs[pack])
                packs[pack] = jnp.where(lane == 16 * seg + 12, tile[3], packs[pack])
        finish(packs, lane)
        for g in range(5):
            k_ref[g, rows(tiles), :] = jnp.where(sub < 2, packs[g], k_in[g, rows(tiles), :])


def seam(r, r_mirror, h, h_mirror, w, sign):
    return w * r_mirror * (sign * (0.5 + h_mirror) - h)


def seam_mirror(r, r_top, h_top, h, w, sign):
    return w * (sign * (0.5 + h_top) * r_top - h * r - h_top * (r - r_top))


def step_kernel(r_ref, u2_ref, v2_ref, w_ref, o_ref, r1):
    lane, sub = iota(1), iota(0)
    _, top = lat_place()
    tiles = o_ref.shape[2] // SUBS
    end = OWN + tiles

    def update(l, t, load):
        u = [u2_ref[l, c, rows(t), :] for c in range(2)]
        u_west = [pltpu.roll(jnp.where(lane == LANES - 1, u[1 - c], u[c]), 1, 1) for c in range(2)]
        v = [v2_ref[l, c, rows(t), :] for c in range(2)]
        v_south = [v2_ref[l, c, rows(t, -1), :] for c in range(2)]
        w = [w_ref[l, c, rows(t), :] for c in range(2)]
        out = []
        for f in range(FIELDS):
            r = [load(f, c, rows(t)) for c in range(2)]
            for c in range(2):
                ahead = pltpu.roll(jnp.where(lane == 0, r[1 - c], r[c]), LANES - 1, 1)
                behind = pltpu.roll(jnp.where(lane == LANES - 1, r[1 - c], r[c]), 1, 1)
                along = u[c] * (ahead - r[c]) + u_west[c] * (r[c] - behind)
                up = v[c] * (load(f, c, rows(t, 1)) - r[c])
                down = v_south[c] * (r[c] - load(f, c, rows(t, -1)))
                out.append((f, c, w[c] * (r[c] + along + up + down)))
        return out

    @pl.loop(0, LEVELS)
    def _(l):
        def first(f, c, at):
            return r_ref[LEVELS * f + l, c, at, :]

        def second(f, c, at):
            return r1[f, c, at, :]

        @pl.loop(SOUTH, end + 1, unroll=UNROLL1)
        def _(t):
            for f, c, value in update(l, t, first):
                r1[f, c, rows(t), :] = value

        def at_top(f, c, load):
            v, v_mirror = v2_ref[l, c, rows(end - 1), :], v2_ref[l, c, rows(end - 1, 2), :]
            r, r_mirror = load(f, c, rows(end - 1)), load(f, c, rows(end - 1, 1))
            add = seam(r, r_mirror, v, v_mirror, w_ref[l, c, rows(end - 1), :], sign_of(f))
            return jnp.where(sub == SUBS - 1, add, 0.0)

        @pl.when(top)
        def _():
            for f in range(FIELDS):
                for c in range(2):
                    v_top, v_mirror = v2_ref[l, c, rows(end, -1), :], v2_ref[l, c, rows(end, 1), :]
                    r, r_top = first(f, c, rows(end)), first(f, c, rows(end, -1))
                    add = seam_mirror(r, r_top, v_top, v_mirror, w_ref[l, c, rows(end), :], sign_of(f))
                    r1[f, c, rows(end), :] += jnp.where(sub == 0, add, 0.0)
                    r1[f, c, rows(end - 1), :] += at_top(f, c, first)

        @pl.loop(OWN, end, unroll=UNROLL2)
        def _(t):
            for f, c, value in update(l, t, second):
                o_ref[f, l, rows(t - OWN), cols(c)] = value

        @pl.when(top)
        def _():
            for f in range(FIELDS):
                for c in range(2):
                    o_ref[f, l, rows(tiles - 1), cols(c)] += at_top(f, c, second)


def edge_kernel(c_ref, k_ref, q_ref, p_ref, i_ref, o_ref, z, z1, buf, sems):
    lane, sub = iota(1), iota(0)
    _, top = lat_place()
    lon_even = lax.axis_index("lon") % 2 == 0
    tiles = i_ref.shape[2] // SUBS
    end = OWN + tiles
    pair = lane // 2 % 8

    def join(t):
        p, q = p_ref[rows(t), :], q_ref[rows(t), :]
        from_west, from_east = jnp.where(lon_even, q, p), jnp.where(lon_even, p, q)
        out = []
        for g in range(5):
            back = (LANES - 2 * g) % LANES
            west, east = (pltpu.roll(x, back, 1) if back else x for x in (from_west, from_east))
            out.append(jnp.where(pair == 1, west, jnp.where(pair == 6, east, k_ref[g, rows(t), :])))
        return out

    @pl.loop(0, tiles, unroll=True)
    def _(t):
        for g, value in enumerate(join(t)):
            z[g, rows(t + OWN), :] = value

    at_seam = partner_columns(c_ref, i_ref.shape[3])[1][:, LANES - 1 :] == 0
    p, q = p_ref[rows(tiles), :], q_ref[rows(tiles), :]
    for g, value in enumerate(join(tiles)):
        z[g, rows(SOUTH), :] = value
        crossed = pltpu.roll(jnp.where(lon_even, p, q), (LANES - 2 * g) % LANES, 1) if g else jnp.where(lon_even, p, q)
        if g != 3:
            crossed = pltpu.roll(crossed, SUBS - 1, 0)
        kept = jnp.where((pair == 6) & at_seam, crossed, k_ref[g, rows(tiles), :])
        value = jnp.where(top & (sub < 2), kept, value)
        if g == 2:
            value = jnp.where(top & (sub == 0), -pltpu.roll(value, LANES - 1, 1), value)
        z[g, rows(end), :] = value

    def update(t, load, mirrored):
        u, v, v_south, w = z[2, rows(t), :], z[3, rows(t), :], z[3, rows(t, -1), :], z[4, rows(t), :]
        u_west = pltpu.roll(u, 1, 1)
        out = []
        for h in range(2):
            r, r_north, r_south = load(h, rows(t)), load(h, rows(t, 1)), load(h, rows(t, -1))
            along = u * (pltpu.roll(r, LANES - 1, 1) - r) + u_west * (r - pltpu.roll(r, 1, 1))
            value = w * (r + along + v * (r_north - r) + v_south * (r - r_south))
            add = seam(r, r_north, v, z[3, rows(t, 2), :], w, sign_of(2 * h))
            value += jnp.where(top & (t == end - 1) & (sub == SUBS - 1), add, 0.0)
            if mirrored:
                add = seam_mirror(r, r_south, v_south, z[3, rows(t, 1), :], w, sign_of(2 * h))
                value += jnp.where(top & (t == end) & (sub == 0), add, 0.0)
            out.append(value)
        return out

    @pl.loop(SOUTH, end + 1, unroll=True)
    def _(t):
        for h, value in enumerate(update(t, lambda h, at: z[h, at, :], True)):
            z1[h, rows(t), :] = value

    def send(t):
        at = rows(t)
        return pltpu.make_async_copy(buf.at[:, :, at, :], o_ref.at[:, :, at, :], sems.at[t])

    @pl.loop(0, tiles, unroll=UNROLL2)
    def _(t):
        value = update(t + OWN, lambda h, at: z1[h, at, :], False)
        for f in range(FIELDS):
            for l in range(LEVELS):
                seg = 16 * (LEVELS * (f % 2) + l)
                west = pltpu.roll(value[f // 2], LANES - 4 - seg, 1)
                east = pltpu.roll(value[f // 2], (LANES + 116 - seg) % LANES, 1)
                buf[f, l, rows(t), cols(0)] = jnp.where(lane < 2, west, i_ref[f, l, rows(t), cols(0)])
                buf[f, l, rows(t), cols(1)] = jnp.where(lane >= LANES - 2, east, i_ref[f, l, rows(t), cols(1)])
        send(t).start()

    @pl.loop(0, tiles)
    def _(t):
        send(t).wait()


def per_device(state_adjoint, east_velocity, north_velocity, ocean_mask, partner):
    nlon, nlat = lax.axis_size("lon"), lax.axis_size("lat")
    fields, levels, height, width = state_adjoint.shape
    axes = ("lon", "lat")
    f32 = jnp.float32

    def device(lon, lat):
        return lon % nlon * nlat + lat

    def both(a, b):
        return [(a, b), (b, a)]

    fold = [(device(nlon - 1 - i, nlat - 1), device(i, nlat - 1)) for i in range(nlon)]
    fold_next = [(device(nlon - i, nlat - 1), device(i, nlat - 1)) for i in range(nlon)]
    within = [e for i in range(nlon) for j in range(0, nlat, 2) for e in both(device(i, j), device(i, j + 1))]
    across = [e for i in range(nlon) for j in range(1, nlat - 1, 2) for e in both(device(i, j), device(i, j + 1))]
    even = [e for i in range(0, nlon, 2) for j in range(nlat) for e in both(device(i, j), device(i + 1, j))]
    odd = [e for i in range(1, nlon, 2) for j in range(nlat) for e in both(device(i, j), device(i + 1, j))]

    def held(x):
        return pltpu.with_memory_space_constraint(x, pltpu.VMEM)

    def call(kernel, name, args, outs, scratch=(), aliases=None, micros=1):
        return pl.pallas_call(
            kernel,
            out_shape=tuple(pltpu.VMEM(shape, f32) for shape in outs),
            in_specs=[VMEM] * len(args),
            out_specs=(VMEM,) * len(outs),
            scratch_shapes=[pltpu.VMEM(shape, f32) for shape in scratch],
            input_output_aliases=aliases or {},
            cost_estimate=pl.CostEstimate(flops=0, bytes_accessed=micros * 3_000_000, transcendentals=0),
            compiler_params=pltpu.CompilerParams(vmem_limit_bytes=SCOPED),
            name=name,
        )(*(held(x) for x in args))

    inputs = (state_adjoint, east_velocity, north_velocity, ocean_mask)
    message = (16 * levels, width)
    to_a, to_b = pl.pallas_call(
        row_kernel,
        out_shape=(pltpu.VMEM(message, f32), pltpu.VMEM(message, f32)),
        in_specs=[pl.BlockSpec(memory_space=pltpu.HBM)] * 4,
        out_specs=(VMEM,) * 2,
        scratch_shapes=[pltpu.VMEM((2,) + x.shape[:-2] + (SUBS, width), x.dtype) for x in inputs]
        + [pltpu.SemaphoreType.DMA((4, 2))],
        compiler_params=pltpu.CompilerParams(vmem_limit_bytes=SCOPED),
        name="pack_rows",
    )(*(pltpu.with_memory_space_constraint(x, pltpu.HBM) for x in inputs))
    from_a = lax.ppermute(to_a, axes, within)
    from_b = lax.ppermute(to_b, axes, across + fold)
    from_f = lax.ppermute(to_b, axes, fold_next)

    tall = height + 4 * SUBS
    ext = [(fields * levels, 2, tall, LANES)] + [(levels, 2, tall, LANES)] * 3
    pack = (height + SUBS, LANES)
    laid = call(prepare_kernel, "prepare", inputs, (*ext, (5,) + pack, pack, pack))
    *laid, to_p, to_q = call(
        halo_kernel,
        "place_rows",
        (from_a, from_b, *laid),
        (*ext, (5,) + pack, pack, pack),
        [(2, message[0] + 2 * SUBS, LANES)] * 2,
        aliases={2 + i: i for i in range(7)},
    )
    from_p = lax.ppermute(to_p, axes, even)
    from_q = lax.ppermute(to_q, axes, odd)

    pairs = partner.reshape(2, LANES)
    *laid, packs = call(
        mirror_kernel,
        "mirror_rows",
        (pairs, from_b, from_f, *laid),
        (*ext, (5,) + pack),
        [(4, message[0] + SUBS, LANES)],
        aliases={3 + i: i for i in range(5)},
    )
    (inner,) = call(step_kernel, "both_steps", laid, (state_adjoint.shape,), [(fields, 2, tall, LANES)], micros=3)
    return pl.pallas_call(
        edge_kernel,
        out_shape=jax.ShapeDtypeStruct(state_adjoint.shape, f32),
        in_specs=[VMEM] * 5,
        out_specs=pl.BlockSpec(memory_space=pl.ANY),
        scratch_shapes=[
            pltpu.VMEM((5, tall, LANES), f32),
            pltpu.VMEM((2, tall, LANES), f32),
            pltpu.VMEM(state_adjoint.shape, f32),
            pltpu.SemaphoreType.DMA((height // SUBS,)),
        ],
        compiler_params=pltpu.CompilerParams(vmem_limit_bytes=SCOPED),
        name="edge_columns",
    )(*(held(x) for x in (pairs, packs, from_q, from_p, inner)))


def solution(mesh):
    placed = (
        P(None, None, "lat", "lon"),
        P(None, "lat", "lon"),
        P(None, "lat", "lon"),
        P(None, "lat", "lon"),
        P("lon"),
    )
    return jax.shard_map(
        per_device,
        mesh=mesh,
        in_specs=placed,
        out_specs=P(None, None, "lat", "lon"),
        check_vma=False,
    )
```

```python
import jax
import jax.numpy as jnp
from jax import lax
from jax.experimental import pallas as pl
from jax.experimental.pallas import tpu as pltpu
from jax.sharding import PartitionSpec as P

FIELDS, LEVELS = 4, 4
QN = FIELDS + 3
LANES, SUBS = 128, 8
SOUTH, OWN = 1, 2
VMEM = pl.BlockSpec(memory_space=pltpu.VMEM)
SCOPED = 4 << 20
UNROLL1, UNROLL2 = 10, 8


def iota(dim):
    return lax.broadcasted_iota(jnp.int32, (SUBS, LANES), dim)


def rows(t, by=0):
    start = SUBS * t
    if not isinstance(start, int):
        start = pl.multiple_of(start, SUBS)
    return pl.ds(start + by, SUBS)


def cols(c):
    return pl.ds(LANES * c, LANES)


def lat_place():
    lat = lax.axis_index("lat")
    return lat % 2 == 0, lat == lax.axis_size("lat") - 1


def sign_of(field):
    return 1.0 if field < 2 else -1.0


def row_kernel(s_in, u_in, v_in, m_in, a_ref, b_ref, s_ref, u_ref, v_ref, m_ref, sems):
    lat_even, _ = lat_place()
    sub = iota(0)
    copies = []
    for i, (src, dst) in enumerate(((s_in, s_ref), (u_in, u_ref), (v_in, v_ref), (m_in, m_ref))):
        lead = (slice(None),) * (len(src.shape) - 2)
        for k, t in enumerate((0, src.shape[-2] // SUBS - 1)):
            copies.append(pltpu.make_async_copy(src.at[lead + (rows(t), slice(None))], dst.at[k], sems.at[i, k]))
    for copy in copies:
        copy.start()
    for copy in copies:
        copy.wait()

    @pl.loop(0, LEVELS)
    def _(l):
        for c in range(2):
            both = []
            for k in range(2):
                w = m_ref[k, l, :, cols(c)].astype(jnp.float32)
                values = [s_ref[k, f, l, :, cols(c)] * w for f in range(FIELDS)]
                both.append(values + [0.5 * u_ref[k, l, :, cols(c)], 0.5 * v_ref[k, l, :, cols(c)], w, w])
            for g in range(2):
                low, high = both[0][4 * g], pltpu.roll(both[1][4 * g], 2, 0)
                for k in range(1, 4):
                    low = jnp.where(sub // 2 == k, pltpu.roll(both[0][4 * g + k], 2 * k, 0), low)
                    high = jnp.where(sub // 2 == k, pltpu.roll(both[1][4 * g + k], (2 * k + 2) % SUBS, 0), high)
                a_ref[rows(2 * l + g), cols(c)] = jnp.where(lat_even, high, low)
                b_ref[rows(2 * l + g), cols(c)] = jnp.where(lat_even, low, high)


def insert(packs, quarter, l, q, side, tile):
    seg = LEVELS * (q % 2) + l if q < FIELDS else l
    g = q // 2 if q < FIELDS else q - 2
    moved = pltpu.roll(tile, (16 * seg + (12 if side else 4)) % LANES, 1)
    packs[g] = jnp.where(quarter == 4 * seg + 1 + side, moved, packs[g])


def finish(packs, lane):
    for g in range(2, 5):
        packs[g] = jnp.where(lane < LANES // 2, packs[g], pltpu.roll(packs[g], LANES // 2, 1))


def outgoing(packs, lane, lon_even, seam_rows=None):
    east = jnp.zeros((SUBS, LANES), jnp.float32)
    west = jnp.zeros((SUBS, LANES), jnp.float32)
    pair = lane // 2 % 8
    for g, tile in enumerate(packs):
        east = jnp.where(pair == 1 + g, pltpu.roll(tile, LANES - 8 + 2 * g, 1), east)
        first = pltpu.roll(tile, 8 + 2 * g, 1)
        if seam_rows is not None:
            first = jnp.where(seam_rows, pltpu.roll(tile, 1 + 2 * g, 1), first)
        west = jnp.where(pair == (6 + g) % 8, first, west)
    return jnp.where(lon_even, east, west), jnp.where(lon_even, west, east)


def prepare_kernel(s_ref, u_ref, v_ref, m_ref, r_ref, u2_ref, v2_ref, w_ref, k_ref, p_ref, q_ref):
    lane = iota(1)
    quarter = lane // 4
    lon_even = lax.axis_index("lon") % 2 == 0

    @pl.loop(0, s_ref.shape[2] // SUBS, unroll=2)
    def _(t):
        src, dst = rows(t), rows(t + OWN)
        packs = [jnp.zeros((SUBS, LANES), jnp.float32)] * 5
        for l in range(LEVELS):
            for c in range(2):
                w = m_ref[l, src, cols(c)].astype(jnp.float32)
                values = [s_ref[f, l, src, cols(c)] * w for f in range(FIELDS)]
                values += [0.5 * u_ref[l, src, cols(c)], 0.5 * v_ref[l, src, cols(c)], w]
                for q, value in enumerate(values):
                    ref = (u2_ref, v2_ref, w_ref)[q - FIELDS] if q >= FIELDS else r_ref
                    ref[LEVELS * q + l if q < FIELDS else l, c, dst, :] = value
                    insert(packs, quarter, l, q, c, value)
        finish(packs, lane)
        for g in range(5):
            k_ref[g, src, :] = packs[g]
        p_ref[src, :], q_ref[src, :] = outgoing(packs, lane, lon_even)


def partner_columns(c_ref, width):
    ncol = lax.axis_size("lon") * width
    lon = lax.axis_index("lon")
    return [lax.rem(c_ref[pl.ds(c, SUBS, stride=0), :] + (lon + 1) * width, ncol) for c in range(2)]


def halo_kernel(
    a_ref, b_ref, r_in, u2_in, v2_in, w_in, k_in, p_in, q_in,
    r_ref, u2_ref, v2_ref, w_ref, k_ref, p_ref, q_ref, north, south,
):
    lane, sub = iota(1), iota(0)
    quarter = lane // 4
    lat_even, top = lat_place()
    lon_even = lax.axis_index("lon") % 2 == 0
    tiles = k_ref.shape[1] // SUBS - 1

    @pl.loop(0, 2 * LEVELS)
    def _(i):
        for c in range(2):
            a, b = a_ref[rows(i), cols(c)], b_ref[rows(i), cols(c)]
            north[c, rows(i + 1), :] = jnp.where(lat_even, a, b)
            south[c, rows(i + 1), :] = jnp.where(lat_even, b, a)

    packs = [jnp.zeros((SUBS, LANES), jnp.float32)] * 5
    for l in range(LEVELS):
        for q in range(QN):
            ref = (u2_ref, v2_ref, w_ref)[q - FIELDS] if q >= FIELDS else r_ref
            index = LEVELS * q + l if q < FIELDS else l
            at = SUBS + 16 * l + 2 * q
            tile = []
            for c in range(2):
                tile.append(jnp.where(sub < 4, north[c, pl.ds(at, SUBS), :], south[c, pl.ds(at - 6, SUBS), :]))
                ref[index, c, rows(SOUTH), :] = tile[c]
                ref[index, c, rows(tiles + OWN), :] = tile[c]
            for c in range(2):
                insert(packs, quarter, l, q, c, tile[c])
    finish(packs, lane)
    for g in range(5):
        k_ref[g, rows(tiles), :] = packs[g]
    p_ref[rows(tiles), :], q_ref[rows(tiles), :] = outgoing(packs, lane, lon_even, top & (sub < 2))


def mirror_kernel(
    c_ref, b_ref, f_ref, r_in, u2_in, v2_in, w_in, k_in, r_ref, u2_ref, v2_ref, w_ref, k_ref, mirrored
):
    lane, sub = iota(1), iota(0)
    quarter = lane // 4
    _, top = lat_place()
    width = b_ref.shape[1]
    tiles = k_ref.shape[1] // SUBS - 1

    @pl.when(top)
    def _():
        source = partner_columns(c_ref, width)
        before = jnp.broadcast_to(source[0][:, :1] + 1, (SUBS, LANES))
        after = jnp.broadcast_to(jnp.maximum(source[1][:, LANES - 1 :] - 1, 0), (SUBS, LANES))

        @pl.loop(0, LEVELS, unroll=True)
        def _(l):
            for g in range(2):
                raw = [(b_ref if s < 2 else f_ref)[rows(2 * l + g), cols(s % 2)] for s in range(4)]
                for c, p in enumerate((*source, before, after)):
                    got = jnp.zeros((SUBS, LANES), jnp.float32)
                    for s in range(4):
                        picked = jnp.take_along_axis(raw[s], p % LANES, axis=1, mode="promise_in_bounds")
                        got = jnp.where(p // LANES == s, picked, got)
                    swapped = jnp.where(sub % 2 == 0, pltpu.roll(got, SUBS - 1, 0), pltpu.roll(got, 1, 0))
                    if g == 1:
                        swapped = jnp.where(sub == 2, -got, jnp.where(sub == 3, got, swapped))
                    mirrored[c, rows(2 * l + g), :] = swapped

        packs = [jnp.zeros((SUBS, LANES), jnp.float32)] * 5
        for l in range(LEVELS):
            for q in range(QN):
                ref = (u2_ref, v2_ref, w_ref)[q - FIELDS] if q >= FIELDS else r_ref
                index = LEVELS * q + l if q < FIELDS else l
                seg = LEVELS * (q % 2) + l if q < FIELDS else l
                pack = q // 2 if q < FIELDS else q - 2
                tile = [mirrored[c, pl.ds(16 * l + 2 * q, SUBS), :] for c in range(4)]
                for c in range(2):
                    insert(packs, quarter, l, q, c, tile[c])
                    north = tile[c]
                    if q == FIELDS:
                        north = -pltpu.roll(jnp.where(lane == 0, tile[1 - c], tile[c]), LANES - 1, 1)
                    ref[index, c, rows(tiles + OWN), :] = north
                packs[pack] = jnp.where(lane == 16 * seg + 3, tile[2], packs[pack])
                packs[pack] = jnp.where(lane == 16 * seg + 12, tile[3], packs[pack])
        finish(packs, lane)
        for g in range(5):
            k_ref[g, rows(tiles), :] = jnp.where(sub < 2, packs[g], k_in[g, rows(tiles), :])


def seam(r, r_mirror, h, h_mirror, w, sign):
    return w * r_mirror * (sign * (0.5 + h_mirror) - h)


def seam_mirror(r, r_top, h_top, h, w, sign):
    return w * (sign * (0.5 + h_top) * r_top - h * r - h_top * (r - r_top))


def step_kernel(r_ref, u2_ref, v2_ref, w_ref, o_ref, r1):
    lane, sub = iota(1), iota(0)
    _, top = lat_place()
    tiles = o_ref.shape[2] // SUBS
    end = OWN + tiles

    def update(l, t, load):
        u = [u2_ref[l, c, rows(t), :] for c in range(2)]
        u_west = [pltpu.roll(jnp.where(lane == LANES - 1, u[1 - c], u[c]), 1, 1) for c in range(2)]
        v = [v2_ref[l, c, rows(t), :] for c in range(2)]
        v_south = [v2_ref[l, c, rows(t, -1), :] for c in range(2)]
        w = [w_ref[l, c, rows(t), :] for c in range(2)]
        out = []
        for f in range(FIELDS):
            r = [load(f, c, rows(t)) for c in range(2)]
            for c in range(2):
                ahead = pltpu.roll(jnp.where(lane == 0, r[1 - c], r[c]), LANES - 1, 1)
                behind = pltpu.roll(jnp.where(lane == LANES - 1, r[1 - c], r[c]), 1, 1)
                along = u[c] * (ahead - r[c]) + u_west[c] * (r[c] - behind)
                up = v[c] * (load(f, c, rows(t, 1)) - r[c])
                down = v_south[c] * (r[c] - load(f, c, rows(t, -1)))
                out.append((f, c, w[c] * (r[c] + along + up + down)))
        return out

    @pl.loop(0, LEVELS)
    def _(l):
        def first(f, c, at):
            return r_ref[LEVELS * f + l, c, at, :]

        def second(f, c, at):
            return r1[f, c, at, :]

        @pl.loop(SOUTH, end + 1, unroll=UNROLL1)
        def _(t):
            for f, c, value in update(l, t, first):
                r1[f, c, rows(t), :] = value

        def at_top(f, c, load):
            v, v_mirror = v2_ref[l, c, rows(end - 1), :], v2_ref[l, c, rows(end - 1, 2), :]
            r, r_mirror = load(f, c, rows(end - 1)), load(f, c, rows(end - 1, 1))
            add = seam(r, r_mirror, v, v_mirror, w_ref[l, c, rows(end - 1), :], sign_of(f))
            return jnp.where(sub == SUBS - 1, add, 0.0)

        @pl.when(top)
        def _():
            for f in range(FIELDS):
                for c in range(2):
                    v_top, v_mirror = v2_ref[l, c, rows(end, -1), :], v2_ref[l, c, rows(end, 1), :]
                    r, r_top = first(f, c, rows(end)), first(f, c, rows(end, -1))
                    add = seam_mirror(r, r_top, v_top, v_mirror, w_ref[l, c, rows(end), :], sign_of(f))
                    r1[f, c, rows(end), :] += jnp.where(sub == 0, add, 0.0)
                    r1[f, c, rows(end - 1), :] += at_top(f, c, first)

        @pl.loop(OWN, end, unroll=UNROLL2)
        def _(t):
            for f, c, value in update(l, t, second):
                o_ref[f, l, rows(t - OWN), cols(c)] = value

        @pl.when(top)
        def _():
            for f in range(FIELDS):
                for c in range(2):
                    o_ref[f, l, rows(tiles - 1), cols(c)] += at_top(f, c, second)


def edge_kernel(c_ref, k_ref, q_ref, p_ref, i_ref, o_ref, z, z1, buf, sems):
    lane, sub = iota(1), iota(0)
    _, top = lat_place()
    lon_even = lax.axis_index("lon") % 2 == 0
    tiles = i_ref.shape[2] // SUBS
    end = OWN + tiles
    pair = lane // 2 % 8

    def join(t):
        p, q = p_ref[rows(t), :], q_ref[rows(t), :]
        from_west, from_east = jnp.where(lon_even, q, p), jnp.where(lon_even, p, q)
        out = []
        for g in range(5):
            back = (LANES - 2 * g) % LANES
            west, east = (pltpu.roll(x, back, 1) if back else x for x in (from_west, from_east))
            out.append(jnp.where(pair == 1, west, jnp.where(pair == 6, east, k_ref[g, rows(t), :])))
        return out

    @pl.loop(0, tiles, unroll=True)
    def _(t):
        for g, value in enumerate(join(t)):
            z[g, rows(t + OWN), :] = value

    at_seam = partner_columns(c_ref, i_ref.shape[3])[1][:, LANES - 1 :] == 0
    p, q = p_ref[rows(tiles), :], q_ref[rows(tiles), :]
    for g, value in enumerate(join(tiles)):
        z[g, rows(SOUTH), :] = value
        crossed = pltpu.roll(jnp.where(lon_even, p, q), (LANES - 2 * g) % LANES, 1) if g else jnp.where(lon_even, p, q)
        if g != 3:
            crossed = pltpu.roll(crossed, SUBS - 1, 0)
        kept = jnp.where((pair == 6) & at_seam, crossed, k_ref[g, rows(tiles), :])
        value = jnp.where(top & (sub < 2), kept, value)
        if g == 2:
            value = jnp.where(top & (sub == 0), -pltpu.roll(value, LANES - 1, 1), value)
        z[g, rows(end), :] = value

    def update(t, load, mirrored):
        u, v, v_south, w = z[2, rows(t), :], z[3, rows(t), :], z[3, rows(t, -1), :], z[4, rows(t), :]
        u_west = pltpu.roll(u, 1, 1)
        out = []
        for h in range(2):
            r, r_north, r_south = load(h, rows(t)), load(h, rows(t, 1)), load(h, rows(t, -1))
            along = u * (pltpu.roll(r, LANES - 1, 1) - r) + u_west * (r - pltpu.roll(r, 1, 1))
            value = w * (r + along + v * (r_north - r) + v_south * (r - r_south))
            add = seam(r, r_north, v, z[3, rows(t, 2), :], w, sign_of(2 * h))
            value += jnp.where(top & (t == end - 1) & (sub == SUBS - 1), add, 0.0)
            if mirrored:
                add = seam_mirror(r, r_south, v_south, z[3, rows(t, 1), :], w, sign_of(2 * h))
                value += jnp.where(top & (t == end) & (sub == 0), add, 0.0)
            out.append(value)
        return out

    @pl.loop(SOUTH, end + 1, unroll=True)
    def _(t):
        for h, value in enumerate(update(t, lambda h, at: z[h, at, :], True)):
            z1[h, rows(t), :] = value

    def send(t):
        at = rows(t)
        return pltpu.make_async_copy(buf.at[:, :, at, :], o_ref.at[:, :, at, :], sems.at[t])

    @pl.loop(0, tiles, unroll=UNROLL2)
    def _(t):
        value = update(t + OWN, lambda h, at: z1[h, at, :], False)
        value = [jnp.where(pair == 1, pltpu.roll(x, LANES - 8, 1), x) for x in value]
        for f in range(FIELDS):
            for l in range(LEVELS):
                seg = 16 * (LEVELS * (f % 2) + l)
                sides = pltpu.roll(value[f // 2], LANES - 4 - seg, 1)
                buf[f, l, rows(t), cols(0)] = jnp.where(lane < 2, sides, i_ref[f, l, rows(t), cols(0)])
                buf[f, l, rows(t), cols(1)] = jnp.where(lane >= LANES - 2, sides, i_ref[f, l, rows(t), cols(1)])
        send(t).start()

    @pl.loop(0, tiles)
    def _(t):
        send(t).wait()


def per_device(state_adjoint, east_velocity, north_velocity, ocean_mask, partner):
    nlon, nlat = lax.axis_size("lon"), lax.axis_size("lat")
    fields, levels, height, width = state_adjoint.shape
    axes = ("lon", "lat")
    f32 = jnp.float32

    def device(lon, lat):
        return lon % nlon * nlat + lat

    def both(a, b):
        return [(a, b), (b, a)]

    fold = [(device(nlon - 1 - i, nlat - 1), device(i, nlat - 1)) for i in range(nlon)]
    fold_next = [(device(nlon - i, nlat - 1), device(i, nlat - 1)) for i in range(nlon)]
    within = [e for i in range(nlon) for j in range(0, nlat, 2) for e in both(device(i, j), device(i, j + 1))]
    across = [e for i in range(nlon) for j in range(1, nlat - 1, 2) for e in both(device(i, j), device(i, j + 1))]
    even = [e for i in range(0, nlon, 2) for j in range(nlat) for e in both(device(i, j), device(i + 1, j))]
    odd = [e for i in range(1, nlon, 2) for j in range(nlat) for e in both(device(i, j), device(i + 1, j))]

    def held(x):
        return pltpu.with_memory_space_constraint(x, pltpu.VMEM)

    def call(kernel, name, args, outs, scratch=(), aliases=None, micros=1):
        return pl.pallas_call(
            kernel,
            out_shape=tuple(pltpu.VMEM(shape, f32) for shape in outs),
            in_specs=[VMEM] * len(args),
            out_specs=(VMEM,) * len(outs),
            scratch_shapes=[pltpu.VMEM(shape, f32) for shape in scratch],
            input_output_aliases=aliases or {},
            cost_estimate=pl.CostEstimate(flops=0, bytes_accessed=micros * 3_000_000, transcendentals=0),
            compiler_params=pltpu.CompilerParams(vmem_limit_bytes=SCOPED),
            name=name,
        )(*(held(x) for x in args))

    inputs = (state_adjoint, east_velocity, north_velocity, ocean_mask)
    message = (16 * levels, width)
    to_a, to_b = pl.pallas_call(
        row_kernel,
        out_shape=(pltpu.VMEM(message, f32), pltpu.VMEM(message, f32)),
        in_specs=[pl.BlockSpec(memory_space=pltpu.HBM)] * 4,
        out_specs=(VMEM,) * 2,
        scratch_shapes=[pltpu.VMEM((2,) + x.shape[:-2] + (SUBS, width), x.dtype) for x in inputs]
        + [pltpu.SemaphoreType.DMA((4, 2))],
        compiler_params=pltpu.CompilerParams(vmem_limit_bytes=SCOPED),
        name="pack_rows",
    )(*(pltpu.with_memory_space_constraint(x, pltpu.HBM) for x in inputs))
    from_a = lax.ppermute(to_a, axes, within)
    from_b = lax.ppermute(to_b, axes, across + fold)
    from_f = lax.ppermute(to_b, axes, fold_next)

    tall = height + 4 * SUBS
    ext = [(fields * levels, 2, tall, LANES)] + [(levels, 2, tall, LANES)] * 3
    pack = (height + SUBS, LANES)
    laid = call(prepare_kernel, "prepare", inputs, (*ext, (5,) + pack, pack, pack))
    *laid, to_p, to_q = call(
        halo_kernel,
        "place_rows",
        (from_a, from_b, *laid),
        (*ext, (5,) + pack, pack, pack),
        [(2, message[0] + 2 * SUBS, LANES)] * 2,
        aliases={2 + i: i for i in range(7)},
    )
    from_p = lax.ppermute(to_p, axes, even)
    from_q = lax.ppermute(to_q, axes, odd)

    pairs = partner.reshape(2, LANES)
    *laid, packs = call(
        mirror_kernel,
        "mirror_rows",
        (pairs, from_b, from_f, *laid),
        (*ext, (5,) + pack),
        [(4, message[0] + SUBS, LANES)],
        aliases={3 + i: i for i in range(5)},
    )
    (inner,) = call(step_kernel, "both_steps", laid, (state_adjoint.shape,), [(fields, 2, tall, LANES)], micros=3)
    return pl.pallas_call(
        edge_kernel,
        out_shape=jax.ShapeDtypeStruct(state_adjoint.shape, f32),
        in_specs=[VMEM] * 5,
        out_specs=pl.BlockSpec(memory_space=pl.ANY),
        scratch_shapes=[
            pltpu.VMEM((5, tall, LANES), f32),
            pltpu.VMEM((2, tall, LANES), f32),
            pltpu.VMEM(state_adjoint.shape, f32),
            pltpu.SemaphoreType.DMA((height // SUBS,)),
        ],
        compiler_params=pltpu.CompilerParams(vmem_limit_bytes=SCOPED),
        name="edge_columns",
    )(*(held(x) for x in (pairs, packs, from_q, from_p, inner)))


def solution(mesh):
    placed = (
        P(None, None, "lat", "lon"),
        P(None, "lat", "lon"),
        P(None, "lat", "lon"),
        P(None, "lat", "lon"),
        P("lon"),
    )
    return jax.shard_map(
        per_device,
        mesh=mesh,
        in_specs=placed,
        out_specs=P(None, None, "lat", "lon"),
        check_vma=False,
    )
```

```python
import jax
import jax.numpy as jnp
from jax import lax
from jax.experimental import pallas as pl
from jax.experimental.pallas import tpu as pltpu
from jax.sharding import PartitionSpec as P

FIELDS, LEVELS = 4, 4
QN = FIELDS + 3
LANES, SUBS = 128, 8
SOUTH, OWN = 1, 2
VMEM = pl.BlockSpec(memory_space=pltpu.VMEM)
SCOPED = 4 << 20
UNROLL1, UNROLL2 = 10, 8


def iota(dim):
    return lax.broadcasted_iota(jnp.int32, (SUBS, LANES), dim)


def rows(t, by=0):
    start = SUBS * t
    if not isinstance(start, int):
        start = pl.multiple_of(start, SUBS)
    return pl.ds(start + by, SUBS)


def cols(c):
    return pl.ds(LANES * c, LANES)


def lat_place():
    lat = lax.axis_index("lat")
    return lat % 2 == 0, lat == lax.axis_size("lat") - 1


def sign_of(field):
    return 1.0 if field < 2 else -1.0


def row_kernel(s_in, u_in, v_in, m_in, a_ref, b_ref, s_ref, u_ref, v_ref, m_ref, sems):
    lat_even, _ = lat_place()
    sub = iota(0)
    copies = []
    for i, (src, dst) in enumerate(((s_in, s_ref), (u_in, u_ref), (v_in, v_ref), (m_in, m_ref))):
        lead = (slice(None),) * (len(src.shape) - 2)
        for k, t in enumerate((0, src.shape[-2] // SUBS - 1)):
            copies.append(pltpu.make_async_copy(src.at[lead + (rows(t), slice(None))], dst.at[k], sems.at[i, k]))
    for copy in copies:
        copy.start()
    for copy in copies:
        copy.wait()

    def put(t, c, values, where):
        low = high = jnp.zeros((SUBS, LANES), jnp.float32)
        for (south, north), (first, count) in zip(values, where):
            here = (sub >= first) & (sub < first + count)
            low = jnp.where(here, pltpu.roll(south, first, 0) if first else south, low)
            high = jnp.where(here, pltpu.roll(north, (first + count) % SUBS, 0) if (first + count) % SUBS else north, high)
        a_ref[rows(t), cols(c)] = jnp.where(lat_even, high, low)
        b_ref[rows(t), cols(c)] = jnp.where(lat_even, low, high)

    for c in range(2):

        @pl.loop(0, LEVELS)
        def _(l):
            w = [m_ref[k, l, :, cols(c)].astype(jnp.float32) for k in range(2)]
            values = [[s_ref[k, f, l, :, cols(c)] * w[k] for k in range(2)] for f in range(FIELDS)]
            put(l, c, values, [(2 * f, 2) for f in range(FIELDS)])

        u, v, w = (
            [[ref[k, l, :, cols(c)].astype(jnp.float32) for k in range(2)] for l in range(LEVELS)]
            for ref in (u_ref, v_ref, m_ref)
        )
        put(LEVELS, c, [[0.5 * x for x in pair] for pair in v], [(2 * l, 2) for l in range(LEVELS)])
        values = [[0.5 * x for x in pair] for pair in u] + w
        put(LEVELS + 1, c, values, [(l, 1) for l in range(2 * LEVELS)])


def place_in_message(l, q):
    if q < FIELDS:
        return SUBS * l + 2 * q, 2
    if q == FIELDS + 1:
        return SUBS * LEVELS + 2 * l, 2
    return SUBS * (LEVELS + 1) + l + (LEVELS if q > FIELDS else 0), 1


def insert(packs, lane, l, q, tile):
    seg = LEVELS * (q % 2) + l if q < FIELDS else l
    g = q // 2 if q < FIELDS else q - 2
    sides = pltpu.roll(jnp.where(lane < LANES // 2, tile[0], tile[1]), (16 * seg + 8) % LANES, 1)
    packs[g] = jnp.where((lane + 4) // 8 == 2 * seg + 1, sides, packs[g])


def arrange(pack, lane):
    return jnp.where(lane // 4 % 4 == 1, pltpu.roll(pack, LANES - 4, 1), pltpu.roll(pack, 4, 1))


def finish(packs, lane):
    for g in range(2, 5):
        packs[g] = jnp.where(lane < LANES // 2, packs[g], pltpu.roll(packs[g], LANES // 2, 1))


def outgoing(packs, lane, lon_even, seam_rows=None):
    east = jnp.zeros((SUBS, LANES), jnp.float32)
    west = jnp.zeros((SUBS, LANES), jnp.float32)
    pair = lane // 2 % 8
    for g, tile in enumerate(packs):
        east = jnp.where(pair == 1 + g, pltpu.roll(tile, (LANES - 4 + 2 * g) % LANES, 1) if g != 2 else tile, east)
        first = pltpu.roll(tile, 4 + 2 * g, 1)
        if seam_rows is not None:
            first = jnp.where(seam_rows, pltpu.roll(tile, 5 + 2 * g, 1), first)
        west = jnp.where(pair == (6 + g) % 8, first, west)
    return jnp.where(lon_even, east, west), jnp.where(lon_even, west, east)


def prepare_kernel(s_ref, u_ref, v_ref, m_ref, r_ref, u2_ref, v2_ref, w_ref, k_ref, p_ref, q_ref):
    lane = iota(1)
    lon_even = lax.axis_index("lon") % 2 == 0

    @pl.loop(0, s_ref.shape[2] // SUBS, unroll=2)
    def _(t):
        src, dst = rows(t), rows(t + OWN)
        packs = [jnp.zeros((SUBS, LANES), jnp.float32)] * 5
        for l in range(LEVELS):
            w = [m_ref[l, src, cols(c)].astype(jnp.float32) for c in range(2)]
            for q in range(QN):
                if q < FIELDS:
                    ref, index, tile = r_ref, LEVELS * q + l, [s_ref[q, l, src, cols(c)] * w[c] for c in range(2)]
                elif q < FIELDS + 2:
                    ref, index, x_ref = (u2_ref, v2_ref)[q - FIELDS], l, (u_ref, v_ref)[q - FIELDS]
                    tile = [0.5 * x_ref[l, src, cols(c)] for c in range(2)]
                else:
                    ref, index, tile = w_ref, l, w
                for c in range(2):
                    ref[index, c, dst, :] = tile[c]
                insert(packs, lane, l, q, tile)
        finish(packs, lane)
        for g in range(5):
            k_ref[g, src, :] = arrange(packs[g], lane)
        p_ref[src, :], q_ref[src, :] = outgoing(packs, lane, lon_even)


def partner_columns(c_ref, width):
    ncol = lax.axis_size("lon") * width
    lon = lax.axis_index("lon")
    return [lax.rem(c_ref[pl.ds(c, SUBS, stride=0), :] + (lon + 1) * width, ncol) for c in range(2)]


def halo_kernel(
    a_ref, b_ref, r_in, u2_in, v2_in, w_in, k_in, p_in, q_in,
    r_ref, u2_ref, v2_ref, w_ref, k_ref, p_ref, q_ref, north, south,
):
    lane, sub = iota(1), iota(0)
    lat_even, top = lat_place()
    lon_even = lax.axis_index("lon") % 2 == 0
    tiles = k_ref.shape[1] // SUBS - 1

    @pl.loop(0, LEVELS + 2, unroll=True)
    def _(i):
        for c in range(2):
            a, b = a_ref[rows(i), cols(c)], b_ref[rows(i), cols(c)]
            north[c, rows(i + 1), :] = jnp.where(lat_even, a, b)
            south[c, rows(i + 1), :] = jnp.where(lat_even, b, a)

    packs = [jnp.zeros((SUBS, LANES), jnp.float32)] * 5
    for l in range(LEVELS):
        for q in range(QN):
            ref = (u2_ref, v2_ref, w_ref)[q - FIELDS] if q >= FIELDS else r_ref
            index = LEVELS * q + l if q < FIELDS else l
            first, count = place_in_message(l, q)
            at, at_south = pl.ds(SUBS + first, SUBS), pl.ds(first + count, SUBS)
            tile = []
            for c in range(2):
                tile.append(jnp.where(sub < 4, north[c, at, :], south[c, at_south, :]))
                ref[index, c, rows(SOUTH), :] = tile[c]
                ref[index, c, rows(tiles + OWN), :] = tile[c]
            insert(packs, lane, l, q, tile)
    finish(packs, lane)
    for g in range(5):
        k_ref[g, rows(tiles), :] = arrange(packs[g], lane)
    p_ref[rows(tiles), :], q_ref[rows(tiles), :] = outgoing(packs, lane, lon_even, top & (sub < 2))


def mirror_kernel(
    c_ref, b_ref, f_ref, r_in, u2_in, v2_in, w_in, k_in, r_ref, u2_ref, v2_ref, w_ref, k_ref, mirrored
):
    lane, sub = iota(1), iota(0)
    _, top = lat_place()
    width = b_ref.shape[1]
    tiles = k_ref.shape[1] // SUBS - 1

    @pl.when(top)
    def _():
        source = partner_columns(c_ref, width)
        before = jnp.broadcast_to(source[0][:, :1] + 1, (SUBS, LANES))
        after = jnp.broadcast_to(jnp.maximum(source[1][:, LANES - 1 :] - 1, 0), (SUBS, LANES))

        for t in range(LEVELS + 2):
            raw = [(b_ref if s < 2 else f_ref)[rows(t), cols(s % 2)] for s in range(4)]
            for c, p in enumerate((*source, before, after)):
                got = jnp.zeros((SUBS, LANES), jnp.float32)
                for s in range(4):
                    picked = jnp.take_along_axis(raw[s], p % LANES, axis=1, mode="promise_in_bounds")
                    got = jnp.where(p // LANES == s, picked, got)
                if t < LEVELS:
                    got = jnp.where(sub % 2 == 0, pltpu.roll(got, SUBS - 1, 0), pltpu.roll(got, 1, 0))
                elif t == LEVELS:
                    got = jnp.where(sub % 2 == 0, -got, got)
                mirrored[c, rows(t), :] = got

        packs, halo = ([jnp.zeros((SUBS, LANES), jnp.float32)] * 5 for _ in range(2))
        for l in range(LEVELS):
            for q in range(QN):
                ref = (u2_ref, v2_ref, w_ref)[q - FIELDS] if q >= FIELDS else r_ref
                index = LEVELS * q + l if q < FIELDS else l
                seg = LEVELS * (q % 2) + l if q < FIELDS else l
                pack = q // 2 if q < FIELDS else q - 2
                tile = [mirrored[c, pl.ds(place_in_message(l, q)[0], SUBS), :] for c in range(4)]
                insert(packs, lane, l, q, tile)
                for c in range(2):
                    north = tile[c]
                    if q == FIELDS:
                        north = -pltpu.roll(jnp.where(lane == 0, tile[1 - c], tile[c]), LANES - 1, 1)
                    ref[index, c, rows(tiles + OWN), :] = north
                halo[pack] = jnp.where(lane == 16 * seg + 3, tile[2], halo[pack])
                halo[pack] = jnp.where(lane == 16 * seg + 12, tile[3], halo[pack])
        finish(packs, lane)
        finish(halo, lane)
        for g in range(5):
            value = jnp.where((lane % 16 == 3) | (lane % 16 == 12), halo[g], arrange(packs[g], lane))
            k_ref[g, rows(tiles), :] = jnp.where(sub < 2, value, k_in[g, rows(tiles), :])


def seam(r, r_mirror, h, h_mirror, w, sign):
    return w * r_mirror * (sign * (0.5 + h_mirror) - h)


def seam_mirror(r, r_top, h_top, h, w, sign):
    return w * (sign * (0.5 + h_top) * r_top - h * r - h_top * (r - r_top))


def step_kernel(r_ref, u2_ref, v2_ref, w_ref, o_ref, r1):
    lane, sub = iota(1), iota(0)
    _, top = lat_place()
    tiles = o_ref.shape[2] // SUBS
    end = OWN + tiles

    def update(l, t, load):
        u = [u2_ref[l, c, rows(t), :] for c in range(2)]
        u_west = [pltpu.roll(jnp.where(lane == LANES - 1, u[1 - c], u[c]), 1, 1) for c in range(2)]
        v = [v2_ref[l, c, rows(t), :] for c in range(2)]
        v_south = [v2_ref[l, c, rows(t, -1), :] for c in range(2)]
        w = [w_ref[l, c, rows(t), :] for c in range(2)]
        out = []
        for f in range(FIELDS):
            r = [load(f, c, rows(t)) for c in range(2)]
            for c in range(2):
                ahead = pltpu.roll(jnp.where(lane == 0, r[1 - c], r[c]), LANES - 1, 1)
                behind = pltpu.roll(jnp.where(lane == LANES - 1, r[1 - c], r[c]), 1, 1)
                along = u[c] * (ahead - r[c]) + u_west[c] * (r[c] - behind)
                up = v[c] * (load(f, c, rows(t, 1)) - r[c])
                down = v_south[c] * (r[c] - load(f, c, rows(t, -1)))
                out.append((f, c, w[c] * (r[c] + along + up + down)))
        return out

    @pl.loop(0, LEVELS)
    def _(l):
        def first(f, c, at):
            return r_ref[LEVELS * f + l, c, at, :]

        def second(f, c, at):
            return r1[f, c, at, :]

        @pl.loop(SOUTH, end + 1, unroll=UNROLL1)
        def _(t):
            for f, c, value in update(l, t, first):
                r1[f, c, rows(t), :] = value

        def at_top(f, c, load):
            v, v_mirror = v2_ref[l, c, rows(end - 1), :], v2_ref[l, c, rows(end - 1, 2), :]
            r, r_mirror = load(f, c, rows(end - 1)), load(f, c, rows(end - 1, 1))
            add = seam(r, r_mirror, v, v_mirror, w_ref[l, c, rows(end - 1), :], sign_of(f))
            return jnp.where(sub == SUBS - 1, add, 0.0)

        @pl.when(top)
        def _():
            for f in range(FIELDS):
                for c in range(2):
                    v_top, v_mirror = v2_ref[l, c, rows(end, -1), :], v2_ref[l, c, rows(end, 1), :]
                    r, r_top = first(f, c, rows(end)), first(f, c, rows(end, -1))
                    add = seam_mirror(r, r_top, v_top, v_mirror, w_ref[l, c, rows(end), :], sign_of(f))
                    r1[f, c, rows(end), :] += jnp.where(sub == 0, add, 0.0)
                    r1[f, c, rows(end - 1), :] += at_top(f, c, first)

        @pl.loop(OWN, end, unroll=UNROLL2)
        def _(t):
            for f, c, value in update(l, t, second):
                o_ref[f, l, rows(t - OWN), cols(c)] = value

        @pl.when(top)
        def _():
            for f in range(FIELDS):
                for c in range(2):
                    o_ref[f, l, rows(tiles - 1), cols(c)] += at_top(f, c, second)


def edge_kernel(c_ref, k_ref, q_ref, p_ref, i_ref, o_ref, z, z1, buf, sems):
    lane, sub = iota(1), iota(0)
    _, top = lat_place()
    lon_even = lax.axis_index("lon") % 2 == 0
    tiles = i_ref.shape[2] // SUBS
    end = OWN + tiles
    pair = lane // 2 % 8

    def join(t):
        p, q = p_ref[rows(t), :], q_ref[rows(t), :]
        from_west, from_east = jnp.where(lon_even, q, p), jnp.where(lon_even, p, q)
        out = []
        for g in range(5):
            back = (LANES - 2 * g) % LANES
            west, east = (pltpu.roll(x, back, 1) if back else x for x in (from_west, from_east))
            out.append(jnp.where(pair == 1, west, jnp.where(pair == 6, east, k_ref[g, rows(t), :])))
        return out

    @pl.loop(0, tiles, unroll=True)
    def _(t):
        for g, value in enumerate(join(t)):
            z[g, rows(t + OWN), :] = value

    at_seam = partner_columns(c_ref, i_ref.shape[3])[1][:, LANES - 1 :] == 0
    p, q = p_ref[rows(tiles), :], q_ref[rows(tiles), :]
    for g, value in enumerate(join(tiles)):
        z[g, rows(SOUTH), :] = value
        crossed = pltpu.roll(jnp.where(lon_even, p, q), (LANES - 2 * g) % LANES, 1) if g else jnp.where(lon_even, p, q)
        if g < 2:
            crossed = pltpu.roll(crossed, SUBS - 1, 0)
        kept = jnp.where((pair == 6) & at_seam, crossed, k_ref[g, rows(tiles), :])
        value = jnp.where(top & (sub < 2), kept, value)
        if g == 2:
            value = jnp.where(top & (sub == 0), -pltpu.roll(value, LANES - 1, 1), value)
        z[g, rows(end), :] = value

    def update(t, load, mirrored):
        u, v, v_south, w = z[2, rows(t), :], z[3, rows(t), :], z[3, rows(t, -1), :], z[4, rows(t), :]
        u_west = pltpu.roll(u, 1, 1)
        out = []
        for h in range(2):
            r, r_north, r_south = load(h, rows(t)), load(h, rows(t, 1)), load(h, rows(t, -1))
            along = u * (pltpu.roll(r, LANES - 1, 1) - r) + u_west * (r - pltpu.roll(r, 1, 1))
            value = w * (r + along + v * (r_north - r) + v_south * (r - r_south))
            add = seam(r, r_north, v, z[3, rows(t, 2), :], w, sign_of(2 * h))
            value += jnp.where(top & (t == end - 1) & (sub == SUBS - 1), add, 0.0)
            if mirrored:
                add = seam_mirror(r, r_south, v_south, z[3, rows(t, 1), :], w, sign_of(2 * h))
                value += jnp.where(top & (t == end) & (sub == 0), add, 0.0)
            out.append(value)
        return out

    @pl.loop(SOUTH, end + 1, unroll=True)
    def _(t):
        for h, value in enumerate(update(t, lambda h, at: z[h, at, :], True)):
            z1[h, rows(t), :] = value

    def send(t):
        at = rows(t)
        return pltpu.make_async_copy(buf.at[:, :, at, :], o_ref.at[:, :, at, :], sems.at[t])

    @pl.loop(0, tiles, unroll=UNROLL2)
    def _(t):
        value = update(t + OWN, lambda h, at: z1[h, at, :], False)
        value = [jnp.where(pair == 1, pltpu.roll(x, LANES - 8, 1), x) for x in value]
        for f in range(FIELDS):
            for l in range(LEVELS):
                seg = 16 * (LEVELS * (f % 2) + l)
                sides = pltpu.roll(value[f // 2], LANES - 4 - seg, 1)
                buf[f, l, rows(t), cols(0)] = jnp.where(lane < 2, sides, i_ref[f, l, rows(t), cols(0)])
                buf[f, l, rows(t), cols(1)] = jnp.where(lane >= LANES - 2, sides, i_ref[f, l, rows(t), cols(1)])
        send(t).start()

    @pl.loop(0, tiles)
    def _(t):
        send(t).wait()


def per_device(state_adjoint, east_velocity, north_velocity, ocean_mask, partner):
    nlon, nlat = lax.axis_size("lon"), lax.axis_size("lat")
    fields, levels, height, width = state_adjoint.shape
    axes = ("lon", "lat")
    f32 = jnp.float32

    def device(lon, lat):
        return lon % nlon * nlat + lat

    def both(a, b):
        return [(a, b), (b, a)]

    fold = [(device(nlon - 1 - i, nlat - 1), device(i, nlat - 1)) for i in range(nlon)]
    fold_next = [(device(nlon - i, nlat - 1), device(i, nlat - 1)) for i in range(nlon)]
    within = [e for i in range(nlon) for j in range(0, nlat, 2) for e in both(device(i, j), device(i, j + 1))]
    across = [e for i in range(nlon) for j in range(1, nlat - 1, 2) for e in both(device(i, j), device(i, j + 1))]
    even = [e for i in range(0, nlon, 2) for j in range(nlat) for e in both(device(i, j), device(i + 1, j))]
    odd = [e for i in range(1, nlon, 2) for j in range(nlat) for e in both(device(i, j), device(i + 1, j))]

    def held(x):
        return pltpu.with_memory_space_constraint(x, pltpu.VMEM)

    def call(kernel, name, args, outs, scratch=(), aliases=None, micros=1):
        return pl.pallas_call(
            kernel,
            out_shape=tuple(pltpu.VMEM(shape, f32) for shape in outs),
            in_specs=[VMEM] * len(args),
            out_specs=(VMEM,) * len(outs),
            scratch_shapes=[pltpu.VMEM(shape, f32) for shape in scratch],
            input_output_aliases=aliases or {},
            cost_estimate=pl.CostEstimate(flops=0, bytes_accessed=micros * 3_000_000, transcendentals=0),
            compiler_params=pltpu.CompilerParams(vmem_limit_bytes=SCOPED),
            name=name,
        )(*(held(x) for x in args))

    inputs = (state_adjoint, east_velocity, north_velocity, ocean_mask)
    message = (SUBS * (levels + 2), width)
    to_a, to_b = pl.pallas_call(
        row_kernel,
        out_shape=(pltpu.VMEM(message, f32), pltpu.VMEM(message, f32)),
        in_specs=[pl.BlockSpec(memory_space=pltpu.HBM)] * 4,
        out_specs=(VMEM,) * 2,
        scratch_shapes=[pltpu.VMEM((2,) + x.shape[:-2] + (SUBS, width), x.dtype) for x in inputs]
        + [pltpu.SemaphoreType.DMA((4, 2))],
        compiler_params=pltpu.CompilerParams(vmem_limit_bytes=SCOPED),
        name="pack_rows",
    )(*(pltpu.with_memory_space_constraint(x, pltpu.HBM) for x in inputs))
    from_a = lax.ppermute(to_a, axes, within)
    from_b = lax.ppermute(to_b, axes, across + fold)
    from_f = lax.ppermute(to_b, axes, fold_next)

    tall = height + 4 * SUBS
    ext = [(fields * levels, 2, tall, LANES)] + [(levels, 2, tall, LANES)] * 3
    pack = (height + SUBS, LANES)
    laid = call(prepare_kernel, "prepare", inputs, (*ext, (5,) + pack, pack, pack))
    *laid, to_p, to_q = call(
        halo_kernel,
        "place_rows",
        (from_a, from_b, *laid),
        (*ext, (5,) + pack, pack, pack),
        [(2, message[0] + 2 * SUBS, LANES)] * 2,
        aliases={2 + i: i for i in range(7)},
    )
    from_p = lax.ppermute(to_p, axes, even)
    from_q = lax.ppermute(to_q, axes, odd)

    pairs = partner.reshape(2, LANES)
    *laid, packs = call(
        mirror_kernel,
        "mirror_rows",
        (pairs, from_b, from_f, *laid),
        (*ext, (5,) + pack),
        [(4, message[0] + SUBS, LANES)],
        aliases={3 + i: i for i in range(5)},
    )
    (inner,) = call(step_kernel, "both_steps", laid, (state_adjoint.shape,), [(fields, 2, tall, LANES)], micros=3)
    return pl.pallas_call(
        edge_kernel,
        out_shape=jax.ShapeDtypeStruct(state_adjoint.shape, f32),
        in_specs=[VMEM] * 5,
        out_specs=pl.BlockSpec(memory_space=pl.ANY),
        scratch_shapes=[
            pltpu.VMEM((5, tall, LANES), f32),
            pltpu.VMEM((2, tall, LANES), f32),
            pltpu.VMEM(state_adjoint.shape, f32),
            pltpu.SemaphoreType.DMA((height // SUBS,)),
        ],
        compiler_params=pltpu.CompilerParams(vmem_limit_bytes=SCOPED),
        name="edge_columns",
    )(*(held(x) for x in (pairs, packs, from_q, from_p, inner)))


def solution(mesh):
    placed = (
        P(None, None, "lat", "lon"),
        P(None, "lat", "lon"),
        P(None, "lat", "lon"),
        P(None, "lat", "lon"),
        P("lon"),
    )
    return jax.shard_map(
        per_device,
        mesh=mesh,
        in_specs=placed,
        out_specs=P(None, None, "lat", "lon"),
        check_vma=False,
    )
```

```python
import jax
import jax.numpy as jnp
from jax import lax
from jax.experimental import pallas as pl
from jax.experimental.pallas import tpu as pltpu
from jax.sharding import PartitionSpec as P

FIELDS, LEVELS = 4, 4
QN = FIELDS + 3
LANES, SUBS = 128, 8
SOUTH, OWN = 1, 2
VMEM = pl.BlockSpec(memory_space=pltpu.VMEM)
SCOPED = 4 << 20
UNROLL = 8


def iota(dim):
    return lax.broadcasted_iota(jnp.int32, (SUBS, LANES), dim)


def rows(t, by=0):
    start = SUBS * t
    if not isinstance(start, int):
        start = pl.multiple_of(start, SUBS)
    return pl.ds(start + by, SUBS)


def cols(c):
    return pl.ds(LANES * c, LANES)


def lat_place():
    lat = lax.axis_index("lat")
    return lat % 2 == 0, lat == lax.axis_size("lat") - 1


def sign_of(field):
    return 1.0 if field < 2 else -1.0


def row_kernel(s_in, u_in, v_in, m_in, a_ref, b_ref, s_ref, u_ref, v_ref, m_ref, sems):
    lat_even, _ = lat_place()
    sub = iota(0)
    copies = []
    for i, (src, dst) in enumerate(((s_in, s_ref), (u_in, u_ref), (v_in, v_ref), (m_in, m_ref))):
        lead = (slice(None),) * (len(src.shape) - 2)
        for k, t in enumerate((0, src.shape[-2] // SUBS - 1)):
            copies.append(pltpu.make_async_copy(src.at[lead + (rows(t), slice(None))], dst.at[k], sems.at[i, k]))
    for copy in copies:
        copy.start()
    for copy in copies:
        copy.wait()

    def put(t, c, values, where):
        low = high = jnp.zeros((SUBS, LANES), jnp.float32)
        for (south, north), (first, count) in zip(values, where):
            here = (sub >= first) & (sub < first + count)
            low = jnp.where(here, pltpu.roll(south, first, 0) if first else south, low)
            high = jnp.where(here, pltpu.roll(north, (first + count) % SUBS, 0) if (first + count) % SUBS else north, high)
        a_ref[rows(t), cols(c)] = jnp.where(lat_even, high, low)
        b_ref[rows(t), cols(c)] = jnp.where(lat_even, low, high)

    for c in range(2):

        @pl.loop(0, LEVELS)
        def _(l):
            w = [m_ref[k, l, :, cols(c)].astype(jnp.float32) for k in range(2)]
            values = [[s_ref[k, f, l, :, cols(c)] * w[k] for k in range(2)] for f in range(FIELDS)]
            put(l, c, values, [(2 * f, 2) for f in range(FIELDS)])

        u, v, w = (
            [[ref[k, l, :, cols(c)].astype(jnp.float32) for k in range(2)] for l in range(LEVELS)]
            for ref in (u_ref, v_ref, m_ref)
        )
        put(LEVELS, c, [[0.5 * x for x in pair] for pair in v], [(2 * l, 2) for l in range(LEVELS)])
        values = [[0.5 * x for x in pair] for pair in u] + w
        put(LEVELS + 1, c, values, [(l, 1) for l in range(2 * LEVELS)])


def place_in_message(l, q):
    if q < FIELDS:
        return SUBS * l + 2 * q, 2
    if q == FIELDS + 1:
        return SUBS * LEVELS + 2 * l, 2
    return SUBS * (LEVELS + 1) + l + (LEVELS if q > FIELDS else 0), 1


def insert(packs, lane, l, q, tile):
    seg = LEVELS * (q % 2) + l if q < FIELDS else l
    g = q // 2 if q < FIELDS else q - 2
    sides = pltpu.roll(jnp.where(lane < LANES // 2, tile[0], tile[1]), (16 * seg + 8) % LANES, 1)
    packs[g] = jnp.where((lane + 4) // 8 == 2 * seg + 1, sides, packs[g])


def arrange(pack, lane):
    return jnp.where(lane // 4 % 4 == 1, pltpu.roll(pack, LANES - 4, 1), pltpu.roll(pack, 4, 1))


def finish(packs, lane):
    for g in range(2, 5):
        packs[g] = jnp.where(lane < LANES // 2, packs[g], pltpu.roll(packs[g], LANES // 2, 1))


def turn(tile, by):
    by %= LANES
    return pltpu.roll(tile, by, 1) if by else tile


def slots(lane):
    slot = lane % 8
    return [(slot // 2 == g, 2 * g) for g in range(3)] + [(slot == 6, 6), (slot == 7, 7)]


def outgoing(packs, lane, lon_even, half, seam_rows=None):
    east = west = jnp.zeros((SUBS, LANES), jnp.float32)
    for g, (here, first) in enumerate(slots(lane)):
        to = first + 8 * half
        west_part = turn(packs[g], to - 8)
        if seam_rows is not None:
            west_part = jnp.where(seam_rows, turn(packs[g], to - 7), west_part)
        west = jnp.where(here, west_part, west)
        east = jnp.where(here, turn(packs[g], to - (6 if g < 3 else 7)), east)
    return jnp.where(lon_even, east, west), jnp.where(lon_even, west, east)


def prepare_kernel(s_ref, u_ref, v_ref, m_ref, r_ref, u2_ref, v2_ref, w_ref, k_ref, p_ref, q_ref):
    lane = iota(1)
    lon_even = lax.axis_index("lon") % 2 == 0

    @pl.loop(0, s_ref.shape[2] // SUBS // 2)
    def _(pair):
        sent = []
        for half in range(2):
            src, dst = rows(2 * pair + half), rows(2 * pair + half + OWN)
            packs = [jnp.zeros((SUBS, LANES), jnp.float32)] * 5
            for l in range(LEVELS):
                w = [m_ref[l, src, cols(c)].astype(jnp.float32) for c in range(2)]
                for q in range(QN):
                    if q < FIELDS:
                        ref, index, tile = r_ref, LEVELS * q + l, [s_ref[q, l, src, cols(c)] * w[c] for c in range(2)]
                    elif q < FIELDS + 2:
                        ref, index, x_ref = (u2_ref, v2_ref)[q - FIELDS], l, (u_ref, v_ref)[q - FIELDS]
                        tile = [0.5 * x_ref[l, src, cols(c)] for c in range(2)]
                    else:
                        ref, index, tile = w_ref, l, w
                    for c in range(2):
                        ref[index, c, dst, :] = tile[c]
                    insert(packs, lane, l, q, tile)
            finish(packs, lane)
            for g in range(5):
                k_ref[g, src, :] = arrange(packs[g], lane)
            sent.append(outgoing(packs, lane, lon_even, half))
        for ref, low, high in zip((p_ref, q_ref), *sent):
            ref[rows(pair), :] = jnp.where(lane % 16 < 8, low, high)


def partner_columns(c_ref, width):
    ncol = lax.axis_size("lon") * width
    lon = lax.axis_index("lon")
    return [lax.rem(c_ref[pl.ds(c, SUBS, stride=0), :] + (lon + 1) * width, ncol) for c in range(2)]


def halo_kernel(
    a_ref, b_ref, r_in, u2_in, v2_in, w_in, k_in, p_in, q_in,
    r_ref, u2_ref, v2_ref, w_ref, k_ref, p_ref, q_ref, north, south,
):
    lane, sub = iota(1), iota(0)
    lat_even, top = lat_place()
    lon_even = lax.axis_index("lon") % 2 == 0
    tiles = k_ref.shape[1] // SUBS - 1

    @pl.loop(0, LEVELS + 2, unroll=True)
    def _(i):
        for c in range(2):
            a, b = a_ref[rows(i), cols(c)], b_ref[rows(i), cols(c)]
            north[c, rows(i + 1), :] = jnp.where(lat_even, a, b)
            south[c, rows(i + 1), :] = jnp.where(lat_even, b, a)

    packs = [jnp.zeros((SUBS, LANES), jnp.float32)] * 5
    for l in range(LEVELS):
        for q in range(QN):
            ref = (u2_ref, v2_ref, w_ref)[q - FIELDS] if q >= FIELDS else r_ref
            index = LEVELS * q + l if q < FIELDS else l
            first, count = place_in_message(l, q)
            at, at_south = pl.ds(SUBS + first, SUBS), pl.ds(first + count, SUBS)
            tile = []
            for c in range(2):
                tile.append(jnp.where(sub < 4, north[c, at, :], south[c, at_south, :]))
                ref[index, c, rows(SOUTH), :] = tile[c]
                ref[index, c, rows(tiles + OWN), :] = tile[c]
            insert(packs, lane, l, q, tile)
    finish(packs, lane)
    for g in range(5):
        k_ref[g, rows(tiles), :] = arrange(packs[g], lane)
    to = rows(tiles // 2)
    p_ref[to, :], q_ref[to, :] = outgoing(packs, lane, lon_even, 0, top & (sub < 2))


def mirror_kernel(
    c_ref, b_ref, f_ref, r_in, u2_in, v2_in, w_in, k_in, r_ref, u2_ref, v2_ref, w_ref, k_ref, mirrored
):
    lane, sub = iota(1), iota(0)
    _, top = lat_place()
    width = b_ref.shape[1]
    tiles = k_ref.shape[1] // SUBS - 1

    @pl.when(top)
    def _():
        source = partner_columns(c_ref, width)
        before = jnp.broadcast_to(source[0][:, :1] + 1, (SUBS, LANES))
        after = jnp.broadcast_to(jnp.maximum(source[1][:, LANES - 1 :] - 1, 0), (SUBS, LANES))

        for t in range(LEVELS + 2):
            raw = [(b_ref if s < 2 else f_ref)[rows(t), cols(s % 2)] for s in range(4)]
            for c, p in enumerate((*source, before, after)):
                got = jnp.zeros((SUBS, LANES), jnp.float32)
                for s in range(4):
                    picked = jnp.take_along_axis(raw[s], p % LANES, axis=1, mode="promise_in_bounds")
                    got = jnp.where(p // LANES == s, picked, got)
                if t < LEVELS:
                    got = jnp.where(sub % 2 == 0, pltpu.roll(got, SUBS - 1, 0), pltpu.roll(got, 1, 0))
                elif t == LEVELS:
                    got = jnp.where(sub % 2 == 0, -got, got)
                mirrored[c, rows(t), :] = got

        packs, halo = ([jnp.zeros((SUBS, LANES), jnp.float32)] * 5 for _ in range(2))
        for l in range(LEVELS):
            for q in range(QN):
                ref = (u2_ref, v2_ref, w_ref)[q - FIELDS] if q >= FIELDS else r_ref
                index = LEVELS * q + l if q < FIELDS else l
                seg = LEVELS * (q % 2) + l if q < FIELDS else l
                pack = q // 2 if q < FIELDS else q - 2
                tile = [mirrored[c, pl.ds(place_in_message(l, q)[0], SUBS), :] for c in range(4)]
                insert(packs, lane, l, q, tile)
                for c in range(2):
                    north = tile[c]
                    if q == FIELDS:
                        north = -pltpu.roll(jnp.where(lane == 0, tile[1 - c], tile[c]), LANES - 1, 1)
                    ref[index, c, rows(tiles + OWN), :] = north
                halo[pack] = jnp.where(lane == 16 * seg + 3, tile[2], halo[pack])
                halo[pack] = jnp.where(lane == 16 * seg + 12, tile[3], halo[pack])
        finish(packs, lane)
        finish(halo, lane)
        for g in range(5):
            value = jnp.where((lane % 16 == 3) | (lane % 16 == 12), halo[g], arrange(packs[g], lane))
            k_ref[g, rows(tiles), :] = jnp.where(sub < 2, value, k_in[g, rows(tiles), :])


def seam(r, r_mirror, h, h_mirror, w, sign):
    return w * r_mirror * (sign * (0.5 + h_mirror) - h)


def seam_mirror(r, r_top, h_top, h, w, sign):
    return w * (sign * (0.5 + h_top) * r_top - h * r - h_top * (r - r_top))


def step_kernel(r_ref, u2_ref, v2_ref, w_ref, o_ref, r1, uw):
    lane, sub = iota(1), iota(0)
    _, top = lat_place()
    tiles = o_ref.shape[2] // SUBS
    end = OWN + tiles

    def update(l, look, load, first):
        def of(ref, c):
            return lambda at: ref[l, c, at, :]

        u = [look(of(u2_ref, c), 0) for c in range(2)]
        if first:
            u_west = [pltpu.roll(jnp.where(lane == LANES - 1, u[1 - c], u[c]), 1, 1) for c in range(2)]
        else:
            u_west = [look(lambda at, c=c: uw[c, at, :], 0) for c in range(2)]
        v = [look(of(v2_ref, c), 0) for c in range(2)]
        v_south = [look(of(v2_ref, c), -1) for c in range(2)]
        w = [look(of(w_ref, c), 0) for c in range(2)]
        out = []
        for f in range(FIELDS):
            reads = [lambda at, c=c: load(f, c, at) for c in range(2)]
            r = [look(read, 0) for read in reads]
            for c in range(2):
                ahead = pltpu.roll(jnp.where(lane == 0, r[1 - c], r[c]), LANES - 1, 1)
                behind = pltpu.roll(jnp.where(lane == LANES - 1, r[1 - c], r[c]), 1, 1)
                along = u[c] * (ahead - r[c]) + u_west[c] * (r[c] - behind)
                up = v[c] * (look(reads[c], 1) - r[c])
                down = v_south[c] * (r[c] - look(reads[c], -1))
                out.append((f, c, w[c] * (r[c] + along + up + down)))
        return out, u_west

    def tile(t):
        return lambda read, by: read(rows(t, by))

    def outside(read, by):
        return jnp.where(sub < SUBS // 2, read(rows(end, by)), read(rows(SOUTH, by)))

    @pl.loop(0, LEVELS)
    def _(l):
        def first(f, c, at):
            return r_ref[LEVELS * f + l, c, at, :]

        def second(f, c, at):
            return r1[f, c, at, :]

        for f, c, value in update(l, outside, first, True)[0]:
            r1[f, c, rows(SOUTH), :] = value
            r1[f, c, rows(end), :] = value

        @pl.loop(OWN, end, unroll=UNROLL)
        def _(t):
            values, u_west = update(l, tile(t), first, True)
            for c in range(2):
                uw[c, rows(t), :] = u_west[c]
            for f, c, value in values:
                r1[f, c, rows(t), :] = value

        def at_top(f, c, load):
            v, v_mirror = v2_ref[l, c, rows(end - 1), :], v2_ref[l, c, rows(end - 1, 2), :]
            r, r_mirror = load(f, c, rows(end - 1)), load(f, c, rows(end - 1, 1))
            add = seam(r, r_mirror, v, v_mirror, w_ref[l, c, rows(end - 1), :], sign_of(f))
            return jnp.where(sub == SUBS - 1, add, 0.0)

        @pl.when(top)
        def _():
            for f in range(FIELDS):
                for c in range(2):
                    v_top, v_mirror = v2_ref[l, c, rows(end, -1), :], v2_ref[l, c, rows(end, 1), :]
                    r, r_top = first(f, c, rows(end)), first(f, c, rows(end, -1))
                    add = seam_mirror(r, r_top, v_top, v_mirror, w_ref[l, c, rows(end), :], sign_of(f))
                    r1[f, c, rows(end), :] += jnp.where(sub == 0, add, 0.0)
                    r1[f, c, rows(end - 1), :] += at_top(f, c, first)

        @pl.loop(OWN, end, unroll=UNROLL)
        def _(t):
            for f, c, value in update(l, tile(t), second, False)[0]:
                o_ref[f, l, rows(t - OWN), cols(c)] = value

        @pl.when(top)
        def _():
            for f in range(FIELDS):
                for c in range(2):
                    o_ref[f, l, rows(tiles - 1), cols(c)] += at_top(f, c, second)


def edge_kernel(c_ref, k_ref, q_ref, p_ref, i_ref, o_ref, z, z1, buf, sems):
    lane, sub = iota(1), iota(0)
    _, top = lat_place()
    lon_even = lax.axis_index("lon") % 2 == 0
    tiles = i_ref.shape[2] // SUBS
    end = OWN + tiles
    pair = lane // 2 % 8

    def join(t):
        p, q = p_ref[rows(t // 2), :], q_ref[rows(t // 2), :]
        from_west, from_east = jnp.where(lon_even, q, p), jnp.where(lon_even, p, q)
        out = []
        for g, (_, first) in enumerate(slots(lane)):
            at = first + 8 * (t % 2)
            west, east = turn(from_west, (2 if g < 3 else 3) - at), turn(from_east, 12 - at)
            out.append((jnp.where(pair == 1, west, jnp.where(pair == 6, east, k_ref[g, rows(t), :])), east))
        return out

    for t in range(tiles):
        for g, (value, _) in enumerate(join(t)):
            z[g, rows(t + OWN), :] = value

    at_seam = partner_columns(c_ref, i_ref.shape[3])[1][:, LANES - 1 :] == 0
    for g, (value, crossed) in enumerate(join(tiles)):
        z[g, rows(SOUTH), :] = value
        if g < 2:
            crossed = pltpu.roll(crossed, SUBS - 1, 0)
        kept = jnp.where((pair == 6) & at_seam, crossed, k_ref[g, rows(tiles), :])
        value = jnp.where(top & (sub < 2), kept, value)
        if g == 2:
            value = jnp.where(top & (sub == 0), -pltpu.roll(value, LANES - 1, 1), value)
        z[g, rows(end), :] = value

    def update(t, load, mirrored):
        u, v, v_south, w = z[2, rows(t), :], z[3, rows(t), :], z[3, rows(t, -1), :], z[4, rows(t), :]
        u_west = pltpu.roll(u, 1, 1)
        out = []
        for h in range(2):
            r, r_north, r_south = load(h, rows(t)), load(h, rows(t, 1)), load(h, rows(t, -1))
            along = u * (pltpu.roll(r, LANES - 1, 1) - r) + u_west * (r - pltpu.roll(r, 1, 1))
            value = w * (r + along + v * (r_north - r) + v_south * (r - r_south))
            add = seam(r, r_north, v, z[3, rows(t, 2), :], w, sign_of(2 * h))
            value += jnp.where(top & (t == end - 1) & (sub == SUBS - 1), add, 0.0)
            if mirrored:
                add = seam_mirror(r, r_south, v_south, z[3, rows(t, 1), :], w, sign_of(2 * h))
                value += jnp.where(top & (t == end) & (sub == 0), add, 0.0)
            out.append(value)
        return out

    @pl.loop(SOUTH, end + 1, unroll=True)
    def _(t):
        for h, value in enumerate(update(t, lambda h, at: z[h, at, :], True)):
            z1[h, rows(t), :] = value

    def send(t):
        at = rows(t)
        return pltpu.make_async_copy(buf.at[:, :, at, :], o_ref.at[:, :, at, :], sems.at[t])

    @pl.loop(0, tiles, unroll=UNROLL)
    def _(t):
        value = update(t + OWN, lambda h, at: z1[h, at, :], False)
        value = [jnp.where(pair == 1, pltpu.roll(x, LANES - 8, 1), x) for x in value]
        for f in range(FIELDS):
            for l in range(LEVELS):
                seg = 16 * (LEVELS * (f % 2) + l)
                sides = pltpu.roll(value[f // 2], LANES - 4 - seg, 1)
                buf[f, l, rows(t), cols(0)] = jnp.where(lane < 2, sides, i_ref[f, l, rows(t), cols(0)])
                buf[f, l, rows(t), cols(1)] = jnp.where(lane >= LANES - 2, sides, i_ref[f, l, rows(t), cols(1)])
        send(t).start()

    @pl.loop(0, tiles)
    def _(t):
        send(t).wait()


def per_device(state_adjoint, east_velocity, north_velocity, ocean_mask, partner):
    nlon, nlat = lax.axis_size("lon"), lax.axis_size("lat")
    fields, levels, height, width = state_adjoint.shape
    axes = ("lon", "lat")
    f32 = jnp.float32

    def device(lon, lat):
        return lon % nlon * nlat + lat

    def both(a, b):
        return [(a, b), (b, a)]

    fold = [(device(nlon - 1 - i, nlat - 1), device(i, nlat - 1)) for i in range(nlon)]
    fold_next = [(device(nlon - i, nlat - 1), device(i, nlat - 1)) for i in range(nlon)]
    within = [e for i in range(nlon) for j in range(0, nlat, 2) for e in both(device(i, j), device(i, j + 1))]
    across = [e for i in range(nlon) for j in range(1, nlat - 1, 2) for e in both(device(i, j), device(i, j + 1))]
    even = [e for i in range(0, nlon, 2) for j in range(nlat) for e in both(device(i, j), device(i + 1, j))]
    odd = [e for i in range(1, nlon, 2) for j in range(nlat) for e in both(device(i, j), device(i + 1, j))]

    def held(x):
        return pltpu.with_memory_space_constraint(x, pltpu.VMEM)

    def call(kernel, name, args, outs, scratch=(), aliases=None, micros=1):
        return pl.pallas_call(
            kernel,
            out_shape=tuple(pltpu.VMEM(shape, f32) for shape in outs),
            in_specs=[VMEM] * len(args),
            out_specs=(VMEM,) * len(outs),
            scratch_shapes=[pltpu.VMEM(shape, f32) for shape in scratch],
            input_output_aliases=aliases or {},
            cost_estimate=pl.CostEstimate(flops=0, bytes_accessed=micros * 3_000_000, transcendentals=0),
            compiler_params=pltpu.CompilerParams(vmem_limit_bytes=SCOPED),
            name=name,
        )(*(held(x) for x in args))

    inputs = (state_adjoint, east_velocity, north_velocity, ocean_mask)
    message = (SUBS * (levels + 2), width)
    to_a, to_b = pl.pallas_call(
        row_kernel,
        out_shape=(pltpu.VMEM(message, f32), pltpu.VMEM(message, f32)),
        in_specs=[pl.BlockSpec(memory_space=pltpu.HBM)] * 4,
        out_specs=(VMEM,) * 2,
        scratch_shapes=[pltpu.VMEM((2,) + x.shape[:-2] + (SUBS, width), x.dtype) for x in inputs]
        + [pltpu.SemaphoreType.DMA((4, 2))],
        compiler_params=pltpu.CompilerParams(vmem_limit_bytes=SCOPED),
        name="pack_rows",
    )(*(pltpu.with_memory_space_constraint(x, pltpu.HBM) for x in inputs))
    from_a = lax.ppermute(to_a, axes, within)
    from_b = lax.ppermute(to_b, axes, across + fold)
    from_f = lax.ppermute(to_b, axes, fold_next)

    tall = height + 4 * SUBS
    ext = [(fields * levels, 2, tall, LANES)] + [(levels, 2, tall, LANES)] * 3
    pack, sides = (height + SUBS, LANES), (height // 2 + SUBS, LANES)
    laid = call(prepare_kernel, "prepare", inputs, (*ext, (5,) + pack, sides, sides))
    *laid, to_p, to_q = call(
        halo_kernel,
        "place_rows",
        (from_a, from_b, *laid),
        (*ext, (5,) + pack, sides, sides),
        [(2, message[0] + 2 * SUBS, LANES)] * 2,
        aliases={2 + i: i for i in range(7)},
    )
    from_p = lax.ppermute(to_p, axes, even)
    from_q = lax.ppermute(to_q, axes, odd)

    pairs = partner.reshape(2, LANES)
    *laid, packs = call(
        mirror_kernel,
        "mirror_rows",
        (pairs, from_b, from_f, *laid),
        (*ext, (5,) + pack),
        [(4, message[0] + SUBS, LANES)],
        aliases={3 + i: i for i in range(5)},
    )
    (inner,) = call(step_kernel, "both_steps", laid, (state_adjoint.shape,), [(fields, 2, tall, LANES), (2, tall, LANES)], micros=3)
    return pl.pallas_call(
        edge_kernel,
        out_shape=jax.ShapeDtypeStruct(state_adjoint.shape, f32),
        in_specs=[VMEM] * 5,
        out_specs=pl.BlockSpec(memory_space=pl.ANY),
        scratch_shapes=[
            pltpu.VMEM((5, tall, LANES), f32),
            pltpu.VMEM((2, tall, LANES), f32),
            pltpu.VMEM(state_adjoint.shape, f32),
            pltpu.SemaphoreType.DMA((height // SUBS,)),
        ],
        compiler_params=pltpu.CompilerParams(vmem_limit_bytes=SCOPED),
        name="edge_columns",
    )(*(held(x) for x in (pairs, packs, from_q, from_p, inner)))


def solution(mesh):
    placed = (
        P(None, None, "lat", "lon"),
        P(None, "lat", "lon"),
        P(None, "lat", "lon"),
        P(None, "lat", "lon"),
        P("lon"),
    )
    return jax.shard_map(
        per_device,
        mesh=mesh,
        in_specs=placed,
        out_specs=P(None, None, "lat", "lon"),
        check_vma=False,
    )
```

```python
import jax
import jax.numpy as jnp
from jax import lax
from jax.experimental import pallas as pl
from jax.experimental.pallas import tpu as pltpu
from jax.sharding import PartitionSpec as P

FIELDS, LEVELS = 4, 4
QN = FIELDS + 3
LANES, SUBS = 128, 8
SOUTH, OWN = 1, 2
VMEM = pl.BlockSpec(memory_space=pltpu.VMEM)
SCOPED = 4 << 20
UNROLL = 8


def iota(dim):
    return lax.broadcasted_iota(jnp.int32, (SUBS, LANES), dim)


def rows(t, by=0):
    start = SUBS * t
    if not isinstance(start, int):
        start = pl.multiple_of(start, SUBS)
    return pl.ds(start + by, SUBS)


def cols(c):
    return pl.ds(LANES * c, LANES)


def lat_place():
    lat = lax.axis_index("lat")
    return lat % 2 == 0, lat == lax.axis_size("lat") - 1


def sign_of(field):
    return 1.0 if field < 2 else -1.0


def row_kernel(s_in, u_in, v_in, m_in, a_ref, b_ref, s_ref, u_ref, v_ref, m_ref, sems):
    lat_even, _ = lat_place()
    sub = iota(0)
    copies = []
    for i, (src, dst) in enumerate(((s_in, s_ref), (u_in, u_ref), (v_in, v_ref), (m_in, m_ref))):
        lead = (slice(None),) * (len(src.shape) - 2)
        for k, t in enumerate((0, src.shape[-2] // SUBS - 1)):
            copies.append(pltpu.make_async_copy(src.at[lead + (rows(t), slice(None))], dst.at[k], sems.at[i, k]))
    for copy in copies:
        copy.start()
    for copy in copies:
        copy.wait()

    def put(t, c, values, where):
        low = high = jnp.zeros((SUBS, LANES), jnp.float32)
        for (south, north), (first, count) in zip(values, where):
            here = (sub >= first) & (sub < first + count)
            low = jnp.where(here, pltpu.roll(south, first, 0) if first else south, low)
            high = jnp.where(here, pltpu.roll(north, (first + count) % SUBS, 0) if (first + count) % SUBS else north, high)
        a_ref[rows(t), cols(c)] = jnp.where(lat_even, high, low)
        b_ref[rows(t), cols(c)] = jnp.where(lat_even, low, high)

    for c in range(2):

        @pl.loop(0, LEVELS)
        def _(l):
            w = [m_ref[k, l, :, cols(c)].astype(jnp.float32) for k in range(2)]
            values = [[s_ref[k, f, l, :, cols(c)] * w[k] for k in range(2)] for f in range(FIELDS)]
            put(l, c, values, [(2 * f, 2) for f in range(FIELDS)])

        u, v, w = (
            [[ref[k, l, :, cols(c)].astype(jnp.float32) for k in range(2)] for l in range(LEVELS)]
            for ref in (u_ref, v_ref, m_ref)
        )
        put(LEVELS, c, [[0.5 * x for x in pair] for pair in v], [(2 * l, 2) for l in range(LEVELS)])
        values = [[0.5 * x for x in pair] for pair in u] + w
        put(LEVELS + 1, c, values, [(l, 1) for l in range(2 * LEVELS)])


def place_in_message(l, q):
    if q < FIELDS:
        return SUBS * l + 2 * q, 2
    if q == FIELDS + 1:
        return SUBS * LEVELS + 2 * l, 2
    return SUBS * (LEVELS + 1) + l + (LEVELS if q > FIELDS else 0), 1


def insert(packs, lane, l, q, tile):
    seg = LEVELS * (q % 2) + l if q < FIELDS else l
    g = q // 2 if q < FIELDS else q - 2
    sides = pltpu.roll(jnp.where(lane < LANES // 2, tile[0], tile[1]), (16 * seg + 8) % LANES, 1)
    packs[g] = jnp.where((lane + 4) // 8 == 2 * seg + 1, sides, packs[g])


def arrange(pack, lane):
    return jnp.where(lane // 4 % 4 == 1, pltpu.roll(pack, LANES - 4, 1), pltpu.roll(pack, 4, 1))


def finish(packs, lane):
    for g in range(2, 5):
        packs[g] = jnp.where(lane < LANES // 2, packs[g], pltpu.roll(packs[g], LANES // 2, 1))


def turn(tile, by):
    by %= LANES
    return pltpu.roll(tile, by, 1) if by else tile


def slots(lane):
    slot = lane % 8
    return [(slot // 2 == g, 2 * g) for g in range(3)] + [(slot == 6, 6), (slot == 7, 7)]


def outgoing(packs, lane, lon_even, half, seam_rows=None):
    east = west = jnp.zeros((SUBS, LANES), jnp.float32)
    for g, (here, first) in enumerate(slots(lane)):
        to = first + 8 * half
        west_part = turn(packs[g], to - 8)
        if seam_rows is not None:
            west_part = jnp.where(seam_rows, turn(packs[g], to - 7), west_part)
        west = jnp.where(here, west_part, west)
        east = jnp.where(here, turn(packs[g], to - (6 if g < 3 else 7)), east)
    return jnp.where(lon_even, east, west), jnp.where(lon_even, west, east)


def prepare_kernel(s_ref, u_ref, v_ref, m_ref, r_ref, u2_ref, v2_ref, w_ref, k_ref, p_ref, q_ref):
    lane = iota(1)
    lon_even = lax.axis_index("lon") % 2 == 0

    @pl.loop(0, s_ref.shape[2] // SUBS // 2)
    def _(pair):
        sent = []
        for half in range(2):
            src, dst = rows(2 * pair + half), rows(2 * pair + half + OWN)
            packs = [jnp.zeros((SUBS, LANES), jnp.float32)] * 5
            for l in range(LEVELS):
                w = [m_ref[l, src, cols(c)].astype(jnp.float32) for c in range(2)]
                for q in range(QN):
                    if q < FIELDS:
                        ref, index, tile = r_ref, LEVELS * q + l, [s_ref[q, l, src, cols(c)] * w[c] for c in range(2)]
                    elif q < FIELDS + 2:
                        ref, index, x_ref = (u2_ref, v2_ref)[q - FIELDS], l, (u_ref, v_ref)[q - FIELDS]
                        tile = [0.5 * x_ref[l, src, cols(c)] for c in range(2)]
                    else:
                        ref, index, tile = w_ref, l, w
                    for c in range(2):
                        ref[index, c, dst, :] = tile[c]
                    insert(packs, lane, l, q, tile)
            finish(packs, lane)
            for g in range(5):
                k_ref[g, src, :] = arrange(packs[g], lane)
            sent.append(outgoing(packs, lane, lon_even, half))
        for ref, low, high in zip((p_ref, q_ref), *sent):
            ref[rows(pair), :] = jnp.where(lane % 16 < 8, low, high)


def partner_columns(c_ref, width):
    ncol = lax.axis_size("lon") * width
    lon = lax.axis_index("lon")
    return [lax.rem(c_ref[pl.ds(c, SUBS, stride=0), :] + (lon + 1) * width, ncol) for c in range(2)]


def halo_kernel(
    a_ref, b_ref, r_in, u2_in, v2_in, w_in, k_in, p_in, q_in,
    r_ref, u2_ref, v2_ref, w_ref, k_ref, p_ref, q_ref, north, south,
):
    lane, sub = iota(1), iota(0)
    lat_even, top = lat_place()
    lon_even = lax.axis_index("lon") % 2 == 0
    tiles = k_ref.shape[1] // SUBS - 1

    @pl.loop(0, LEVELS + 2, unroll=True)
    def _(i):
        for c in range(2):
            a, b = a_ref[rows(i), cols(c)], b_ref[rows(i), cols(c)]
            north[c, rows(i + 1), :] = jnp.where(lat_even, a, b)
            south[c, rows(i + 1), :] = jnp.where(lat_even, b, a)

    packs = [jnp.zeros((SUBS, LANES), jnp.float32)] * 5
    for l in range(LEVELS):
        for q in range(QN):
            ref = (u2_ref, v2_ref, w_ref)[q - FIELDS] if q >= FIELDS else r_ref
            index = LEVELS * q + l if q < FIELDS else l
            first, count = place_in_message(l, q)
            at, at_south = pl.ds(SUBS + first, SUBS), pl.ds(first + count, SUBS)
            tile = []
            for c in range(2):
                tile.append(jnp.where(sub < 4, north[c, at, :], south[c, at_south, :]))
                ref[index, c, rows(SOUTH), :] = tile[c]
                ref[index, c, rows(tiles + OWN), :] = tile[c]
            insert(packs, lane, l, q, tile)
    finish(packs, lane)
    for g in range(5):
        k_ref[g, rows(tiles), :] = arrange(packs[g], lane)
    to = rows(tiles // 2)
    p_ref[to, :], q_ref[to, :] = outgoing(packs, lane, lon_even, 0, top & (sub < 2))


def mirror_kernel(
    c_ref, b_ref, f_ref, r_in, u2_in, v2_in, w_in, k_in, r_ref, u2_ref, v2_ref, w_ref, k_ref, mirrored
):
    lane, sub = iota(1), iota(0)
    _, top = lat_place()
    width = b_ref.shape[1]
    tiles = k_ref.shape[1] // SUBS - 1

    def pick(raw, which, p):
        tile = jnp.where(which < 2, jnp.where(which < 1, raw[0], raw[1]), jnp.where(which < 3, raw[2], raw[3]))
        return jnp.take_along_axis(tile, p % LANES, axis=1, mode="promise_in_bounds")

    @pl.when(top)
    def _():
        source = partner_columns(c_ref, width)
        before = jnp.broadcast_to(source[0][:, :1] + 1, (SUBS, LANES))
        after = jnp.broadcast_to(jnp.maximum(source[1][:, LANES - 1 :] - 1, 0), (SUBS, LANES))

        for t in range(LEVELS + 2):
            raw = [(b_ref if s < 2 else f_ref)[rows(t), cols(s % 2)] for s in range(4)]
            for c, p in enumerate((*source, before, after)):
                last = jnp.broadcast_to(p[:, :1] // LANES, (SUBS, LANES))
                got = pick(raw, last, p)
                if c < 2:
                    got = jnp.where(p // LANES == last, got, pick(raw, last - 1, p))
                if t < LEVELS:
                    got = jnp.where(sub % 2 == 0, pltpu.roll(got, SUBS - 1, 0), pltpu.roll(got, 1, 0))
                elif t == LEVELS:
                    got = jnp.where(sub % 2 == 0, -got, got)
                mirrored[c, rows(t), :] = got

        packs, halo = ([jnp.zeros((SUBS, LANES), jnp.float32)] * 5 for _ in range(2))
        for l in range(LEVELS):
            for q in range(QN):
                ref = (u2_ref, v2_ref, w_ref)[q - FIELDS] if q >= FIELDS else r_ref
                index = LEVELS * q + l if q < FIELDS else l
                seg = LEVELS * (q % 2) + l if q < FIELDS else l
                pack = q // 2 if q < FIELDS else q - 2
                tile = [mirrored[c, pl.ds(place_in_message(l, q)[0], SUBS), :] for c in range(4)]
                insert(packs, lane, l, q, tile)
                for c in range(2):
                    north = tile[c]
                    if q == FIELDS:
                        north = -pltpu.roll(jnp.where(lane == 0, tile[1 - c], tile[c]), LANES - 1, 1)
                    ref[index, c, rows(tiles + OWN), :] = north
                halo[pack] = jnp.where(lane == 16 * seg + 3, tile[2], halo[pack])
                halo[pack] = jnp.where(lane == 16 * seg + 12, tile[3], halo[pack])
        finish(packs, lane)
        finish(halo, lane)
        for g in range(5):
            value = jnp.where((lane % 16 == 3) | (lane % 16 == 12), halo[g], arrange(packs[g], lane))
            k_ref[g, rows(tiles), :] = jnp.where(sub < 2, value, k_in[g, rows(tiles), :])


def seam(r, r_mirror, h, h_mirror, w, sign):
    return w * r_mirror * (sign * (0.5 + h_mirror) - h)


def seam_mirror(r, r_top, h_top, h, w, sign):
    return w * (sign * (0.5 + h_top) * r_top - h * r - h_top * (r - r_top))


def step_kernel(r_ref, u2_ref, v2_ref, w_ref, o_ref, r1, uw):
    lane, sub = iota(1), iota(0)
    _, top = lat_place()
    tiles = o_ref.shape[2] // SUBS
    end = OWN + tiles

    def update(l, look, load, first):
        def of(ref, c):
            return lambda at: ref[l, c, at, :]

        u = [look(of(u2_ref, c), 0) for c in range(2)]
        if first:
            u_west = [pltpu.roll(jnp.where(lane == LANES - 1, u[1 - c], u[c]), 1, 1) for c in range(2)]
        else:
            u_west = [look(lambda at, c=c: uw[c, at, :], 0) for c in range(2)]
        v = [look(of(v2_ref, c), 0) for c in range(2)]
        v_south = [look(of(v2_ref, c), -1) for c in range(2)]
        w = [look(of(w_ref, c), 0) for c in range(2)]
        out = []
        for f in range(FIELDS):
            reads = [lambda at, c=c: load(f, c, at) for c in range(2)]
            r = [look(read, 0) for read in reads]
            for c in range(2):
                ahead = pltpu.roll(jnp.where(lane == 0, r[1 - c], r[c]), LANES - 1, 1)
                behind = pltpu.roll(jnp.where(lane == LANES - 1, r[1 - c], r[c]), 1, 1)
                along = u[c] * (ahead - r[c]) + u_west[c] * (r[c] - behind)
                up = v[c] * (look(reads[c], 1) - r[c])
                down = v_south[c] * (r[c] - look(reads[c], -1))
                out.append((f, c, w[c] * (r[c] + along + up + down)))
        return out, u_west

    def tile(t):
        return lambda read, by: read(rows(t, by))

    def outside(read, by):
        return jnp.where(sub < SUBS // 2, read(rows(end, by)), read(rows(SOUTH, by)))

    @pl.loop(0, LEVELS)
    def _(l):
        def first(f, c, at):
            return r_ref[LEVELS * f + l, c, at, :]

        def second(f, c, at):
            return r1[f, c, at, :]

        def at_top(f, c, load):
            v, v_mirror = v2_ref[l, c, rows(end - 1), :], v2_ref[l, c, rows(end - 1, 2), :]
            r, r_mirror = load(f, c, rows(end - 1)), load(f, c, rows(end - 1, 1))
            add = seam(r, r_mirror, v, v_mirror, w_ref[l, c, rows(end - 1), :], sign_of(f))
            return jnp.where(top & (sub == SUBS - 1), add, 0.0)

        def at_mirror(f, c):
            v_top, v_mirror = v2_ref[l, c, rows(end, -1), :], v2_ref[l, c, rows(end, 1), :]
            r, r_top = first(f, c, rows(end)), first(f, c, rows(end, -1))
            add = seam_mirror(r, r_top, v_top, v_mirror, w_ref[l, c, rows(end), :], sign_of(f))
            return jnp.where(top & (sub == 0), add, 0.0)

        for f, c, value in update(l, outside, first, True)[0]:
            r1[f, c, rows(SOUTH), :] = value
            r1[f, c, rows(end), :] = value + at_mirror(f, c)

        for t in range(OWN, end):
            values, u_west = update(l, tile(t), first, True)
            for c in range(2):
                uw[c, rows(t), :] = u_west[c]
            for f, c, value in values:
                r1[f, c, rows(t), :] = value + at_top(f, c, first) if t == end - 1 else value

        for t in range(OWN, end):
            for f, c, value in update(l, tile(t), second, False)[0]:
                o_ref[f, l, rows(t - OWN), cols(c)] = value + at_top(f, c, second) if t == end - 1 else value


def edge_kernel(c_ref, k_ref, q_ref, p_ref, i_ref, o_ref, z, z1, buf, sems):
    lane, sub = iota(1), iota(0)
    _, top = lat_place()
    lon_even = lax.axis_index("lon") % 2 == 0
    tiles = i_ref.shape[2] // SUBS
    end = OWN + tiles
    pair = lane // 2 % 8

    def join(t):
        p, q = p_ref[rows(t // 2), :], q_ref[rows(t // 2), :]
        from_west, from_east = jnp.where(lon_even, q, p), jnp.where(lon_even, p, q)
        out = []
        for g, (_, first) in enumerate(slots(lane)):
            at = first + 8 * (t % 2)
            west, east = turn(from_west, (2 if g < 3 else 3) - at), turn(from_east, 12 - at)
            out.append((jnp.where(pair == 1, west, jnp.where(pair == 6, east, k_ref[g, rows(t), :])), east))
        return out

    for t in range(tiles):
        for g, (value, _) in enumerate(join(t)):
            z[g, rows(t + OWN), :] = value

    at_seam = partner_columns(c_ref, i_ref.shape[3])[1][:, LANES - 1 :] == 0
    for g, (value, crossed) in enumerate(join(tiles)):
        z[g, rows(SOUTH), :] = value
        if g < 2:
            crossed = pltpu.roll(crossed, SUBS - 1, 0)
        kept = jnp.where((pair == 6) & at_seam, crossed, k_ref[g, rows(tiles), :])
        value = jnp.where(top & (sub < 2), kept, value)
        if g == 2:
            value = jnp.where(top & (sub == 0), -pltpu.roll(value, LANES - 1, 1), value)
        z[g, rows(end), :] = value

    def update(t, load, mirrored):
        u, v, v_south, w = z[2, rows(t), :], z[3, rows(t), :], z[3, rows(t, -1), :], z[4, rows(t), :]
        u_west = pltpu.roll(u, 1, 1)
        out = []
        for h in range(2):
            r, r_north, r_south = load(h, rows(t)), load(h, rows(t, 1)), load(h, rows(t, -1))
            along = u * (pltpu.roll(r, LANES - 1, 1) - r) + u_west * (r - pltpu.roll(r, 1, 1))
            value = w * (r + along + v * (r_north - r) + v_south * (r - r_south))
            add = seam(r, r_north, v, z[3, rows(t, 2), :], w, sign_of(2 * h))
            value += jnp.where(top & (t == end - 1) & (sub == SUBS - 1), add, 0.0)
            if mirrored:
                add = seam_mirror(r, r_south, v_south, z[3, rows(t, 1), :], w, sign_of(2 * h))
                value += jnp.where(top & (t == end) & (sub == 0), add, 0.0)
            out.append(value)
        return out

    @pl.loop(SOUTH, end + 1, unroll=True)
    def _(t):
        for h, value in enumerate(update(t, lambda h, at: z[h, at, :], True)):
            z1[h, rows(t), :] = value

    def send(t):
        at = rows(t)
        return pltpu.make_async_copy(buf.at[:, :, at, :], o_ref.at[:, :, at, :], sems.at[t])

    @pl.loop(0, tiles, unroll=UNROLL)
    def _(t):
        value = update(t + OWN, lambda h, at: z1[h, at, :], False)
        value = [jnp.where(pair == 1, pltpu.roll(x, LANES - 8, 1), x) for x in value]
        for f in range(FIELDS):
            for l in range(LEVELS):
                seg = 16 * (LEVELS * (f % 2) + l)
                sides = pltpu.roll(value[f // 2], LANES - 4 - seg, 1)
                buf[f, l, rows(t), cols(0)] = jnp.where(lane < 2, sides, i_ref[f, l, rows(t), cols(0)])
                buf[f, l, rows(t), cols(1)] = jnp.where(lane >= LANES - 2, sides, i_ref[f, l, rows(t), cols(1)])
        send(t).start()

    @pl.loop(0, tiles)
    def _(t):
        send(t).wait()


def per_device(state_adjoint, east_velocity, north_velocity, ocean_mask, partner):
    nlon, nlat = lax.axis_size("lon"), lax.axis_size("lat")
    fields, levels, height, width = state_adjoint.shape
    axes = ("lon", "lat")
    f32 = jnp.float32

    def device(lon, lat):
        return lon % nlon * nlat + lat

    def both(a, b):
        return [(a, b), (b, a)]

    fold = [(device(nlon - 1 - i, nlat - 1), device(i, nlat - 1)) for i in range(nlon)]
    fold_next = [(device(nlon - i, nlat - 1), device(i, nlat - 1)) for i in range(nlon)]
    within = [e for i in range(nlon) for j in range(0, nlat, 2) for e in both(device(i, j), device(i, j + 1))]
    across = [e for i in range(nlon) for j in range(1, nlat - 1, 2) for e in both(device(i, j), device(i, j + 1))]
    even = [e for i in range(0, nlon, 2) for j in range(nlat) for e in both(device(i, j), device(i + 1, j))]
    odd = [e for i in range(1, nlon, 2) for j in range(nlat) for e in both(device(i, j), device(i + 1, j))]

    def held(x):
        return pltpu.with_memory_space_constraint(x, pltpu.VMEM)

    def call(kernel, name, args, outs, scratch=(), aliases=None, micros=1):
        return pl.pallas_call(
            kernel,
            out_shape=tuple(pltpu.VMEM(shape, f32) for shape in outs),
            in_specs=[VMEM] * len(args),
            out_specs=(VMEM,) * len(outs),
            scratch_shapes=[pltpu.VMEM(shape, f32) for shape in scratch],
            input_output_aliases=aliases or {},
            cost_estimate=pl.CostEstimate(flops=0, bytes_accessed=micros * 3_000_000, transcendentals=0),
            compiler_params=pltpu.CompilerParams(vmem_limit_bytes=SCOPED),
            name=name,
        )(*(held(x) for x in args))

    inputs = (state_adjoint, east_velocity, north_velocity, ocean_mask)
    message = (SUBS * (levels + 2), width)
    to_a, to_b = pl.pallas_call(
        row_kernel,
        out_shape=(pltpu.VMEM(message, f32), pltpu.VMEM(message, f32)),
        in_specs=[pl.BlockSpec(memory_space=pltpu.HBM)] * 4,
        out_specs=(VMEM,) * 2,
        scratch_shapes=[pltpu.VMEM((2,) + x.shape[:-2] + (SUBS, width), x.dtype) for x in inputs]
        + [pltpu.SemaphoreType.DMA((4, 2))],
        compiler_params=pltpu.CompilerParams(vmem_limit_bytes=SCOPED),
        name="pack_rows",
    )(*(pltpu.with_memory_space_constraint(x, pltpu.HBM) for x in inputs))
    from_a = lax.ppermute(to_a, axes, within)
    from_b = lax.ppermute(to_b, axes, across + fold)
    from_f = lax.ppermute(to_b, axes, fold_next)

    tall = height + 4 * SUBS
    ext = [(fields * levels, 2, tall, LANES)] + [(levels, 2, tall, LANES)] * 3
    pack, sides = (height + SUBS, LANES), (height // 2 + SUBS, LANES)
    laid = call(prepare_kernel, "prepare", inputs, (*ext, (5,) + pack, sides, sides))
    *laid, to_p, to_q = call(
        halo_kernel,
        "place_rows",
        (from_a, from_b, *laid),
        (*ext, (5,) + pack, sides, sides),
        [(2, message[0] + 2 * SUBS, LANES)] * 2,
        aliases={2 + i: i for i in range(7)},
    )
    from_p = lax.ppermute(to_p, axes, even)
    from_q = lax.ppermute(to_q, axes, odd)

    pairs = partner.reshape(2, LANES)
    *laid, packs = call(
        mirror_kernel,
        "mirror_rows",
        (pairs, from_b, from_f, *laid),
        (*ext, (5,) + pack),
        [(4, message[0] + SUBS, LANES)],
        aliases={3 + i: i for i in range(5)},
    )
    (inner,) = call(step_kernel, "both_steps", laid, (state_adjoint.shape,), [(fields, 2, tall, LANES), (2, tall, LANES)], micros=3)
    return pl.pallas_call(
        edge_kernel,
        out_shape=jax.ShapeDtypeStruct(state_adjoint.shape, f32),
        in_specs=[VMEM] * 5,
        out_specs=pl.BlockSpec(memory_space=pl.ANY),
        scratch_shapes=[
            pltpu.VMEM((5, tall, LANES), f32),
            pltpu.VMEM((2, tall, LANES), f32),
            pltpu.VMEM(state_adjoint.shape, f32),
            pltpu.SemaphoreType.DMA((height // SUBS,)),
        ],
        compiler_params=pltpu.CompilerParams(vmem_limit_bytes=SCOPED),
        name="edge_columns",
    )(*(held(x) for x in (pairs, packs, from_q, from_p, inner)))


def solution(mesh):
    placed = (
        P(None, None, "lat", "lon"),
        P(None, "lat", "lon"),
        P(None, "lat", "lon"),
        P(None, "lat", "lon"),
        P("lon"),
    )
    return jax.shard_map(
        per_device,
        mesh=mesh,
        in_specs=placed,
        out_specs=P(None, None, "lat", "lon"),
        check_vma=False,
    )
```

```python
import jax
import jax.numpy as jnp
from jax import lax
from jax.experimental import pallas as pl
from jax.experimental.pallas import tpu as pltpu
from jax.sharding import PartitionSpec as P

FIELDS, LEVELS = 4, 4
QN = FIELDS + 3
LANES, SUBS = 128, 8
SOUTH, OWN = 1, 2
VMEM = pl.BlockSpec(memory_space=pltpu.VMEM)
SCOPED = 4 << 20


def iota(dim):
    return lax.broadcasted_iota(jnp.int32, (SUBS, LANES), dim)


def rows(t, by=0):
    start = SUBS * t
    if not isinstance(start, int):
        start = pl.multiple_of(start, SUBS)
    return pl.ds(start + by, SUBS)


def cols(c):
    return pl.ds(LANES * c, LANES)


def lat_place():
    lat = lax.axis_index("lat")
    return lat % 2 == 0, lat == lax.axis_size("lat") - 1


def sign_of(field):
    return 1.0 if field < 2 else -1.0


def row_kernel(s_in, u_in, v_in, m_in, a_ref, b_ref, s_ref, u_ref, v_ref, m_ref, sems):
    lat_even, _ = lat_place()
    sub = iota(0)
    copies = []
    for i, (src, dst) in enumerate(((s_in, s_ref), (u_in, u_ref), (v_in, v_ref), (m_in, m_ref))):
        lead = (slice(None),) * (len(src.shape) - 2)
        for k, t in enumerate((0, src.shape[-2] // SUBS - 1)):
            copies.append(pltpu.make_async_copy(src.at[lead + (rows(t), slice(None))], dst.at[k], sems.at[i, k]))
    for copy in copies:
        copy.start()
    for copy in copies:
        copy.wait()

    def put(t, c, values, where):
        low = high = jnp.zeros((SUBS, LANES), jnp.float32)
        for (south, north), (first, count) in zip(values, where):
            here = (sub >= first) & (sub < first + count)
            low = jnp.where(here, pltpu.roll(south, first, 0) if first else south, low)
            high = jnp.where(here, pltpu.roll(north, (first + count) % SUBS, 0) if (first + count) % SUBS else north, high)
        a_ref[rows(t), cols(c)] = jnp.where(lat_even, high, low)
        b_ref[rows(t), cols(c)] = jnp.where(lat_even, low, high)

    for c in range(2):

        @pl.loop(0, LEVELS)
        def _(l):
            w = [m_ref[k, l, :, cols(c)].astype(jnp.float32) for k in range(2)]
            values = [[s_ref[k, f, l, :, cols(c)] * w[k] for k in range(2)] for f in range(FIELDS)]
            put(l, c, values, [(2 * f, 2) for f in range(FIELDS)])

        u, v, w = (
            [[ref[k, l, :, cols(c)].astype(jnp.float32) for k in range(2)] for l in range(LEVELS)]
            for ref in (u_ref, v_ref, m_ref)
        )
        put(LEVELS, c, [[0.5 * x for x in pair] for pair in v], [(2 * l, 2) for l in range(LEVELS)])
        values = [[0.5 * x for x in pair] for pair in u] + w
        put(LEVELS + 1, c, values, [(l, 1) for l in range(2 * LEVELS)])


def place_in_message(l, q):
    if q < FIELDS:
        return SUBS * l + 2 * q, 2
    if q == FIELDS + 1:
        return SUBS * LEVELS + 2 * l, 2
    return SUBS * (LEVELS + 1) + l + (LEVELS if q > FIELDS else 0), 1


def insert(packs, lane, l, q, tile):
    seg = LEVELS * (q % 2) + l if q < FIELDS else l
    g = q // 2 if q < FIELDS else q - 2
    sides = pltpu.roll(jnp.where(lane < LANES // 2, tile[0], tile[1]), (16 * seg + 8) % LANES, 1)
    packs[g] = jnp.where((lane + 4) // 8 == 2 * seg + 1, sides, packs[g])


def arrange(pack, lane):
    return jnp.where(lane // 4 % 4 == 1, pltpu.roll(pack, LANES - 4, 1), pltpu.roll(pack, 4, 1))


def finish(packs, lane):
    for g in range(2, 5):
        packs[g] = jnp.where(lane < LANES // 2, packs[g], pltpu.roll(packs[g], LANES // 2, 1))


def turn(tile, by):
    by %= LANES
    return pltpu.roll(tile, by, 1) if by else tile


def slots(lane):
    slot = lane % 8
    return [(slot // 2 == g, 2 * g) for g in range(3)] + [(slot == 6, 6), (slot == 7, 7)]


def outgoing(packs, lane, lon_even, half, seam_rows=None):
    east = west = jnp.zeros((SUBS, LANES), jnp.float32)
    for g, (here, first) in enumerate(slots(lane)):
        to = first + 8 * half
        west_part = turn(packs[g], to - 8)
        if seam_rows is not None:
            west_part = jnp.where(seam_rows, turn(packs[g], to - 7), west_part)
        west = jnp.where(here, west_part, west)
        east = jnp.where(here, turn(packs[g], to - (6 if g < 3 else 7)), east)
    return jnp.where(lon_even, east, west), jnp.where(lon_even, west, east)


def prepare_kernel(s_ref, u_ref, v_ref, m_ref, r_ref, u2_ref, v2_ref, w_ref, k_ref, p_ref, q_ref):
    lane = iota(1)
    lon_even = lax.axis_index("lon") % 2 == 0

    @pl.loop(0, s_ref.shape[2] // SUBS // 2)
    def _(pair):
        sent = []
        for half in range(2):
            src, dst = rows(2 * pair + half), rows(2 * pair + half + OWN)
            packs = [jnp.zeros((SUBS, LANES), jnp.float32)] * 5
            for l in range(LEVELS):
                w = [m_ref[l, src, cols(c)].astype(jnp.float32) for c in range(2)]
                for q in range(QN):
                    if q < FIELDS:
                        ref, index, tile = r_ref, LEVELS * q + l, [s_ref[q, l, src, cols(c)] * w[c] for c in range(2)]
                    elif q < FIELDS + 2:
                        ref, index, x_ref = (u2_ref, v2_ref)[q - FIELDS], l, (u_ref, v_ref)[q - FIELDS]
                        tile = [0.5 * x_ref[l, src, cols(c)] for c in range(2)]
                    else:
                        ref, index, tile = w_ref, l, w
                    for c in range(2):
                        ref[index, c, dst, :] = tile[c]
                    insert(packs, lane, l, q, tile)
            finish(packs, lane)
            for g in range(5):
                k_ref[g, src, :] = arrange(packs[g], lane)
            sent.append(outgoing(packs, lane, lon_even, half))
        for ref, low, high in zip((p_ref, q_ref), *sent):
            ref[rows(pair), :] = jnp.where(lane % 16 < 8, low, high)


def partner_columns(c_ref, width):
    ncol = lax.axis_size("lon") * width
    lon = lax.axis_index("lon")
    return [lax.rem(c_ref[pl.ds(c, SUBS, stride=0), :] + (lon + 1) * width, ncol) for c in range(2)]


def halo_kernel(
    a_ref, b_ref, r_in, u2_in, v2_in, w_in, k_in, p_in, q_in,
    r_ref, u2_ref, v2_ref, w_ref, k_ref, p_ref, q_ref, north, south,
):
    lane, sub = iota(1), iota(0)
    lat_even, top = lat_place()
    lon_even = lax.axis_index("lon") % 2 == 0
    tiles = k_ref.shape[1] // SUBS - 1

    @pl.loop(0, LEVELS + 2, unroll=True)
    def _(i):
        for c in range(2):
            a, b = a_ref[rows(i), cols(c)], b_ref[rows(i), cols(c)]
            north[c, rows(i + 1), :] = jnp.where(lat_even, a, b)
            south[c, rows(i + 1), :] = jnp.where(lat_even, b, a)

    packs = [jnp.zeros((SUBS, LANES), jnp.float32)] * 5
    for l in range(LEVELS):
        for q in range(QN):
            ref = (u2_ref, v2_ref, w_ref)[q - FIELDS] if q >= FIELDS else r_ref
            index = LEVELS * q + l if q < FIELDS else l
            first, count = place_in_message(l, q)
            at, at_south = pl.ds(SUBS + first, SUBS), pl.ds(first + count, SUBS)
            tile = []
            for c in range(2):
                tile.append(jnp.where(sub < 4, north[c, at, :], south[c, at_south, :]))
                ref[index, c, rows(SOUTH), :] = tile[c]
                ref[index, c, rows(tiles + OWN), :] = tile[c]
            insert(packs, lane, l, q, tile)
    finish(packs, lane)
    for g in range(5):
        k_ref[g, rows(tiles), :] = arrange(packs[g], lane)
    to = rows(tiles // 2)
    p_ref[to, :], q_ref[to, :] = outgoing(packs, lane, lon_even, 0, top & (sub < 2))


def mirror_kernel(
    c_ref, b_ref, f_ref, r_in, u2_in, v2_in, w_in, k_in, r_ref, u2_ref, v2_ref, w_ref, k_ref, mirrored
):
    lane, sub = iota(1), iota(0)
    _, top = lat_place()
    width = b_ref.shape[1]
    tiles = k_ref.shape[1] // SUBS - 1

    def pick(raw, which, p):
        tile = jnp.where(which < 2, jnp.where(which < 1, raw[0], raw[1]), jnp.where(which < 3, raw[2], raw[3]))
        return jnp.take_along_axis(tile, p % LANES, axis=1, mode="promise_in_bounds")

    @pl.when(top)
    def _():
        source = partner_columns(c_ref, width)
        before = jnp.broadcast_to(source[0][:, :1] + 1, (SUBS, LANES))
        after = jnp.broadcast_to(jnp.maximum(source[1][:, LANES - 1 :] - 1, 0), (SUBS, LANES))

        for t in range(LEVELS + 2):
            raw = [(b_ref if s < 2 else f_ref)[rows(t), cols(s % 2)] for s in range(4)]
            for c, p in enumerate((*source, before, after)):
                last = jnp.broadcast_to(p[:, :1] // LANES, (SUBS, LANES))
                got = pick(raw, last, p)
                if c < 2:
                    got = jnp.where(p // LANES == last, got, pick(raw, last - 1, p))
                if t < LEVELS:
                    got = jnp.where(sub % 2 == 0, pltpu.roll(got, SUBS - 1, 0), pltpu.roll(got, 1, 0))
                elif t == LEVELS:
                    got = jnp.where(sub % 2 == 0, -got, got)
                mirrored[c, rows(t), :] = got

        packs, halo = ([jnp.zeros((SUBS, LANES), jnp.float32)] * 5 for _ in range(2))
        for l in range(LEVELS):
            for q in range(QN):
                ref = (u2_ref, v2_ref, w_ref)[q - FIELDS] if q >= FIELDS else r_ref
                index = LEVELS * q + l if q < FIELDS else l
                seg = LEVELS * (q % 2) + l if q < FIELDS else l
                pack = q // 2 if q < FIELDS else q - 2
                tile = [mirrored[c, pl.ds(place_in_message(l, q)[0], SUBS), :] for c in range(4)]
                insert(packs, lane, l, q, tile)
                for c in range(2):
                    north = tile[c]
                    if q == FIELDS:
                        north = -pltpu.roll(jnp.where(lane == 0, tile[1 - c], tile[c]), LANES - 1, 1)
                    ref[index, c, rows(tiles + OWN), :] = north
                halo[pack] = jnp.where(lane == 16 * seg + 3, tile[2], halo[pack])
                halo[pack] = jnp.where(lane == 16 * seg + 12, tile[3], halo[pack])
        finish(packs, lane)
        finish(halo, lane)
        for g in range(5):
            value = jnp.where((lane % 16 == 3) | (lane % 16 == 12), halo[g], arrange(packs[g], lane))
            k_ref[g, rows(tiles), :] = jnp.where(sub < 2, value, k_in[g, rows(tiles), :])


def seam(r, r_mirror, h, h_mirror, w, sign):
    return w * r_mirror * (sign * (0.5 + h_mirror) - h)


def seam_mirror(r, r_top, h_top, h, w, sign):
    return w * (sign * (0.5 + h_top) * r_top - h * r - h_top * (r - r_top))


def step_kernel(r_ref, u2_ref, v2_ref, w_ref, o_ref, r1, uw):
    lane, sub = iota(1), iota(0)
    _, top = lat_place()
    tiles = o_ref.shape[2] // SUBS
    end = OWN + tiles

    def update(l, look, load, first):
        def of(ref, c):
            return lambda at: ref[l, c, at, :]

        u = [look(of(u2_ref, c), 0) for c in range(2)]
        if first:
            u_west = [pltpu.roll(jnp.where(lane == LANES - 1, u[1 - c], u[c]), 1, 1) for c in range(2)]
        else:
            u_west = [look(lambda at, c=c: uw[c, at, :], 0) for c in range(2)]
        v = [look(of(v2_ref, c), 0) for c in range(2)]
        v_south = [look(of(v2_ref, c), -1) for c in range(2)]
        w = [look(of(w_ref, c), 0) for c in range(2)]
        out = []
        for f in range(FIELDS):
            reads = [lambda at, c=c: load(f, c, at) for c in range(2)]
            r = [look(read, 0) for read in reads]
            for c in range(2):
                ahead = pltpu.roll(jnp.where(lane == 0, r[1 - c], r[c]), LANES - 1, 1)
                behind = pltpu.roll(jnp.where(lane == LANES - 1, r[1 - c], r[c]), 1, 1)
                along = u[c] * (ahead - r[c]) + u_west[c] * (r[c] - behind)
                up = v[c] * (look(reads[c], 1) - r[c])
                down = v_south[c] * (r[c] - look(reads[c], -1))
                out.append((f, c, w[c] * (r[c] + along + up + down)))
        return out, u_west

    def tile(t):
        return lambda read, by: read(rows(t, by))

    def outside(read, by):
        return jnp.where(sub < SUBS // 2, read(rows(end, by)), read(rows(SOUTH, by)))

    @pl.loop(0, LEVELS)
    def _(l):
        def first(f, c, at):
            return r_ref[LEVELS * f + l, c, at, :]

        def second(f, c, at):
            return r1[f, c, at, :]

        def at_top(f, c, load):
            v, v_mirror = v2_ref[l, c, rows(end - 1), :], v2_ref[l, c, rows(end - 1, 2), :]
            r, r_mirror = load(f, c, rows(end - 1)), load(f, c, rows(end - 1, 1))
            add = seam(r, r_mirror, v, v_mirror, w_ref[l, c, rows(end - 1), :], sign_of(f))
            return jnp.where(top & (sub == SUBS - 1), add, 0.0)

        def at_mirror(f, c):
            v_top, v_mirror = v2_ref[l, c, rows(end, -1), :], v2_ref[l, c, rows(end, 1), :]
            r, r_top = first(f, c, rows(end)), first(f, c, rows(end, -1))
            add = seam_mirror(r, r_top, v_top, v_mirror, w_ref[l, c, rows(end), :], sign_of(f))
            return jnp.where(top & (sub == 0), add, 0.0)

        for f, c, value in update(l, outside, first, True)[0]:
            r1[f, c, rows(SOUTH), :] = value
            r1[f, c, rows(end), :] = value + at_mirror(f, c)

        for t in range(OWN, end):
            values, u_west = update(l, tile(t), first, True)
            for c in range(2):
                uw[c, rows(t), :] = u_west[c]
            for f, c, value in values:
                r1[f, c, rows(t), :] = value + at_top(f, c, first) if t == end - 1 else value

        for t in range(OWN, end):
            for f, c, value in update(l, tile(t), second, False)[0]:
                o_ref[f, l, rows(t - OWN), cols(c)] = value + at_top(f, c, second) if t == end - 1 else value


def edge_kernel(c_ref, k_ref, q_ref, p_ref, i_ref, o_ref, z, z1, buf, sems):
    lane, sub = iota(1), iota(0)
    _, top = lat_place()
    lon_even = lax.axis_index("lon") % 2 == 0
    tiles = i_ref.shape[2] // SUBS
    end = OWN + tiles
    pair = lane // 2 % 8

    def join(t):
        p, q = p_ref[rows(t // 2), :], q_ref[rows(t // 2), :]
        from_west, from_east = jnp.where(lon_even, q, p), jnp.where(lon_even, p, q)
        out = []
        for g, (_, first) in enumerate(slots(lane)):
            at = first + 8 * (t % 2)
            west, east = turn(from_west, (2 if g < 3 else 3) - at), turn(from_east, 12 - at)
            out.append((jnp.where(pair == 1, west, jnp.where(pair == 6, east, k_ref[g, rows(t), :])), east))
        return out

    for t in range(tiles):
        for g, (value, _) in enumerate(join(t)):
            z[g, rows(t + OWN), :] = value

    at_seam = partner_columns(c_ref, i_ref.shape[3])[1][:, LANES - 1 :] == 0
    for g, (value, crossed) in enumerate(join(tiles)):
        z[g, rows(SOUTH), :] = value
        if g < 2:
            crossed = pltpu.roll(crossed, SUBS - 1, 0)
        kept = jnp.where((pair == 6) & at_seam, crossed, k_ref[g, rows(tiles), :])
        value = jnp.where(top & (sub < 2), kept, value)
        if g == 2:
            value = jnp.where(top & (sub == 0), -pltpu.roll(value, LANES - 1, 1), value)
        z[g, rows(end), :] = value

    def update(t, load):
        u, v, v_south, w = z[2, rows(t), :], z[3, rows(t), :], z[3, rows(t, -1), :], z[4, rows(t), :]
        u_west = pltpu.roll(u, 1, 1)
        out = []
        for h in range(2):
            r, r_north, r_south = load(h, rows(t)), load(h, rows(t, 1)), load(h, rows(t, -1))
            along = u * (pltpu.roll(r, LANES - 1, 1) - r) + u_west * (r - pltpu.roll(r, 1, 1))
            value = w * (r + along + v * (r_north - r) + v_south * (r - r_south))
            if t == end - 1:
                add = seam(r, r_north, v, z[3, rows(t, 2), :], w, sign_of(2 * h))
                value += jnp.where(top & (sub == SUBS - 1), add, 0.0)
            if t == end:
                add = seam_mirror(r, r_south, v_south, z[3, rows(t, 1), :], w, sign_of(2 * h))
                value += jnp.where(top & (sub == 0), add, 0.0)
            out.append(value)
        return out

    for t in range(SOUTH, end + 1):
        for h, value in enumerate(update(t, lambda h, at: z[h, at, :])):
            z1[h, rows(t), :] = value

    def send(t):
        at = rows(t)
        return pltpu.make_async_copy(buf.at[:, :, at, :], o_ref.at[:, :, at, :], sems.at[t])

    for t in range(tiles):
        value = update(t + OWN, lambda h, at: z1[h, at, :])
        value = [jnp.where(pair == 1, pltpu.roll(x, LANES - 8, 1), x) for x in value]
        for f in range(FIELDS):
            for l in range(LEVELS):
                seg = 16 * (LEVELS * (f % 2) + l)
                sides = pltpu.roll(value[f // 2], LANES - 4 - seg, 1)
                buf[f, l, rows(t), cols(0)] = jnp.where(lane < 2, sides, i_ref[f, l, rows(t), cols(0)])
                buf[f, l, rows(t), cols(1)] = jnp.where(lane >= LANES - 2, sides, i_ref[f, l, rows(t), cols(1)])
        send(t).start()

    @pl.loop(0, tiles)
    def _(t):
        send(t).wait()


def per_device(state_adjoint, east_velocity, north_velocity, ocean_mask, partner):
    nlon, nlat = lax.axis_size("lon"), lax.axis_size("lat")
    fields, levels, height, width = state_adjoint.shape
    axes = ("lon", "lat")
    f32 = jnp.float32

    def device(lon, lat):
        return lon % nlon * nlat + lat

    def both(a, b):
        return [(a, b), (b, a)]

    fold = [(device(nlon - 1 - i, nlat - 1), device(i, nlat - 1)) for i in range(nlon)]
    fold_next = [(device(nlon - i, nlat - 1), device(i, nlat - 1)) for i in range(nlon)]
    within = [e for i in range(nlon) for j in range(0, nlat, 2) for e in both(device(i, j), device(i, j + 1))]
    across = [e for i in range(nlon) for j in range(1, nlat - 1, 2) for e in both(device(i, j), device(i, j + 1))]
    even = [e for i in range(0, nlon, 2) for j in range(nlat) for e in both(device(i, j), device(i + 1, j))]
    odd = [e for i in range(1, nlon, 2) for j in range(nlat) for e in both(device(i, j), device(i + 1, j))]

    def held(x):
        return pltpu.with_memory_space_constraint(x, pltpu.VMEM)

    def call(kernel, name, args, outs, scratch=(), aliases=None, micros=1):
        return pl.pallas_call(
            kernel,
            out_shape=tuple(pltpu.VMEM(shape, f32) for shape in outs),
            in_specs=[VMEM] * len(args),
            out_specs=(VMEM,) * len(outs),
            scratch_shapes=[pltpu.VMEM(shape, f32) for shape in scratch],
            input_output_aliases=aliases or {},
            cost_estimate=pl.CostEstimate(flops=0, bytes_accessed=micros * 3_000_000, transcendentals=0),
            compiler_params=pltpu.CompilerParams(vmem_limit_bytes=SCOPED),
            name=name,
        )(*(held(x) for x in args))

    inputs = (state_adjoint, east_velocity, north_velocity, ocean_mask)
    message = (SUBS * (levels + 2), width)
    to_a, to_b = pl.pallas_call(
        row_kernel,
        out_shape=(pltpu.VMEM(message, f32), pltpu.VMEM(message, f32)),
        in_specs=[pl.BlockSpec(memory_space=pltpu.HBM)] * 4,
        out_specs=(VMEM,) * 2,
        scratch_shapes=[pltpu.VMEM((2,) + x.shape[:-2] + (SUBS, width), x.dtype) for x in inputs]
        + [pltpu.SemaphoreType.DMA((4, 2))],
        compiler_params=pltpu.CompilerParams(vmem_limit_bytes=SCOPED),
        name="pack_rows",
    )(*(pltpu.with_memory_space_constraint(x, pltpu.HBM) for x in inputs))
    from_a = lax.ppermute(to_a, axes, within)
    from_b = lax.ppermute(to_b, axes, across + fold)
    from_f = lax.ppermute(to_b, axes, fold_next)

    tall = height + 4 * SUBS
    ext = [(fields * levels, 2, tall, LANES)] + [(levels, 2, tall, LANES)] * 3
    pack, sides = (height + SUBS, LANES), (height // 2 + SUBS, LANES)
    laid = call(prepare_kernel, "prepare", inputs, (*ext, (5,) + pack, sides, sides))
    *laid, to_p, to_q = call(
        halo_kernel,
        "place_rows",
        (from_a, from_b, *laid),
        (*ext, (5,) + pack, sides, sides),
        [(2, message[0] + 2 * SUBS, LANES)] * 2,
        aliases={2 + i: i for i in range(7)},
    )
    from_p = lax.ppermute(to_p, axes, even)
    from_q = lax.ppermute(to_q, axes, odd)

    pairs = partner.reshape(2, LANES)
    *laid, packs = call(
        mirror_kernel,
        "mirror_rows",
        (pairs, from_b, from_f, *laid),
        (*ext, (5,) + pack),
        [(4, message[0] + SUBS, LANES)],
        aliases={3 + i: i for i in range(5)},
    )
    (inner,) = call(step_kernel, "both_steps", laid, (state_adjoint.shape,), [(fields, 2, tall, LANES), (2, tall, LANES)], micros=3)
    return pl.pallas_call(
        edge_kernel,
        out_shape=jax.ShapeDtypeStruct(state_adjoint.shape, f32),
        in_specs=[VMEM] * 5,
        out_specs=pl.BlockSpec(memory_space=pl.ANY),
        scratch_shapes=[
            pltpu.VMEM((5, tall, LANES), f32),
            pltpu.VMEM((2, tall, LANES), f32),
            pltpu.VMEM(state_adjoint.shape, f32),
            pltpu.SemaphoreType.DMA((height // SUBS,)),
        ],
        compiler_params=pltpu.CompilerParams(vmem_limit_bytes=SCOPED),
        name="edge_columns",
    )(*(held(x) for x in (pairs, packs, from_q, from_p, inner)))


def solution(mesh):
    placed = (
        P(None, None, "lat", "lon"),
        P(None, "lat", "lon"),
        P(None, "lat", "lon"),
        P(None, "lat", "lon"),
        P("lon"),
    )
    return jax.shard_map(
        per_device,
        mesh=mesh,
        in_specs=placed,
        out_specs=P(None, None, "lat", "lon"),
        check_vma=False,
    )
```
